32 devices in a mesh: scen: 2 (over x), tm: 16 (over z, y, core).
Axes of the slice: x: 2, y: 2, z: 4, core: 2. Of those that a mesh axis runs over, the one named last changes fastest.
Arguments:
- states: bfloat16 [64, 384], P(('scen', 'tm')), parts along dimension 0, may hold values from -6 to 6
- gradient: float32 [64, 384], P(('scen', 'tm')), parts along dimension 0, may hold values from -0.1 to 0.1
- active_mask: int32 [64, 384], P(('scen', 'tm')), parts along dimension 0, may hold values 0 or 1
- zone_weight: float32 [64, 16], P(('scen', 'tm')), parts along dimension 0, may hold values from 0.001 to 0.004
- zone_map: int32 [768], P('scen'), parts along dimension 0, may hold values from 0 to 15
- w_in: bfloat16 [384, 2048], P('tm'), may hold values from -0.3125 to 0.3125
- w_out: bfloat16 [2048, 384], replicated, may hold values from -0.0625 to 0.0625
- bias: float32 [2048], replicated, may hold values from -3 to 3
Outputs:
- step: float32 [64, 384], P(('scen', 'tm')), parts along dimension 0
The draws below stay inside these ranges and needn't reach their ends.
There are 2 independent parts, one for each index of `scen`. The reference program is written for one: setup_inputs(seed, part) draws one part's arguments, and reference() takes and returns one part's arrays. A program takes and returns all parts, laid end to end along the dimension named above; an argument that names none is the same for every part. Nothing has to cross between parts.
Inputs may be any that keep to these rules, and one draw needn't show every extreme that they name: `zone_map`: each entry names one of the 16 zones.
All inputs are finite; a program needn't handle non-finite values. No bound on the sum of `active_mask` on one device may be relied on, other than what follows from the above.
Results may differ from the reference program's by a relative error of at most 0.0035.
Values may be sent and summed in bfloat16 or wider, within the bound.
A program may use at most 128 MiB of HBM per device.

```python
import math
import jax
import jax.numpy as jnp
from jax import lax

S = 384
H = 2048
ZONES = 16
SECTIONS = 32


def draw_gradient(key, part):
    base = jax.random.normal(key, (SECTIONS, S), jnp.float32) * 0.02
    return jnp.clip(base, -0.1, 0.1)


def place_ends(values, stream_key, least, high):
    longest = values.shape.index(max(values.shape))
    spots = []
    for shift in (0, 1):
        where = [jax.random.randint(jax.random.fold_in(stream_key, axis), (), 0, length) for axis, length in enumerate(values.shape)]
        where[longest] = (where[longest] + shift) % values.shape[longest]
        spots.append(tuple(where))
    return values.at[spots[0]].set(least).at[spots[1]].set(high)


def block_scale(key, shape, cuts, least, high):
    level = 1.0
    for axis_at, shards_of in cuts:
        steps = jax.random.uniform(jax.random.fold_in(jax.random.fold_in(key, 6), axis_at), (shards_of,), jnp.float32, least / len(cuts), high / len(cuts))
        level = level * jnp.repeat(jnp.exp(steps), shape[axis_at] // shards_of).reshape((-1,) + (1,) * (len(shape) - 1 - axis_at))
    return level


def centred(stream_key, extent, scale, most, pieces=(), kind=jnp.bfloat16):
    level = block_scale(stream_key, extent, pieces, -0.22, 0.18) if pieces else 1.0
    drawn = jax.random.normal(stream_key, extent, jnp.float32) * scale * level
    return jnp.minimum(jnp.maximum(drawn, -most), most).astype(kind)


def setup_inputs(seed: int = 0, part: int = 0) -> dict:
    key_list = jax.random.split(jax.random.key(seed), 9)
    part_keys = jax.random.split(jax.random.fold_in(key_list[8], part), 9)
    return {
        "states": centred(part_keys[0], (SECTIONS, S), 1.0, 6.0, ((0, 16),)),
        "gradient": draw_gradient(jax.random.fold_in(jax.random.fold_in(key_list[8], part), 71), part),
        "active_mask": place_ends((jax.random.randint(part_keys[2], (SECTIONS, S), 0, 4) < 1).astype(jnp.int32), jax.random.fold_in(part_keys[2], 1), 0, 1),
        "zone_weight": jnp.clip(jnp.exp(math.log(0.004) - 1.3862944 * jax.random.uniform(part_keys[3], (SECTIONS, ZONES), jnp.float32) ** block_scale(part_keys[3], (SECTIONS, ZONES), ((0, 16),), -0.2, 0.2)), 0.001, 0.004),
        "zone_map": place_ends(jax.random.randint(part_keys[4], (S,), 0, ZONES), jax.random.fold_in(part_keys[4], 1), 0, ZONES - 1).astype(jnp.int32),
        "w_in": centred(key_list[5], (S, H), S ** -0.5, 0.3125, ((0, 16),)),
        "w_out": centred(key_list[6], (H, S), (4 * H) ** -0.5, 0.0625),
        "bias": centred(key_list[7], (H,), 0.5, 3.0, (), jnp.float32),
    }


RHO = 1.0

def matmul(left, right):
    return jnp.dot(left, right, precision=lax.Precision.HIGHEST)

def inverse_factor(matrix):
    width = matrix.shape[0]
    factor = jnp.linalg.cholesky(matrix)
    return jax.scipy.linalg.solve_triangular(factor, jnp.eye(width, dtype=matrix.dtype), lower=True)

def merge_pair(lower, upper):
    middle = lower[2] + upper[0]
    middle_rhs = lower[4] + upper[3]
    inverse = inverse_factor(middle)
    left_solved = matmul(inverse, lower[1].T)
    right_solved = matmul(inverse, upper[1])
    rhs_solved = matmul(inverse, middle_rhs)
    first_first = lower[0] - matmul(left_solved.T, left_solved)
    first_last = -matmul(left_solved.T, right_solved)
    last_last = upper[2] - matmul(right_solved.T, right_solved)
    first_rhs = lower[3] - matmul(left_solved.T, rhs_solved)
    last_rhs = upper[4] - matmul(right_solved.T, rhs_solved)
    return ((first_first, first_last, last_last, first_rhs, last_rhs), (inverse, left_solved, right_solved, rhs_solved))

def back_solve(store, outer_first, outer_last):
    inverse, left_solved, right_solved, rhs_solved = store
    value = rhs_solved - matmul(left_solved, outer_first) - matmul(right_solved, outer_last)
    return matmul(inverse.T, value)

def element_blocks(jacobian, weight_row, grad_row):
    width = jacobian.shape[0]
    first_first = jnp.diag(weight_row) + RHO * matmul(jacobian, jacobian.T)
    first_last = -RHO * jacobian
    last_last = RHO * jnp.eye(width, dtype=jnp.float32)
    return (first_first, first_last, last_last, grad_row, jnp.zeros_like(grad_row))

def solve_ends(chain):
    width = chain[0].shape[0]
    top = jnp.concatenate([chain[0], chain[1]], axis=1)
    bottom = jnp.concatenate([chain[1].T, chain[2]], axis=1)
    system = jnp.concatenate([top, bottom], axis=0)
    inverse = inverse_factor(system)
    rhs = jnp.concatenate([chain[3], chain[4]])
    ends = matmul(inverse.T, matmul(inverse, rhs))
    return (ends[:width], ends[width:])

def reference(states, gradient, active_mask, zone_weight, zone_map, w_in, w_out, bias):
    hidden_in = jnp.dot(states.astype(jnp.float32), w_in.astype(jnp.float32), preferred_element_type=jnp.float32) + bias
    slopes = (1.0 - jnp.tanh(hidden_in) ** 2).astype(jnp.bfloat16)

    def one_section(slope):
        weighted = w_in * slope[None, :]
        product = jnp.dot(weighted.astype(jnp.float32), w_out.astype(jnp.float32), preferred_element_type=jnp.float32)
        return product + jnp.eye(S, dtype=jnp.float32)
    jacobians = lax.map(one_section, slopes)
    weights = zone_weight[:, zone_map] * (1.0 + 4.0 * active_mask.astype(jnp.float32))
    elements = jax.vmap(element_blocks)(jacobians, weights, gradient)
    first = jax.tree.map(lambda part_array: part_array[0], elements)
    rest = jax.tree.map(lambda part_array: part_array[1:], elements)

    def fold(carry, item):
        merged, store = merge_pair(carry, item)
        return (merged, store)
    chain, stores = lax.scan(fold, first, rest)
    start_state, end_state = solve_ends(chain)

    def backward(outer_last, store):
        middle = back_solve(store, start_state, outer_last)
        return (middle, middle)
    _, middles = lax.scan(backward, end_state, stores, reverse=True)
    return jnp.concatenate([start_state[None, :], middles], axis=0)
```

```python
import functools
import math

import jax
import jax.numpy as jnp
from jax import lax
from jax.experimental import pallas as pl
from jax.experimental.pallas import tpu as pltpu
from jax.sharding import PartitionSpec as P


def from_partner(array, axis, bit):
    return lax.ppermute(array, axis, [(i, i ^ 1 << bit) for i in range(lax.axis_size(axis))])


def matmul(left, right):
    return jnp.dot(left, right, precision=lax.Precision.HIGHEST)


def dot_exact(left, right, dims=((1,), (0,))):
    return lax.dot_general(
        left, right, (dims, ((), ())), precision=lax.Precision.HIGHEST, preferred_element_type=jnp.float32
    )


def dot_fast(left, right):
    return jnp.dot(
        left.astype(jnp.bfloat16), right.astype(jnp.bfloat16), preferred_element_type=jnp.float32
    )


def invert_in_place(m_ref, x_ref, e_ref):
    width = m_ref.shape[0]
    row_ids = lax.broadcasted_iota(jnp.int32, (width, width), 0)
    col_ids = lax.broadcasted_iota(jnp.int32, (width, width), 1)
    diagonal = row_ids == col_ids
    matrix = m_ref[...]
    square = dot_fast(matrix, matrix)
    trace = jnp.sum(jnp.where(diagonal, matrix, 0.0))
    frobenius = jnp.sum(matrix * matrix)
    bound = jnp.max(jnp.sum(jnp.abs(square), axis=1))
    scale = jnp.minimum(trace / frobenius, 1.9 * lax.rsqrt(bound))
    x_ref[...] = jnp.where(diagonal, 2.0 * scale, 0.0) - (scale * scale) * matrix
    first = jnp.where(diagonal, 1.0, 0.0) - (2.0 * scale) * matrix + (scale * scale) * square
    e_ref[...] = first

    def coarse_step(carry):
        count, _ = carry
        x_ref[...] = x_ref[...] + dot_fast(x_ref[...], e_ref[...])
        residual = jnp.where(diagonal, 1.0, 0.0) - dot_fast(m_ref[...], x_ref[...])
        e_ref[...] = residual
        return count + 1, jnp.sum(residual * residual)

    lax.while_loop(lambda c: (c[0] < 10) & (c[1] > 0.25), coarse_step, (0, jnp.sum(first * first)))

    def fine_step(carry):
        count, _ = carry
        residual = jnp.where(diagonal, 1.0, 0.0) - dot_exact(m_ref[...], x_ref[...])
        x_ref[...] = x_ref[...] + dot_fast(x_ref[...], residual)
        return count + 1, jnp.sum(residual * residual)

    _, last = lax.while_loop(
        lambda c: (c[0] < 12) & jnp.logical_not(c[1] <= 1e-7), fine_step, (0, jnp.float32(1.0))
    )

    @pl.when(jnp.logical_not(last <= 1e-7))
    def _():
        x_ref[...] = m_ref[...]

        def pivot_step(k, carry):
            current = x_ref[...]
            row = x_ref[pl.ds(k, 1), :]
            column = jnp.sum(jnp.where(col_ids == k, current, 0.0), axis=1, keepdims=True)
            pivot = jnp.sum(jnp.where(col_ids[:1] == k, row, 0.0), axis=1, keepdims=True)
            scaled = row / pivot
            updated = jnp.where(col_ids == k, -column / pivot, current - column * scaled)
            own_row = jnp.where(col_ids == k, 1.0 / pivot, scaled)
            x_ref[...] = jnp.where(row_ids == k, own_row, updated)
            return carry

        lax.fori_loop(0, width, pivot_step, 0)


def unpack_first(packed, row_ids, col_ids):
    return jnp.where(row_ids <= col_ids, packed, jnp.transpose(packed))


def unpack_last(packed, diagonal, row_ids, col_ids):
    whole = jnp.where(row_ids > col_ids, packed, jnp.transpose(packed))
    return jnp.where(row_ids == col_ids, diagonal, whole)


def finish(left, right, rhs, ff, ll, fr, lr, x_ref, block_ref, vector_ref, gl_ref, gr_ref, gs_ref):
    width = x_ref.shape[0]
    inverse = x_ref[...]
    gl_ref[...] = dot_exact(left, inverse)
    gr_ref[...] = dot_exact(inverse, right)
    solved = dot_exact(jnp.broadcast_to(rhs, (8, width)), inverse)
    gs_ref[...] = solved[:1]
    row_ids = lax.broadcasted_iota(jnp.int32, (width, width), 0)
    col_ids = lax.broadcasted_iota(jnp.int32, (width, width), 1)
    new_ff = ff() - dot_exact(gl_ref[...], left, ((1,), (1,)))
    block_ref[width : 2 * width] = -dot_exact(gl_ref[...], right)
    new_ll = ll() - dot_exact(jnp.transpose(right), gr_ref[...])
    block_ref[:width] = jnp.where(row_ids <= col_ids, new_ff, new_ll)
    vector_ref[2:3] = jnp.sum(jnp.where(row_ids == col_ids, new_ll, 0.0), axis=0, keepdims=True)
    vector_ref[0:1] = fr - dot_exact(solved, left, ((1,), (1,)))[:1]
    vector_ref[1:2] = lr - dot_exact(solved, right)[:1]


def first_kernel(
    m_ref, mr_ref, l_ref, r_ref, ff_ref, ll_ref, fr_ref, lr_ref,
    block_ref, vector_ref, gl_ref, gr_ref, gs_ref, x_ref, e_ref
):
    invert_in_place(m_ref, x_ref, e_ref)
    finish(
        l_ref[...], r_ref[...], mr_ref[...], lambda: ff_ref[...], lambda: ll_ref[...],
        fr_ref[...], lr_ref[...], x_ref, block_ref, vector_ref, gl_ref, gr_ref, gs_ref
    )


def merge_kernel(
    flag_ref, own_ref, other_ref, ov_ref, pv_ref,
    block_ref, vector_ref, gl_ref, gr_ref, gs_ref, x_ref, e_ref, m_ref
):
    width = x_ref.shape[0]
    is_upper = flag_ref[0] == 1
    spans = [pl.ds(k * width, width) for k in range(2)]
    row_ids = lax.broadcasted_iota(jnp.int32, (width, width), 0)
    col_ids = lax.broadcasted_iota(jnp.int32, (width, width), 1)
    lower_rhs = jnp.where(is_upper, pv_ref[...], ov_ref[...])
    upper_rhs = jnp.where(is_upper, ov_ref[...], pv_ref[...])

    def lower(k):
        return jnp.where(is_upper, other_ref[spans[k], :], own_ref[spans[k], :])

    def upper(k):
        return jnp.where(is_upper, own_ref[spans[k], :], other_ref[spans[k], :])

    m_ref[...] = unpack_last(lower(0), lower_rhs[2:3], row_ids, col_ids) + unpack_first(
        upper(0), row_ids, col_ids
    )
    invert_in_place(m_ref, x_ref, e_ref)
    finish(
        lower(1), upper(1), lower_rhs[1:2] + upper_rhs[0:1], lambda: unpack_first(lower(0), row_ids, col_ids),
        lambda: unpack_last(upper(0), upper_rhs[2:3], row_ids, col_ids),
        lower_rhs[0:1], upper_rhs[1:2], x_ref, block_ref, vector_ref, gl_ref, gr_ref, gs_ref
    )


def call_merge(kernel, name, width, parts, scratch, in_specs=None):
    full = jax.ShapeDtypeStruct((width, width), jnp.float32)
    result = pl.pallas_call(
        kernel,
        out_shape=(
            jax.ShapeDtypeStruct((2 * width, width), jnp.float32),
            jax.ShapeDtypeStruct((3, width), jnp.float32),
            full, full, jax.ShapeDtypeStruct((1, width), jnp.float32),
        ),
        in_specs=in_specs or [pl.BlockSpec(memory_space=pltpu.VMEM)] * len(parts),
        scratch_shapes=[pltpu.VMEM((width, width), jnp.float32)] * scratch,
        compiler_params=pltpu.CompilerParams(vmem_limit_bytes=48 << 20),
        name=name,
    )(*parts)
    return result[:2], result[2:]


def eliminate(*parts):
    return call_merge(
        first_kernel, "eliminate", parts[0].shape[0],
        [part if part.ndim == 2 else part[None] for part in parts], 2
    )


def merge(upper_flag, own, other):
    vmem = pl.BlockSpec(memory_space=pltpu.VMEM)
    return call_merge(
        merge_kernel, "merge", own[0].shape[1],
        [upper_flag.astype(jnp.int32)[None], own[0], other[0], own[1], other[1]], 3,
        [pl.BlockSpec(memory_space=pltpu.SMEM)] + [vmem] * 4
    )


def exchange(block, vector, core, level):
    if level == 0:
        return from_partner((block, vector), "tm", level)
    half = block.shape[0] // 2
    share = lax.dynamic_slice_in_dim(block, core * half, half, axis=0)
    received, other_vector = from_partner((share, vector), "tm", level)
    swapped = from_partner(received, "tm", 0)
    other = jnp.where(
        core == 1,
        jnp.concatenate([swapped, received]),
        jnp.concatenate([received, swapped]),
    )
    return other, other_vector


def gather_rows(rows, level_count):
    place = lax.axis_index("tm")
    held = rows[None]
    for level in reversed(range(level_count)):
        other = from_partner(held, "tm", level)
        upper_flag = jnp.bitwise_and(jnp.right_shift(place, level), 1) == 1
        held = jnp.stack([jnp.where(upper_flag, other, held), jnp.where(upper_flag, held, other)])
        held = held.reshape((-1,) + rows.shape)
    bits = held.reshape((2,) * level_count + rows.shape)
    order = tuple(reversed(range(level_count))) + (level_count, level_count + 1)
    return bits.transpose(order).reshape(-1, rows.shape[1])


def root_kernel(m_ref, mr_ref, o_ref, x_ref, e_ref):
    invert_in_place(m_ref, x_ref, e_ref)
    o_ref[...] = dot_exact(jnp.broadcast_to(mr_ref[...], (8, m_ref.shape[0])), x_ref[...])[:1]


def root_solve(matrix, rhs):
    width = matrix.shape[0]
    return pl.pallas_call(
        root_kernel,
        out_shape=jax.ShapeDtypeStruct((1, width), jnp.float32),
        scratch_shapes=[pltpu.VMEM((width, width), jnp.float32)] * 2,
        compiler_params=pltpu.CompilerParams(vmem_limit_bytes=48 << 20),
        name="root",
    )(matrix, rhs)


def direct_device(states, gradient, active_mask, zone_weight, zone_map, w_in, w_out, bias):
    width = states.shape[1]
    devices = lax.axis_size("tm")
    place = lax.axis_index("tm")
    is_first = place == 0
    is_last = place == devices - 1
    zone_count = zone_weight.shape[1]
    zone_table = (
        zone_map[None, :] == lax.broadcasted_iota(jnp.int32, (zone_count, width), 0)
    ).astype(jnp.float32)
    weights = jnp.dot(zone_weight, zone_table, precision=lax.Precision.HIGHEST) * (
        1.0 + 4.0 * active_mask.astype(jnp.float32)
    )
    later = jnp.stack([states[1].astype(jnp.float32), gradient[1], weights[1]])
    before = lax.ppermute(later, "tm", [(i, i + 1) for i in range(devices - 1)])
    whole_rows = gather_rows(w_in, devices.bit_length() - 1)
    rows = jnp.stack([before[0].astype(jnp.bfloat16), states[0]])
    hidden_in = jnp.dot(rows, whole_rows, preferred_element_type=jnp.float32) + bias
    slopes = (1.0 - jnp.tanh(hidden_in) ** 2).astype(jnp.bfloat16)
    weighted = slopes[:, None, :] * whole_rows[None, :, :]
    flat = weighted.reshape(2 * width, whole_rows.shape[1])
    product = jnp.dot(flat, w_out, preferred_element_type=jnp.float32).reshape(2, width, width)
    eye = jnp.eye(width, dtype=jnp.float32)
    jac_before = product[0] + eye
    jac_own = product[1] + eye
    last_diag = 1.0 / (1.0 + weights[1])
    column_scale = jnp.where(is_last, weights[1] * last_diag, 1.0)
    tail = jnp.where(is_last, gradient[1] * last_diag, 0.0)
    middle = (
        jnp.diag(weights[0] + jnp.where(is_first, 0.0, 1.0))
        + matmul(jac_own * column_scale[None, :], jac_own.T)
    )
    middle_rhs = gradient[0] + matmul(jac_own, tail)
    left = jnp.where(is_first, 0.0, -jac_before)
    right = jnp.where(is_last, 0.0, -jac_own)
    first_first = jnp.diag(before[2]) + matmul(left, left.T)
    own, local_store = eliminate(
        middle, middle_rhs, left, right, first_first, eye, before[1], jnp.zeros_like(middle_rhs)
    )
    core = jnp.bitwise_and(place, 1)
    level_count = devices.bit_length() - 1
    level_stores = []
    for level in range(level_count):
        upper_flag = jnp.bitwise_and(jnp.right_shift(place, level), 1) == 1
        if level == level_count - 1:
            row_ids = lax.broadcasted_iota(jnp.int32, (width, width), 0)
            packed, flipped = own[0][:width], own[0][:width].T
            keep = jnp.where(upper_flag, row_ids <= row_ids.T, row_ids > row_ids.T)
            block = jnp.where(keep, packed, flipped)
            block = jnp.where((row_ids == row_ids.T) & ~upper_flag, own[1][2:3], block)
            vector = jnp.where(upper_flag, own[1][:1], own[1][1:2])
            other_block, other_vector = exchange(block, vector, core, level)
            root = root_solve(block + other_block, vector + other_vector)[0]
            break
        own, store = merge(upper_flag, own, exchange(own[0], own[1], core, level))
        level_stores.append((store, upper_flag))
    top_flag = jnp.right_shift(place, level_count - 1) == 1
    start = jnp.where(top_flag, root, 0.0)
    end = jnp.where(top_flag, 0.0, root)
    for store, upper_flag in reversed(level_stores):
        value = back_solve(store, start, end)
        start = jnp.where(upper_flag, value, start)
        end = jnp.where(upper_flag, end, value)
    value = back_solve(local_store, start, end)
    end = jnp.where(is_last, tail + last_diag * matmul(value, jac_own), end)
    return jnp.stack([value, end], axis=0)


def back_solve(store, outer_first, outer_last):
    left_solved, right_solved, rhs_solved = store
    return rhs_solved[0] - matmul(outer_first, left_solved) - matmul(right_solved, outer_last)


MESH = pl.DeviceIdType.MESH
F32 = jnp.float32
BF16 = jnp.bfloat16


def low(x):
    return x.astype(BF16)


def dot1(a, b):
    return jnp.dot(a, b, preferred_element_type=F32)


def split(x):
    high = low(x)
    return high, low(x - high.astype(F32))


def dot3(a, b):
    ah, al = split(a)
    bh, bl = split(b)
    return dot1(ah, bh) + (dot1(ah, bl) + dot1(al, bh))


def row_dot(x, m):
    return dot3(jnp.broadcast_to(x, (8, x.shape[1])), m)[:1]


def row_dot_t(x, m):
    return dot_exact(jnp.broadcast_to(x, (8, x.shape[1])), m, ((1,), (1,)))[:1]


def total(x):
    return jnp.sum(jnp.sum(x, axis=1, keepdims=True), axis=0, keepdims=True)


def diagonal_mask(width):
    return lax.broadcasted_iota(jnp.int32, (width, width), 0) == lax.broadcasted_iota(
        jnp.int32, (width, width), 1
    )


def invert(b_ref, delta, least, steps, fine, x_ref, pair_ref):
    width = b_ref.shape[0]
    eye = diagonal_mask(width)

    def on_diagonal(value):
        return jnp.where(eye, value, 0.0)

    whole = b_ref[...]
    coarse = low(whole)
    square = dot1(coarse, coarse)
    most = delta + jnp.sqrt(jnp.sqrt(total(square * square)))
    alpha = 2.0 / (least + most)
    error = (most - least) / (most + least)
    rest = 1.0 - alpha * delta
    factor = 2.0 / (2.0 - error * error)
    x = factor * alpha * (on_diagonal(1.0 + rest) - alpha * whole)
    e = on_diagonal(1.0 - factor + factor * rest * rest) + factor * (
        alpha * alpha * square - 2.0 * alpha * rest * whole
    )
    x_ref[...] = x
    pair_ref[:width] = low(x)
    pair_ref[width:] = low(e)

    def step(_, err):
        c = 2.0 / (2.0 - err * err)
        product = dot1(pair_ref[...], pair_ref[width:])
        x = c * (x_ref[...] + product[:width])
        x_ref[...] = x
        pair_ref[:width] = low(x)
        pair_ref[width:] = low(on_diagonal(1.0 - c) + c * product[width:])
        return err * err / (2.0 - err * err)

    error = lax.fori_loop(0, steps - 2, step, error * error / (2.0 - error * error))
    c = 2.0 / (2.0 - error * error)
    x_ref[...] = c * (x_ref[...] + dot1(pair_ref[:width], pair_ref[width:]))

    def polish(_, unused):
        x = x_ref[...]
        residual = on_diagonal(1.0) - delta * x - dot3(b_ref[...], x)
        x_ref[...] = x + dot1(low(x), low(residual))
        return total(residual * residual)

    return lax.fori_loop(0, fine, polish, jnp.zeros((1, 1), F32))


def bad_if(value, limit):
    return jnp.where(value <= limit, 0.0, 1.0)


def merge_chains(left, right, out, x_ref, b_ref, pair_ref, steps, fine, before_products):
    b_ref[...] = dot1(low(right[1][...]), low(left[0][...]))
    residual = invert(b_ref, 1.0, 1.0, steps, fine, x_ref, pair_ref)
    before_products()
    carried = dot3(left[2][...], x_ref[...])
    transposed = dot3(carried, right[2][...])
    out[2][...] = transposed
    out[3][...] = jnp.transpose(transposed)
    out[1][...] = dot3(dot3(carried, right[1][...]), left[3][...]) + left[1][...]
    spread = dot3(left[0][...], x_ref[...])
    out[0][...] = dot3(dot3(right[3][...], spread), right[2][...]) + right[0][...]
    b1, e1, b2, e2 = left[4](), left[5](), right[4](), right[5]()
    b = row_dot(row_dot(b1 + row_dot(e2, left[0][...]), x_ref[...]), right[2][...]) + b2
    e = row_dot_t(e2 - row_dot(b1, right[1][...]), carried) + e1
    return b, e, residual


def open_chain(left, right, x_ref, x, lam):
    t = row_dot(lam, right[3][...]) + right[5]()
    middle = row_dot(row_dot(x, left[2][...]) + left[4]() + row_dot(t, left[0][...]), x_ref[...])
    return middle, t - row_dot(middle, right[1][...])


def fast_kernel(
    devices, greenhouses, rows_in,
    states_ref, gradient_ref, mask_ref, zone_ref, map_ref, own_ref, bias_ref, wout_hbm,
    out_ref, bad_ref,
    parts, whole, wout, small, sect, slope, k_ref, kt_ref, leaf, leaf_v, chain, chain_a, chain_v, top, top_v,
    x0_ref, x1_ref, x2_ref, xr_ref, b_ref, pair_ref, side, side_v, z_ref, z_v, zo_ref, zo_v, zout, zout_v,
    pack_out, pack_in, pack_v, o_buf, o_in, result, result_in, flags,
    w_send, w_recv, s_send, s_recv, local_sem, c_send, c_recv, p_send, p_recv, q_send, q_recv, v_send, v_recv,
    o_send, o_recv, r_send, r_recv, f_send, f_recv,
):
    width = states_ref.shape[1]
    groups = devices // 4
    me = lax.axis_index("tm")
    house = lax.axis_index("scen")
    g = lax.div(me, 4)
    r = lax.rem(me, 4)
    c = lax.rem(r, 2)
    y = lax.div(r, 2)
    core = me + 1 - 2 * c
    across = me + 2 - 4 * y
    diagonal = across + 1 - 2 * c
    has_left = g > 0
    has_right = g < groups - 1
    is_left = g < groups // 2
    depth = jnp.where(is_left, g, groups - 1 - g)
    inward = me + jnp.where(is_left, 4, -4)
    outward = me - jnp.where(is_left, 4, -4)
    is_root = depth == groups // 2 - 1
    is_end = depth == 0
    right_end = jnp.logical_and(is_end, jnp.logical_not(is_left))
    left_end = jnp.logical_and(is_end, is_left)
    solves = jnp.logical_not(right_end)
    writes = y == c

    def remote(src, dst, send, recv, target):
        return pltpu.make_async_remote_copy(
            src_ref=src, dst_ref=dst, send_sem=send, recv_sem=recv, device_id=target, device_id_type=MESH
        )

    wout_copy = pltpu.make_async_copy(wout_hbm, wout, local_sem)
    wout_copy.start()

    barrier = pltpu.get_barrier_semaphore()

    def greet(target):
        pl.semaphore_signal(barrier, inc=1, device_id=target, device_id_type=MESH)

    for target in (core, across, diagonal):
        greet({"tm": target})
    for k in range(1, greenhouses):
        greet({"scen": lax.rem(house + k, greenhouses)})

    @pl.when(has_left)
    def _():
        greet({"tm": me - 4})

    @pl.when(has_right)
    def _():
        greet({"tm": me + 4})

    weights = jnp.zeros(gradient_ref.shape, F32)
    for zone in range(zone_ref.shape[1]):
        weights = jnp.where(map_ref[...] == zone, zone_ref[:, zone : zone + 1], weights)
    weights = weights * (1.0 + 4.0 * mask_ref[...].astype(F32))
    small[r] = jnp.zeros((8, width), F32)
    small[r, 0:2] = states_ref[...].astype(F32)
    small[r, 2:4] = gradient_ref[...]
    small[r, 4:6] = weights
    parts[me] = own_ref[...]
    sect[...] = jnp.zeros_like(sect)

    pl.semaphore_wait(barrier, 3 + greenhouses - 1 + has_left.astype(jnp.int32) + has_right.astype(jnp.int32))

    def shard(s, kind, target):
        return remote(parts.at[s], parts.at[s], w_send.at[kind, s], w_recv.at[s], {"tm": target})

    def arrived(s):
        shard(s, 3, core).wait_recv()

    small_copies = [
        remote(small.at[r], small.at[r], s_send.at[k], s_recv.at[r], {"tm": target})
        for k, target in enumerate((core, across, diagonal))
    ]

    def spread_out(s, to_right, to_left, act):
        if to_right is not None:
            @pl.when(to_right)
            def _():
                act(shard(s, 0, me + 4))
        if to_left is not None:
            @pl.when(to_left)
            def _():
                act(shard(s, 1, me - 4))
        act(shard(s, 2, across))
        act(shard(s, 3, core))

    def begin(copy):
        copy.start()

    def end(copy):
        copy.wait_send()

    def from_across(s, act):
        if act is begin:
            arrived(s)
        act(shard(s, 3, core))

    def line(act):
        spread_out(me, has_right, has_left, act)
        if act is begin:
            for copy in small_copies:
                copy.start()
        for k in range(1, groups + 1):
            if k < groups:
                @pl.when(g >= k)
                def _():
                    if act is begin:
                        arrived(me - 4 * k)
                    spread_out(me - 4 * k, has_right, None, act)

                @pl.when(g + k <= groups - 1)
                def _():
                    if act is begin:
                        arrived(me + 4 * k)
                    spread_out(me + 4 * k, None, has_left, act)
            if k == 1:
                from_across(across, act)
            else:
                @pl.when(g >= k - 1)
                def _():
                    from_across(across - 4 * (k - 1), act)

                @pl.when(g + k - 1 <= groups - 1)
                def _():
                    from_across(across + 4 * (k - 1), act)

    line(begin)
    for j in range(groups):
        arrived(4 * j + lax.rem(core, 4))
        arrived(4 * j + lax.rem(diagonal, 4))
    for target in (core, across, diagonal):
        remote(small.at[r], small.at[lax.rem(target, 4)], s_send.at[0], s_recv.at[lax.rem(target, 4)], {"tm": core}).wait_recv()

    pieces = own_ref.shape[0] // rows_in
    span = own_ref.shape[1]
    batch = next(q for q in range(1, 17) if q * rows_in % 16 == 0)
    for first in range(0, devices, batch):
        blocks = [parts[first + k].astype(F32) for k in range(batch)]
        for j in range(pieces):
            tall = jnp.concatenate([block[j * rows_in : (j + 1) * rows_in] for block in blocks], axis=0)
            whole[first * rows_in : (first + batch) * rows_in, j * span : (j + 1) * span] = low(tall)

    for k in range(3):
        sect[k, 0:2] = small[2 * c, 2 * k : 2 * k + 2]
        sect[k, 2:4] = small[2 * c + 1, 2 * k : 2 * k + 2]
    hidden = dot1(low(sect[0]), whole[...]) + bias_ref[...]
    bent = jnp.tanh(hidden)
    slope[...] = low(1.0 - bent * bent).astype(F32)
    wout_copy.wait()

    def section(t, carry):
        weighted = whole[...] * low(slope[pl.ds(t, 1), :])
        product = dot1(weighted, wout[...])
        k_ref[t] = product
        kt_ref[t] = jnp.transpose(product)
        return carry

    lax.fori_loop(0, 4, section, 0)

    eye = diagonal_mask(width)

    def on_diagonal(row):
        return jnp.where(eye, row, 0.0)

    def column(row):
        return jnp.sum(on_diagonal(row), axis=1, keepdims=True)

    def pair(q, carry):
        w0, w1 = sect[2, pl.ds(2 * q, 1)], sect[2, pl.ds(2 * q + 1, 1)]
        g0, g1 = sect[1, pl.ds(2 * q, 1)], sect[1, pl.ds(2 * q + 1, 1)]
        d = 1.0 / (1.0 + w1)
        dw = w1 * d
        k0, k1, k0t, k1t = k_ref[2 * q], k_ref[2 * q + 1], kt_ref[2 * q], kt_ref[2 * q + 1]
        scaled = column(d) * k1
        transposed = on_diagonal(d) + k0 * d + scaled + dot1(low(k0 * d), low(k1))
        leaf[q, 2] = transposed
        leaf[q, 3] = jnp.transpose(transposed)
        leaf[q, 0] = on_diagonal(1.0 + d) + scaled + k1t * d + dot1(low(k1t * d), low(k1))
        light = k0 * dw
        leaf[q, 1] = on_diagonal(w0 + dw) + light + column(dw) * k0t + dot1(low(light), low(k0t))
        rhs = d * g1
        leaf_v[q, 0:1] = rhs + row_dot(rhs, k1)
        leaf_v[q, 1:2] = rhs + row_dot(rhs, k0t) + g0
        return carry

    lax.fori_loop(0, 2, pair, 0)

    def chain_of(quad, fourth, vector):
        return [quad.at[0], quad.at[1], quad.at[2], fourth, lambda: vector[0:1], lambda: vector[1:2]]

    lower, upper = (chain_of(leaf.at[q], leaf.at[q, 3], leaf_v.at[q]) for q in range(2))
    mine = chain_of(chain.at[c], chain_a.at[c], chain_v.at[c])
    b, e, residual = merge_chains(lower, upper, mine, x0_ref, b_ref, pair_ref, 3, 1, lambda: None)
    chain_v[c] = jnp.zeros((8, width), F32)
    chain_v[c, 0:1] = b
    chain_v[c, 1:2] = e
    chain_v[c, 2:3] = jnp.broadcast_to(bad_if(residual, 0.01), (1, width))

    def chain_copy(slot, k):
        return remote(chain.at[slot, k], chain.at[slot, k], c_send.at[k], c_recv.at[k], {"tm": core})

    def vector_copy(slot):
        return remote(chain_v.at[slot], chain_v.at[slot], c_send.at[3], c_recv.at[3], {"tm": core})

    chain_copy(c, c).start()
    chain_copy(c, 1 - c).start()
    chain_copy(c, 2).start()
    vector_copy(c).start()
    chain_copy(1 - c, 1 - c).wait_recv()

    def rest_arrived():
        chain_copy(1 - c, c).wait_recv()
        chain_copy(1 - c, 2).wait_recv()
        vector_copy(1 - c).wait_recv()
        chain_a[1 - c] = jnp.transpose(chain[1 - c, 2])

    first, second = (chain_of(chain.at[q], chain_a.at[q], chain_v.at[q]) for q in range(2))
    b, e, residual = merge_chains(first, second, chain_of(top, top.at[3], top_v), x1_ref, b_ref, pair_ref, 5, 1, rest_arrived)
    bad = jnp.maximum(jnp.maximum(chain_v[0, 2:3], chain_v[1, 2:3]), bad_if(residual, 0.01))

    sign = jnp.where(is_left, 1.0, -1.0)
    for k, (a_index, b_index) in enumerate(((3, 2), (2, 3), (1, 0), (0, 1))):
        side[k] = jnp.where(is_left, top[a_index], top[b_index])
    side_v[0:1] = jnp.where(is_left, e, -b)
    side_v[1:2] = jnp.where(is_left, b, e)
    side_v[2:3] = bad

    blocks = width // 128
    tiles = [(i, j) for i in range(blocks) for j in range(i + 1)]
    half = len(tiles) // 2

    def tile_copy(which, k):
        return remote(pack_out.at[k], pack_in.at[which, k], p_send.at[k], p_recv.at[which, k], {"tm": inward})

    def tile_pass(which, k):
        return remote(pack_in.at[which, k], pack_in.at[which, k], q_send.at[which, k], q_recv.at[which, k], {"tm": core})

    def row_copy(which):
        return remote(zout_v, pack_v.at[which], v_send, v_recv.at[which], {"tm": inward})

    def receive(which, m_ref, row_ref):
        for j in range(half):
            tile_copy(which, 2 * j + c).wait_recv()
            tile_pass(which, 2 * j + c).start()
        for j in range(half):
            tile_pass(which, 2 * j + 1 - c).wait_recv()
        row_copy(which).wait_recv()
        for k, (i, j) in enumerate(tiles):
            tile = pack_in[which, k]
            m_ref[128 * i : 128 * i + 128, 128 * j : 128 * j + 128] = tile
            if i != j:
                m_ref[128 * j : 128 * j + 128, 128 * i : 128 * i + 128] = jnp.transpose(tile)
        row_ref[...] = pack_v[which]

    @pl.when(is_end)
    def _():
        z_ref[...] = jnp.where(eye, 1.0, 0.0)
        z_v[...] = jnp.zeros_like(z_v)

    @pl.when(jnp.logical_not(is_end))
    def _():
        receive(0, z_ref, z_v)

    @pl.when(solves)
    def _():
        delta = jnp.where(left_end, 0.0, 1.0)
        floor = jnp.min(small[0, 4:5], axis=1, keepdims=True)
        least = jnp.where(left_end, floor, 1.0)
        b_ref[...] = dot3(side[2], z_ref[...])
        residual = invert(b_ref, delta, least, 9, 1, x2_ref, pair_ref)
        reach = dot3(side[0], dot3(z_ref[...], x2_ref[...]))
        zout[...] = dot3(reach, side[1]) + side[3]
        v = side_v[0:1]
        row = row_dot(z_v[0:1] + row_dot(v, z_ref[...]), x2_ref[...])
        zout_v[...] = jnp.zeros_like(zout_v)
        zout_v[0:1] = row_dot(row, side[1]) + side_v[1:2]
        zout_v[2:3] = jnp.maximum(jnp.maximum(side_v[2:3], z_v[2:3]), bad_if(residual, 2.0))

    @pl.when(right_end)
    def _():
        zout[...] = side[3]
        zout_v[...] = jnp.zeros_like(zout_v)
        zout_v[0:1] = side_v[1:2]
        zout_v[2:3] = side_v[2:3]

    for k, (i, j) in enumerate(tiles):
        pack_out[k] = zout[128 * i : 128 * i + 128, 128 * j : 128 * j + 128]
    which = is_root.astype(jnp.int32)
    for j in range(half):
        tile_copy(which, 2 * j + c).start()
    row_copy(which).start()

    def outer_copy():
        return remote(o_buf, o_in, o_send, o_recv, {"tm": outward})

    flag_copies = [remote(flags.at[0], flags.at[1], f_send.at[0], f_recv.at[0], {"tm": inward})]
    for k in range(1, greenhouses):
        flag_copies.append(
            remote(flags.at[2], flags.at[2 + k], f_send.at[k], f_recv.at[k], {"scen": lax.rem(house + k, greenhouses)})
        )
    last = 2 + greenhouses
    flag_out = remote(flags.at[last], flags.at[last], f_send.at[greenhouses], f_recv.at[greenhouses], {"tm": outward})

    @pl.when(is_root)
    def _():
        receive(1, zo_ref, zo_v)
        b_ref[...] = dot3(zo_ref[...], zout[...])
        invert(b_ref, 1.0, 1.0, 9, 1, xr_ref, pair_ref)
        rhs = zout_v[0:1] + sign * row_dot(zo_v[0:1], zout[...])
        value = row_dot(rhs, xr_ref[...])
        for _ in range(2):
            left_over = rhs - value - row_dot(row_dot(value, zo_ref[...]), zout[...])
            value = value + row_dot(left_over, xr_ref[...])
        failed = bad_if(total(left_over * left_over), 1e-4 * total(rhs * rhs))
        o_in[0:1] = zo_v[0:1] - sign * row_dot(value, zo_ref[...])
        flags[0] = jnp.broadcast_to(
            jnp.maximum(jnp.maximum(zout_v[2:3, :128], zo_v[2:3, :128]), failed), (8, 128)
        )
        flag_copies[0].start()

    @pl.when(jnp.logical_not(is_root))
    def _():
        outer_copy().wait_recv()

    outer = o_in[0:1]
    side_v[3:4] = jnp.zeros((1, width), F32)

    @pl.when(solves)
    def _():
        w = sign * side_v[0:1] + row_dot(outer, side[0])
        value = row_dot(z_v[0:1] + sign * row_dot(w, z_ref[...]), x2_ref[...])
        side_v[3:4] = value
        o_buf[...] = jnp.broadcast_to(w - sign * row_dot(value, side[2]), o_buf.shape)

    @pl.when(jnp.logical_not(is_end))
    def _():
        outer_copy().start()

    @pl.when(is_root)
    def _():
        flag_copies[0].wait_recv()
        flags[2] = jnp.maximum(flags[0], flags[1])
        for copy in flag_copies[1:]:
            copy.start()

    own_value = side_v[3:4]
    start = jnp.where(is_left, own_value, outer)
    finish_lam = jnp.where(is_left, outer, own_value)

    def result_copy(slot):
        return remote(result.at[slot], result_in, r_send, r_recv, {"tm": core})

    @pl.when(writes)
    def _():
        middle, lam = open_chain(first, second, x1_ref, start, finish_lam)
        x_a = jnp.where(c == 0, start, middle)
        lam_b = jnp.where(c == 0, lam, finish_lam)
        middle, lam = open_chain(lower, upper, x0_ref, x_a, lam_b)
        for q, x, lam_q in ((0, x_a, lam), (1, middle, lam_b)):
            w1, g1 = sect[2, 2 * q + 1 : 2 * q + 2], sect[1, 2 * q + 1 : 2 * q + 2]
            result[q, 0:1] = x
            result[q, 1:2] = (
                x + row_dot(x, k_ref[2 * q]) + lam_q + row_dot(lam_q, kt_ref[2 * q + 1]) + g1
            ) / (1.0 + w1)
        result_copy(1 - c).start()
        out_ref[...] = result[c, 0:2]

    @pl.when(jnp.logical_not(writes))
    def _():
        result_copy(0).wait_recv()
        out_ref[...] = result_in[0:2]

    @pl.when(is_root)
    def _():
        for copy in flag_copies[1:]:
            copy.wait_recv()
        worst = flags[2]
        for k in range(1, greenhouses):
            worst = jnp.maximum(worst, flags[2 + k])
        flags[last] = worst

    @pl.when(jnp.logical_not(is_root))
    def _():
        flag_out.wait_recv()

    @pl.when(jnp.logical_not(is_end))
    def _():
        flag_out.start()

    bad_ref[...] = flags[last]

    line(end)
    for copy in small_copies:
        copy.wait_send()
    for k in range(3):
        chain_copy(c, k).wait_send()
    vector_copy(c).wait_send()
    for j in range(half):
        tile_copy(which, 2 * j + c).wait_send()
    row_copy(which).wait_send()

    @pl.when(jnp.logical_not(is_end))
    def _():
        for j in range(half):
            tile_pass(0, 2 * j + c).wait_send()
        outer_copy().wait_send()
        flag_out.wait_send()

    @pl.when(is_root)
    def _():
        for j in range(half):
            tile_pass(1, 2 * j + c).wait_send()
        for copy in flag_copies:
            copy.wait_send()

    @pl.when(writes)
    def _():
        result_copy(1 - c).wait_send()


def fast_device(states, gradient, active_mask, zone_weight, zone_map, w_in, w_out, bias):
    width = states.shape[1]
    hidden = w_in.shape[1]
    devices = lax.axis_size("tm")
    greenhouses = lax.axis_size("scen")
    rows = w_in.shape[0]
    pieces = 16 // math.gcd(rows, 16)
    span = hidden // pieces
    own = jnp.concatenate([w_in[:, k * span : (k + 1) * span] for k in range(pieces)], axis=0)
    tiles = (width // 128) * (width // 128 + 1) // 2
    square = lambda *lead: pltpu.VMEM(lead + (width, width), F32)
    lines = lambda *lead: pltpu.VMEM(lead + (8, width), F32)
    dma = pltpu.SemaphoreType.DMA
    vmem = pl.BlockSpec(memory_space=pltpu.VMEM)
    scratch = [
        pltpu.VMEM((devices,) + own.shape, BF16), pltpu.VMEM((rows * devices, hidden), BF16), pltpu.VMEM(w_out.shape, BF16),
        lines(4), lines(3), pltpu.VMEM((8, hidden), F32), square(4), square(4), square(2, 4), lines(2),
        square(2, 3), square(2), lines(2), square(4), lines(),
        square(), square(), square(), square(), square(), pltpu.VMEM((2 * width, width), BF16), square(4), lines(),
        square(), lines(), square(), lines(), square(), lines(),
        pltpu.VMEM((tiles, 128, 128), F32), pltpu.VMEM((2, tiles, 128, 128), F32), lines(2), lines(), lines(), lines(2), lines(),
        pltpu.VMEM((3 + greenhouses, 8, 128), F32),
        dma((4, devices)), dma((devices,)), dma((3,)), dma((4,)), dma, dma((4,)), dma((4,)), dma((tiles,)), dma((2, tiles)),
        dma((2, tiles)), dma((2, tiles)), dma, dma((2,)), dma, dma, dma, dma,
        dma((greenhouses + 1,)), dma((greenhouses + 1,)),
    ]
    return pl.pallas_call(
        functools.partial(fast_kernel, devices, greenhouses, rows),
        out_shape=(jax.ShapeDtypeStruct((2, width), F32), jax.ShapeDtypeStruct((8, 128), F32)),
        in_specs=[vmem] * 7 + [pl.BlockSpec(memory_space=pl.ANY)],
        out_specs=(vmem, vmem),
        scratch_shapes=scratch,
        compiler_params=pltpu.CompilerParams(collective_id=0, has_side_effects=True, vmem_limit_bytes=58 << 20),
        name="gauss_newton",
    )(states, gradient, active_mask, zone_weight, zone_map[None], own, bias[None], w_out)


def per_device(*arrays):
    value, bad = fast_device(*arrays)
    return lax.cond(bad[0, 0] > 0.0, lambda: direct_device(*arrays), lambda: value)


def solution(mesh):
    return jax.shard_map(
        per_device,
        mesh=mesh,
        in_specs=(
            P(("scen", "tm"), None),
            P(("scen", "tm"), None),
            P(("scen", "tm"), None),
            P(("scen", "tm"), None),
            P("scen"),
            P("tm", None),
            P(),
            P(),
        ),
        out_specs=P(("scen", "tm"), None),
        check_vma=False,
    )
```

```python
import functools
import math

import jax
import jax.numpy as jnp
from jax import lax
from jax.experimental import pallas as pl
from jax.experimental.pallas import tpu as pltpu
from jax.sharding import PartitionSpec as P


def from_partner(array, axis, bit):
    return lax.ppermute(array, axis, [(i, i ^ 1 << bit) for i in range(lax.axis_size(axis))])


def matmul(left, right):
    return jnp.dot(left, right, precision=lax.Precision.HIGHEST)


def dot_exact(left, right, dims=((1,), (0,))):
    return lax.dot_general(
        left, right, (dims, ((), ())), precision=lax.Precision.HIGHEST, preferred_element_type=jnp.float32
    )


def dot_fast(left, right):
    return jnp.dot(
        left.astype(jnp.bfloat16), right.astype(jnp.bfloat16), preferred_element_type=jnp.float32
    )


def invert_in_place(m_ref, x_ref, e_ref):
    width = m_ref.shape[0]
    row_ids = lax.broadcasted_iota(jnp.int32, (width, width), 0)
    col_ids = lax.broadcasted_iota(jnp.int32, (width, width), 1)
    diagonal = row_ids == col_ids
    matrix = m_ref[...]
    square = dot_fast(matrix, matrix)
    trace = jnp.sum(jnp.where(diagonal, matrix, 0.0))
    frobenius = jnp.sum(matrix * matrix)
    bound = jnp.max(jnp.sum(jnp.abs(square), axis=1))
    scale = jnp.minimum(trace / frobenius, 1.9 * lax.rsqrt(bound))
    x_ref[...] = jnp.where(diagonal, 2.0 * scale, 0.0) - (scale * scale) * matrix
    first = jnp.where(diagonal, 1.0, 0.0) - (2.0 * scale) * matrix + (scale * scale) * square
    e_ref[...] = first

    def coarse_step(carry):
        count, _ = carry
        x_ref[...] = x_ref[...] + dot_fast(x_ref[...], e_ref[...])
        residual = jnp.where(diagonal, 1.0, 0.0) - dot_fast(m_ref[...], x_ref[...])
        e_ref[...] = residual
        return count + 1, jnp.sum(residual * residual)

    lax.while_loop(lambda c: (c[0] < 10) & (c[1] > 0.25), coarse_step, (0, jnp.sum(first * first)))

    def fine_step(carry):
        count, _ = carry
        residual = jnp.where(diagonal, 1.0, 0.0) - dot_exact(m_ref[...], x_ref[...])
        x_ref[...] = x_ref[...] + dot_fast(x_ref[...], residual)
        return count + 1, jnp.sum(residual * residual)

    _, last = lax.while_loop(
        lambda c: (c[0] < 12) & jnp.logical_not(c[1] <= 1e-7), fine_step, (0, jnp.float32(1.0))
    )

    @pl.when(jnp.logical_not(last <= 1e-7))
    def _():
        x_ref[...] = m_ref[...]

        def pivot_step(k, carry):
            current = x_ref[...]
            row = x_ref[pl.ds(k, 1), :]
            column = jnp.sum(jnp.where(col_ids == k, current, 0.0), axis=1, keepdims=True)
            pivot = jnp.sum(jnp.where(col_ids[:1] == k, row, 0.0), axis=1, keepdims=True)
            scaled = row / pivot
            updated = jnp.where(col_ids == k, -column / pivot, current - column * scaled)
            own_row = jnp.where(col_ids == k, 1.0 / pivot, scaled)
            x_ref[...] = jnp.where(row_ids == k, own_row, updated)
            return carry

        lax.fori_loop(0, width, pivot_step, 0)


def unpack_first(packed, row_ids, col_ids):
    return jnp.where(row_ids <= col_ids, packed, jnp.transpose(packed))


def unpack_last(packed, diagonal, row_ids, col_ids):
    whole = jnp.where(row_ids > col_ids, packed, jnp.transpose(packed))
    return jnp.where(row_ids == col_ids, diagonal, whole)


def finish(left, right, rhs, ff, ll, fr, lr, x_ref, block_ref, vector_ref, gl_ref, gr_ref, gs_ref):
    width = x_ref.shape[0]
    inverse = x_ref[...]
    gl_ref[...] = dot_exact(left, inverse)
    gr_ref[...] = dot_exact(inverse, right)
    solved = dot_exact(jnp.broadcast_to(rhs, (8, width)), inverse)
    gs_ref[...] = solved[:1]
    row_ids = lax.broadcasted_iota(jnp.int32, (width, width), 0)
    col_ids = lax.broadcasted_iota(jnp.int32, (width, width), 1)
    new_ff = ff() - dot_exact(gl_ref[...], left, ((1,), (1,)))
    block_ref[width : 2 * width] = -dot_exact(gl_ref[...], right)
    new_ll = ll() - dot_exact(jnp.transpose(right), gr_ref[...])
    block_ref[:width] = jnp.where(row_ids <= col_ids, new_ff, new_ll)
    vector_ref[2:3] = jnp.sum(jnp.where(row_ids == col_ids, new_ll, 0.0), axis=0, keepdims=True)
    vector_ref[0:1] = fr - dot_exact(solved, left, ((1,), (1,)))[:1]
    vector_ref[1:2] = lr - dot_exact(solved, right)[:1]


def first_kernel(
    m_ref, mr_ref, l_ref, r_ref, ff_ref, ll_ref, fr_ref, lr_ref,
    block_ref, vector_ref, gl_ref, gr_ref, gs_ref, x_ref, e_ref
):
    invert_in_place(m_ref, x_ref, e_ref)
    finish(
        l_ref[...], r_ref[...], mr_ref[...], lambda: ff_ref[...], lambda: ll_ref[...],
        fr_ref[...], lr_ref[...], x_ref, block_ref, vector_ref, gl_ref, gr_ref, gs_ref
    )


def merge_kernel(
    flag_ref, own_ref, other_ref, ov_ref, pv_ref,
    block_ref, vector_ref, gl_ref, gr_ref, gs_ref, x_ref, e_ref, m_ref
):
    width = x_ref.shape[0]
    is_upper = flag_ref[0] == 1
    spans = [pl.ds(k * width, width) for k in range(2)]
    row_ids = lax.broadcasted_iota(jnp.int32, (width, width), 0)
    col_ids = lax.broadcasted_iota(jnp.int32, (width, width), 1)
    lower_rhs = jnp.where(is_upper, pv_ref[...], ov_ref[...])
    upper_rhs = jnp.where(is_upper, ov_ref[...], pv_ref[...])

    def lower(k):
        return jnp.where(is_upper, other_ref[spans[k], :], own_ref[spans[k], :])

    def upper(k):
        return jnp.where(is_upper, own_ref[spans[k], :], other_ref[spans[k], :])

    m_ref[...] = unpack_last(lower(0), lower_rhs[2:3], row_ids, col_ids) + unpack_first(
        upper(0), row_ids, col_ids
    )
    invert_in_place(m_ref, x_ref, e_ref)
    finish(
        lower(1), upper(1), lower_rhs[1:2] + upper_rhs[0:1], lambda: unpack_first(lower(0), row_ids, col_ids),
        lambda: unpack_last(upper(0), upper_rhs[2:3], row_ids, col_ids),
        lower_rhs[0:1], upper_rhs[1:2], x_ref, block_ref, vector_ref, gl_ref, gr_ref, gs_ref
    )


def call_merge(kernel, name, width, parts, scratch, in_specs=None):
    full = jax.ShapeDtypeStruct((width, width), jnp.float32)
    result = pl.pallas_call(
        kernel,
        out_shape=(
            jax.ShapeDtypeStruct((2 * width, width), jnp.float32),
            jax.ShapeDtypeStruct((3, width), jnp.float32),
            full, full, jax.ShapeDtypeStruct((1, width), jnp.float32),
        ),
        in_specs=in_specs or [pl.BlockSpec(memory_space=pltpu.VMEM)] * len(parts),
        scratch_shapes=[pltpu.VMEM((width, width), jnp.float32)] * scratch,
        compiler_params=pltpu.CompilerParams(vmem_limit_bytes=48 << 20),
        name=name,
    )(*parts)
    return result[:2], result[2:]


def eliminate(*parts):
    return call_merge(
        first_kernel, "eliminate", parts[0].shape[0],
        [part if part.ndim == 2 else part[None] for part in parts], 2
    )


def merge(upper_flag, own, other):
    vmem = pl.BlockSpec(memory_space=pltpu.VMEM)
    return call_merge(
        merge_kernel, "merge", own[0].shape[1],
        [upper_flag.astype(jnp.int32)[None], own[0], other[0], own[1], other[1]], 3,
        [pl.BlockSpec(memory_space=pltpu.SMEM)] + [vmem] * 4
    )


def exchange(block, vector, core, level):
    if level == 0:
        return from_partner((block, vector), "tm", level)
    half = block.shape[0] // 2
    share = lax.dynamic_slice_in_dim(block, core * half, half, axis=0)
    received, other_vector = from_partner((share, vector), "tm", level)
    swapped = from_partner(received, "tm", 0)
    other = jnp.where(
        core == 1,
        jnp.concatenate([swapped, received]),
        jnp.concatenate([received, swapped]),
    )
    return other, other_vector


def gather_rows(rows, level_count):
    place = lax.axis_index("tm")
    held = rows[None]
    for level in reversed(range(level_count)):
        other = from_partner(held, "tm", level)
        upper_flag = jnp.bitwise_and(jnp.right_shift(place, level), 1) == 1
        held = jnp.stack([jnp.where(upper_flag, other, held), jnp.where(upper_flag, held, other)])
        held = held.reshape((-1,) + rows.shape)
    bits = held.reshape((2,) * level_count + rows.shape)
    order = tuple(reversed(range(level_count))) + (level_count, level_count + 1)
    return bits.transpose(order).reshape(-1, rows.shape[1])


def root_kernel(m_ref, mr_ref, o_ref, x_ref, e_ref):
    invert_in_place(m_ref, x_ref, e_ref)
    o_ref[...] = dot_exact(jnp.broadcast_to(mr_ref[...], (8, m_ref.shape[0])), x_ref[...])[:1]


def root_solve(matrix, rhs):
    width = matrix.shape[0]
    return pl.pallas_call(
        root_kernel,
        out_shape=jax.ShapeDtypeStruct((1, width), jnp.float32),
        scratch_shapes=[pltpu.VMEM((width, width), jnp.float32)] * 2,
        compiler_params=pltpu.CompilerParams(vmem_limit_bytes=48 << 20),
        name="root",
    )(matrix, rhs)


def direct_device(states, gradient, active_mask, zone_weight, zone_map, w_in, w_out, bias):
    width = states.shape[1]
    devices = lax.axis_size("tm")
    place = lax.axis_index("tm")
    is_first = place == 0
    is_last = place == devices - 1
    zone_count = zone_weight.shape[1]
    zone_table = (
        zone_map[None, :] == lax.broadcasted_iota(jnp.int32, (zone_count, width), 0)
    ).astype(jnp.float32)
    weights = jnp.dot(zone_weight, zone_table, precision=lax.Precision.HIGHEST) * (
        1.0 + 4.0 * active_mask.astype(jnp.float32)
    )
    later = jnp.stack([states[1].astype(jnp.float32), gradient[1], weights[1]])
    before = lax.ppermute(later, "tm", [(i, i + 1) for i in range(devices - 1)])
    whole_rows = gather_rows(w_in, devices.bit_length() - 1)
    rows = jnp.stack([before[0].astype(jnp.bfloat16), states[0]])
    hidden_in = jnp.dot(rows, whole_rows, preferred_element_type=jnp.float32) + bias
    slopes = (1.0 - jnp.tanh(hidden_in) ** 2).astype(jnp.bfloat16)
    weighted = slopes[:, None, :] * whole_rows[None, :, :]
    flat = weighted.reshape(2 * width, whole_rows.shape[1])
    product = jnp.dot(flat, w_out, preferred_element_type=jnp.float32).reshape(2, width, width)
    eye = jnp.eye(width, dtype=jnp.float32)
    jac_before = product[0] + eye
    jac_own = product[1] + eye
    last_diag = 1.0 / (1.0 + weights[1])
    column_scale = jnp.where(is_last, weights[1] * last_diag, 1.0)
    tail = jnp.where(is_last, gradient[1] * last_diag, 0.0)
    middle = (
        jnp.diag(weights[0] + jnp.where(is_first, 0.0, 1.0))
        + matmul(jac_own * column_scale[None, :], jac_own.T)
    )
    middle_rhs = gradient[0] + matmul(jac_own, tail)
    left = jnp.where(is_first, 0.0, -jac_before)
    right = jnp.where(is_last, 0.0, -jac_own)
    first_first = jnp.diag(before[2]) + matmul(left, left.T)
    own, local_store = eliminate(
        middle, middle_rhs, left, right, first_first, eye, before[1], jnp.zeros_like(middle_rhs)
    )
    core = jnp.bitwise_and(place, 1)
    level_count = devices.bit_length() - 1
    level_stores = []
    for level in range(level_count):
        upper_flag = jnp.bitwise_and(jnp.right_shift(place, level), 1) == 1
        if level == level_count - 1:
            row_ids = lax.broadcasted_iota(jnp.int32, (width, width), 0)
            packed, flipped = own[0][:width], own[0][:width].T
            keep = jnp.where(upper_flag, row_ids <= row_ids.T, row_ids > row_ids.T)
            block = jnp.where(keep, packed, flipped)
            block = jnp.where((row_ids == row_ids.T) & ~upper_flag, own[1][2:3], block)
            vector = jnp.where(upper_flag, own[1][:1], own[1][1:2])
            other_block, other_vector = exchange(block, vector, core, level)
            root = root_solve(block + other_block, vector + other_vector)[0]
            break
        own, store = merge(upper_flag, own, exchange(own[0], own[1], core, level))
        level_stores.append((store, upper_flag))
    top_flag = jnp.right_shift(place, level_count - 1) == 1
    start = jnp.where(top_flag, root, 0.0)
    end = jnp.where(top_flag, 0.0, root)
    for store, upper_flag in reversed(level_stores):
        value = back_solve(store, start, end)
        start = jnp.where(upper_flag, value, start)
        end = jnp.where(upper_flag, end, value)
    value = back_solve(local_store, start, end)
    end = jnp.where(is_last, tail + last_diag * matmul(value, jac_own), end)
    return jnp.stack([value, end], axis=0)


def back_solve(store, outer_first, outer_last):
    left_solved, right_solved, rhs_solved = store
    return rhs_solved[0] - matmul(outer_first, left_solved) - matmul(right_solved, outer_last)


MESH = pl.DeviceIdType.MESH
F32 = jnp.float32
BF16 = jnp.bfloat16


def low(x):
    return x.astype(BF16)


def dot1(a, b):
    return jnp.dot(a, b, preferred_element_type=F32)


def split(x):
    high = low(x)
    return high, low(x - high.astype(F32))


def dot3(a, b):
    ah, al = split(a)
    bh, bl = split(b)
    return dot1(jnp.concatenate([ah, ah, al], axis=1), jnp.concatenate([bh, bl, bh], axis=0))


def row_to_column(row, m):
    return jnp.sum(m * row, axis=1, keepdims=True)


def column_to_row(column, m):
    return jnp.sum(m * column, axis=0, keepdims=True)


def to_column(row):
    return row_to_column(row, jnp.where(diagonal_mask(row.shape[1]), 1.0, 0.0))


def to_row(column):
    return column_to_row(column, jnp.where(diagonal_mask(column.shape[0]), 1.0, 0.0))


def row_dot(row, m):
    return column_to_row(to_column(row), m)


def total(x):
    return jnp.sum(jnp.sum(x, axis=1, keepdims=True), axis=0, keepdims=True)


def diagonal_mask(width):
    return lax.broadcasted_iota(jnp.int32, (width, width), 0) == lax.broadcasted_iota(
        jnp.int32, (width, width), 1
    )


def invert(b_ref, delta, least, steps, fine, reach, x_ref, pair_ref):
    width = b_ref.shape[0]
    eye = diagonal_mask(width)

    def on_diagonal(value):
        return jnp.where(eye, value, 0.0)

    whole = b_ref[...]
    coarse = low(whole)
    square = dot1(coarse, coarse)
    most = delta + jnp.sqrt(jnp.sqrt(total(square * square)))
    alpha = 2.0 / (least + most)
    error = (most - least) / (most + least)
    rest = 1.0 - alpha * delta
    factor = 2.0 / (2.0 - error * error)
    x = factor * alpha * (on_diagonal(1.0 + rest) - alpha * whole)
    e = on_diagonal(1.0 - factor + factor * rest * rest) + factor * (
        alpha * alpha * square - 2.0 * alpha * rest * whole
    )
    x_ref[...] = x
    pair_ref[:width] = low(x)
    pair_ref[width:] = low(e)

    def step(_, err):
        c = 2.0 / (2.0 - err * err)
        product = dot1(pair_ref[...], pair_ref[width:])
        x = c * (x_ref[...] + product[:width])
        x_ref[...] = x
        pair_ref[:width] = low(x)
        pair_ref[width:] = low(on_diagonal(1.0 - c) + c * product[width:])
        return err * err / (2.0 - err * err)

    error = lax.fori_loop(0, steps - 2, step, error * error / (2.0 - error * error))
    c = 2.0 / (2.0 - error * error)
    x_ref[...] = c * (x_ref[...] + dot1(pair_ref[:width], pair_ref[width:]))
    error = error * error / (2.0 - error * error)

    def polish(_, unused):
        x = x_ref[...]
        residual = on_diagonal(1.0) - delta * x - dot3(b_ref[...], x)
        x_ref[...] = x + dot1(low(x), low(residual))
        return total(residual * residual)

    residual = lax.fori_loop(0, fine, polish, jnp.zeros((1, 1), F32))
    return jnp.maximum(bad_if(error, reach), bad_if(residual, 0.2))


def bad_if(value, limit):
    return jnp.where(value <= limit, 0.0, 1.0)


def merge_chains(left, right, out, x_ref, b_ref, pair_ref, steps, fine, reach, before_products):
    b_ref[...] = dot1(low(right[1][...]), low(left[0][...]))
    failed = invert(b_ref, 1.0, 1.0, steps, fine, reach, x_ref, pair_ref)
    before_products()
    carried = dot3(left[2][...], x_ref[...])
    transposed = dot3(carried, right[2][...])
    out[2][...] = transposed
    out[3][...] = jnp.transpose(transposed)
    out[1][...] = dot3(dot3(carried, right[1][...]), left[3][...]) + left[1][...]
    spread = dot3(left[0][...], x_ref[...])
    out[0][...] = dot3(dot3(right[3][...], spread), right[2][...]) + right[0][...]
    b1, e1, b2, e2 = left[4](), left[5](), right[4](), right[5]()
    b1_column = to_column(b1)
    row = column_to_row(b1_column + row_to_column(e2, left[0][...]), x_ref[...])
    b = to_row(row_to_column(row, right[3][...])) + b2
    row = e2 - column_to_row(b1_column, right[1][...])
    e = to_row(row_to_column(row, carried)) + e1
    return b, e, failed


def open_chain(left, right, x_ref, x, lam):
    t = row_dot(lam, right[3][...]) + right[5]()
    drift = row_to_column(x, left[3][...]) + to_column(left[4]()) + row_to_column(t, left[0][...])
    middle = column_to_row(drift, x_ref[...])
    return middle, t - row_dot(middle, right[1][...])


def fast_kernel(
    devices, greenhouses, rows_in,
    states_ref, gradient_ref, mask_ref, zone_ref, map_ref, own_ref, bias_ref, wout_hbm,
    out_ref, bad_ref,
    parts, whole, wout, small, sect, slope, k_ref, kt_ref, leaf, leaf_v, chain, chain_a, chain_v, top, top_v,
    x0_ref, x1_ref, x2_ref, xr_ref, b_ref, pair_ref, side, side_v, z_ref, z_v, zo_ref, zo_v, zout, zout_v,
    pack_out, pack_in, pack_v, o_buf, o_in, result, result_in, flags,
    w_send, w_recv, s_send, s_recv, local_sem, c_send, c_recv, p_send, p_recv, q_send, q_recv, v_send, v_recv,
    o_send, o_recv, r_send, r_recv, f_send, f_recv,
):
    width = states_ref.shape[1]
    groups = devices // 4
    me = lax.axis_index("tm")
    house = lax.axis_index("scen")
    g = lax.div(me, 4)
    r = lax.rem(me, 4)
    c = lax.rem(r, 2)
    y = lax.div(r, 2)
    core = me + 1 - 2 * c
    across = me + 2 - 4 * y
    diagonal = across + 1 - 2 * c
    is_left = g < groups // 2
    depth = jnp.where(is_left, g, groups - 1 - g)
    inward = me + jnp.where(is_left, 4, -4)
    outward = me - jnp.where(is_left, 4, -4)
    is_root = depth == groups // 2 - 1
    is_end = depth == 0
    right_end = jnp.logical_and(is_end, jnp.logical_not(is_left))
    left_end = jnp.logical_and(is_end, is_left)
    solves = jnp.logical_not(right_end)
    writes = y == c

    def remote(src, dst, send, recv, target):
        return pltpu.make_async_remote_copy(
            src_ref=src, dst_ref=dst, send_sem=send, recv_sem=recv, device_id=target, device_id_type=MESH
        )

    cleanup = []

    wout_copy = pltpu.make_async_copy(wout_hbm, wout, local_sem)
    wout_copy.start()

    barrier = pltpu.get_barrier_semaphore()

    def greet(target):
        pl.semaphore_signal(barrier, inc=1, device_id=target, device_id_type=MESH)

    for target in (core, across, diagonal):
        greet({"tm": target})
    for k in range(1, greenhouses):
        greet({"scen": lax.rem(house + k, greenhouses)})

    for k in range(1, groups):
        greet({"tm": 4 * lax.rem(g + k, groups) + r})

    weights = jnp.zeros(gradient_ref.shape, F32)
    for zone in range(zone_ref.shape[1]):
        weights = jnp.where(map_ref[...][None] == zone, zone_ref[:, zone : zone + 1], weights)
    weights = weights * (1.0 + 4.0 * mask_ref[...].astype(F32))
    small[r] = jnp.zeros((8, width), F32)
    small[r, 0:2] = states_ref[...].astype(F32)
    small[r, 2:4] = gradient_ref[...]
    small[r, 4:6] = weights
    mine = own_ref[...].astype(F32)
    chunks, _, span = parts.shape[2:]
    pieces = mine.shape[1] // span
    folded = low(jnp.concatenate([mine[:, k * span : (k + 1) * span] for k in range(pieces)], axis=0))
    for j in range(chunks):
        parts[g, r, j] = folded[16 * j : 16 * j + 16]
    sect[...] = jnp.zeros_like(sect)

    pl.semaphore_wait(barrier, 3 + greenhouses - 1 + groups - 1)

    shared = greenhouses == 2 and chunks == 3
    some = pl.ds(house, 2) if shared else pl.ds(0, chunks)
    alone = 2 * house
    missing = 2 - 2 * house
    other = lax.rem(r + 2, 4)

    def line_copy(k, way, sender):
        block = parts.at[sender, r, some]
        return remote(block, block, w_send.at[way, k], w_recv.at[0, sender], {"tm": me + 4 * k * (1 - 2 * way)})

    def across_copy(sender, row):
        block = parts.at[sender, row, some]
        return remote(block, block, w_send.at[2, sender], w_recv.at[1, sender], {"tm": across})

    def hand_copy(sender, row, which_row, chunk):
        block = parts.at[sender, row, chunk]
        return remote(block, block, w_send.at[3 + which_row, sender], w_recv.at[2 + which_row, sender], {"scen": 1 - house})

    def core_copy(row, k, chunk):
        block = parts.at[:, row, chunk]
        return remote(block, block, w_send.at[5, k], w_recv.at[4, k], {"tm": core})

    small_copies = [
        remote(small.at[r], small.at[r], s_send.at[k], s_recv.at[r], {"tm": target})
        for k, target in enumerate((core, across, diagonal))
    ]

    def begin(copy):
        copy.start()

    def end(copy):
        copy.wait_send()

    def by_distance(visit, least=1):
        for k in range(least, groups):
            if k == 0:
                visit(0, g)
                continue

            @pl.when(g >= k)
            def _():
                visit(k, g - k)

            @pl.when(g + k <= groups - 1)
            def _():
                visit(k, g + k)

    def line(act):
        act(across_copy(g, r))
        for k in range(1, groups):
            for way in range(2):
                @pl.when(g + k <= groups - 1 if way == 0 else g >= k)
                def _():
                    act(line_copy(k, way, g))
        if act is begin:
            for copy in small_copies:
                copy.start()

        def from_line(k, sender):
            if act is begin:
                line_copy(k, 0, sender).wait_recv()
            act(across_copy(sender, r))
            if shared:
                act(hand_copy(sender, r, 0, alone))

        by_distance(from_line)
        act(core_copy(r, 0, some))

        def from_across(k, sender):
            if act is begin:
                across_copy(sender, other).wait_recv()
            if shared:
                act(hand_copy(sender, other, 1, alone))

        by_distance(from_across, 0)
        act(core_copy(other, 1, some))
        if shared:
            if act is begin:
                by_distance(lambda k, sender: hand_copy(sender, r, 0, missing).wait_recv())
            act(core_copy(r, 2, missing))
            if act is begin:
                by_distance(lambda k, sender: hand_copy(sender, other, 1, missing).wait_recv(), 0)
            act(core_copy(other, 3, missing))

    line(begin)
    cleanup.append(lambda: line(end))
    cleanup.append(lambda: [copy.wait_send() for copy in small_copies] and None)
    beside = lax.rem(core, 4)
    beyond = lax.rem(diagonal, 4)
    core_copy(beside, 0, some).wait_recv()
    core_copy(beyond, 1, some).wait_recv()
    if shared:
        core_copy(beside, 2, missing).wait_recv()
        core_copy(beyond, 3, missing).wait_recv()
    for target in (core, across, diagonal):
        remote(small.at[r], small.at[lax.rem(target, 4)], s_send.at[0], s_recv.at[lax.rem(target, 4)], {"tm": core}).wait_recv()

    batch = next(q for q in range(1, 17) if q * rows_in % 16 == 0)
    for first in range(0, devices, batch):
        blocks = [
            jnp.concatenate([parts[(first + k) // 4, (first + k) % 4, j].astype(F32) for j in range(chunks)], axis=0) for k in range(batch)
        ]
        for j in range(pieces):
            tall = jnp.concatenate([block[j * rows_in : (j + 1) * rows_in] for block in blocks], axis=0)
            whole[first * rows_in : (first + batch) * rows_in, j * span : (j + 1) * span] = low(tall)

    for k in range(3):
        sect[k, 0:2] = small[2 * c, 2 * k : 2 * k + 2]
        sect[k, 2:4] = small[2 * c + 1, 2 * k : 2 * k + 2]
    hidden = dot1(low(sect[0]), whole[...]) + bias_ref[...][None]
    bent = jnp.tanh(hidden)
    slope[...] = low(1.0 - bent * bent).astype(F32)
    wout_copy.wait()

    def section(t, carry):
        weighted = whole[...] * low(slope[pl.ds(t, 1), :])
        product = dot1(weighted, wout[...])
        k_ref[t] = product
        kt_ref[t] = jnp.transpose(product)
        return carry

    lax.fori_loop(0, 4, section, 0)

    eye = diagonal_mask(width)

    def on_diagonal(row):
        return jnp.where(eye, row, 0.0)

    def column(row):
        return jnp.sum(on_diagonal(row), axis=1, keepdims=True)

    def pair(q, carry):
        w0, w1 = sect[2, pl.ds(2 * q, 1)], sect[2, pl.ds(2 * q + 1, 1)]
        g0, g1 = sect[1, pl.ds(2 * q, 1)], sect[1, pl.ds(2 * q + 1, 1)]
        d = 1.0 / (1.0 + w1)
        dw = w1 * d
        k0, k1, k0t, k1t = k_ref[2 * q], k_ref[2 * q + 1], kt_ref[2 * q], kt_ref[2 * q + 1]
        scaled = column(d) * k1
        transposed = on_diagonal(d) + k0 * d + scaled + dot1(low(k0 * d), low(k1))
        leaf[q, 2] = transposed
        leaf[q, 3] = jnp.transpose(transposed)
        leaf[q, 0] = on_diagonal(1.0 + d) + scaled + k1t * d + dot1(low(k1t * d), low(k1))
        light = k0 * dw
        leaf[q, 1] = on_diagonal(w0 + dw) + light + column(dw) * k0t + dot1(low(light), low(k0t))
        rhs = d * g1
        rhs_column = to_column(rhs)
        leaf_v[q, 0:1] = rhs + column_to_row(rhs_column, k1)
        leaf_v[q, 1:2] = rhs + column_to_row(rhs_column, k0t) + g0
        return carry

    lax.fori_loop(0, 2, pair, 0)

    def chain_of(quad, fourth, vector):
        return [quad.at[0], quad.at[1], quad.at[2], fourth, lambda: vector[0:1], lambda: vector[1:2]]

    lower, upper = (chain_of(leaf.at[q], leaf.at[q, 3], leaf_v.at[q]) for q in range(2))
    mine = chain_of(chain.at[c], chain_a.at[c], chain_v.at[c])
    b, e, failed = merge_chains(lower, upper, mine, x0_ref, b_ref, pair_ref, 2, 0, 1e-3, lambda: None)
    chain_v[c] = jnp.zeros((8, width), F32)
    chain_v[c, 0:1] = b
    chain_v[c, 1:2] = e
    chain_v[c, 2:3] = jnp.broadcast_to(failed, (1, width))

    def chain_copy(slot, k):
        return remote(chain.at[slot, k], chain.at[slot, k], c_send.at[k], c_recv.at[k], {"tm": core})

    def vector_copy(slot):
        return remote(chain_v.at[slot], chain_v.at[slot], c_send.at[3], c_recv.at[3], {"tm": core})

    chain_copy(c, c).start()
    chain_copy(c, 1 - c).start()
    chain_copy(c, 2).start()
    vector_copy(c).start()
    cleanup.append(lambda: [chain_copy(c, k).wait_send() for k in range(3)] and None)
    cleanup.append(lambda: vector_copy(c).wait_send())
    chain_copy(1 - c, 1 - c).wait_recv()

    def rest_arrived():
        chain_copy(1 - c, c).wait_recv()
        chain_copy(1 - c, 2).wait_recv()
        vector_copy(1 - c).wait_recv()
        chain_a[1 - c] = jnp.transpose(chain[1 - c, 2])

    first, second = (chain_of(chain.at[q], chain_a.at[q], chain_v.at[q]) for q in range(2))
    b, e, failed = merge_chains(first, second, chain_of(top, top.at[3], top_v), x1_ref, b_ref, pair_ref, 3, 1, 0.02, rest_arrived)
    bad = jnp.maximum(jnp.maximum(chain_v[0, 2:3], chain_v[1, 2:3]), failed)

    sign = jnp.where(is_left, 1.0, -1.0)
    for k, (a_index, b_index) in enumerate(((3, 2), (2, 3), (1, 0), (0, 1))):
        side[k] = jnp.where(is_left, top[a_index], top[b_index])
    side_v[0:1] = jnp.where(is_left, e, -b)
    side_v[1:2] = jnp.where(is_left, b, e)
    side_v[2:3] = bad

    blocks = width // 128
    tiles = [(i, j) for i in range(blocks) for j in range(i + 1)]
    half = len(tiles) // 2

    def tile_copy(which, k):
        return remote(pack_out.at[k], pack_in.at[which, k], p_send.at[k], p_recv.at[which, k], {"tm": inward})

    def tile_pass(which, k):
        return remote(pack_in.at[which, k], pack_in.at[which, k], q_send.at[which, k], q_recv.at[which, k], {"tm": core})

    def row_copy(which):
        return remote(zout_v, pack_v.at[which], v_send, v_recv.at[which], {"tm": inward})

    def receive(which, m_ref, row_ref):
        for j in range(half):
            tile_copy(which, 2 * j + c).wait_recv()
            tile_pass(which, 2 * j + c).start()
        for j in range(half):
            tile_pass(which, 2 * j + 1 - c).wait_recv()
        row_copy(which).wait_recv()
        for k, (i, j) in enumerate(tiles):
            tile = pack_in[which, k]
            m_ref[128 * i : 128 * i + 128, 128 * j : 128 * j + 128] = tile
            if i != j:
                m_ref[128 * j : 128 * j + 128, 128 * i : 128 * i + 128] = jnp.transpose(tile)
        row_ref[...] = pack_v[which]

    @pl.when(is_end)
    def _():
        z_ref[...] = jnp.where(eye, 1.0, 0.0)
        z_v[...] = jnp.zeros_like(z_v)

    @pl.when(jnp.logical_not(is_end))
    def _():
        receive(0, z_ref, z_v)

    @pl.when(solves)
    def _():
        delta = jnp.where(left_end, 0.0, 1.0)
        floor = jnp.min(small[0, 4:5], axis=1, keepdims=True)
        least = jnp.where(left_end, floor, 1.0)
        b_ref[...] = dot3(side[2], z_ref[...])
        failed = invert(b_ref, delta, least, jnp.where(left_end, 6, 5), 2, 0.2, x2_ref, pair_ref)
        reach = dot3(side[0], dot3(z_ref[...], x2_ref[...]))
        zout[...] = dot3(reach, side[1]) + side[3]
        v = side_v[0:1]
        row = column_to_row(to_column(z_v[0:1]) + row_to_column(v, z_ref[...]), x2_ref[...])
        zout_v[...] = jnp.zeros_like(zout_v)
        zout_v[0:1] = to_row(row_to_column(row, side[0])) + side_v[1:2]
        zout_v[2:3] = jnp.maximum(jnp.maximum(side_v[2:3], z_v[2:3]), failed)

    @pl.when(right_end)
    def _():
        zout[...] = side[3]
        zout_v[...] = jnp.zeros_like(zout_v)
        zout_v[0:1] = side_v[1:2]
        zout_v[2:3] = side_v[2:3]

    for k, (i, j) in enumerate(tiles):
        pack_out[k] = zout[128 * i : 128 * i + 128, 128 * j : 128 * j + 128]
    which = is_root.astype(jnp.int32)
    for j in range(half):
        tile_copy(which, 2 * j + c).start()
    row_copy(which).start()

    def tiles_sent():
        for j in range(half):
            tile_copy(which, 2 * j + c).wait_send()
        row_copy(which).wait_send()

        @pl.when(jnp.logical_not(is_end))
        def _():
            for j in range(half):
                tile_pass(0, 2 * j + c).wait_send()

    cleanup.append(tiles_sent)
    def outer_copy():
        return remote(o_buf, o_in, o_send, o_recv, {"tm": outward})

    flag_copies = [remote(flags.at[0], flags.at[1], f_send.at[0], f_recv.at[0], {"tm": inward})]
    for k in range(1, greenhouses):
        flag_copies.append(
            remote(flags.at[2], flags.at[2 + k], f_send.at[k], f_recv.at[k], {"scen": lax.rem(house + k, greenhouses)})
        )
    last = 2 + greenhouses
    flag_out = remote(flags.at[last], flags.at[last], f_send.at[greenhouses], f_recv.at[greenhouses], {"tm": outward})

    @pl.when(is_root)
    def _():
        receive(1, zo_ref, zo_v)
        b_ref[...] = dot3(zo_ref[...], zout[...])
        invert(b_ref, 1.0, 1.0, 5, 1, 0.3, xr_ref, pair_ref)
        rhs = to_column(zout_v[0:1]) + sign * row_to_column(zo_v[0:1], zout[...])
        value = column_to_row(rhs, xr_ref[...])
        for _ in range(2):
            column_now = to_column(value)
            left_over = rhs - column_now - row_to_column(column_to_row(column_now, zo_ref[...]), zout[...])
            value = value + column_to_row(left_over, xr_ref[...])
        failed = bad_if(total(left_over * left_over), 1e-4 * total(rhs * rhs))
        o_in[0:1] = zo_v[0:1] - sign * row_dot(value, zo_ref[...])
        flags[0] = jnp.broadcast_to(
            jnp.maximum(jnp.maximum(zout_v[2:3, :128], zo_v[2:3, :128]), failed), (8, 128)
        )
        flag_copies[0].start()

    @pl.when(jnp.logical_not(is_root))
    def _():
        outer_copy().wait_recv()

    outer = o_in[0:1]
    side_v[3:4] = jnp.zeros((1, width), F32)

    @pl.when(solves)
    def _():
        w = sign * side_v[0:1] + row_dot(outer, side[0])
        value = column_to_row(to_column(z_v[0:1]) + sign * row_to_column(w, z_ref[...]), x2_ref[...])
        side_v[3:4] = value
        o_buf[...] = jnp.broadcast_to(w - sign * row_dot(value, side[2]), o_buf.shape)

    @pl.when(jnp.logical_not(is_end))
    def _():
        outer_copy().start()

    @pl.when(is_root)
    def _():
        flag_copies[0].wait_recv()
        flags[2] = jnp.maximum(flags[0], flags[1])
        for copy in flag_copies[1:]:
            copy.start()

    own_value = side_v[3:4]
    start = jnp.where(is_left, own_value, outer)
    finish_lam = jnp.where(is_left, outer, own_value)

    def result_copy(slot):
        return remote(result.at[slot], result_in, r_send, r_recv, {"tm": core})

    @pl.when(writes)
    def _():
        middle, lam = open_chain(first, second, x1_ref, start, finish_lam)
        x_a = jnp.where(c == 0, start, middle)
        lam_b = jnp.where(c == 0, lam, finish_lam)
        middle, lam = open_chain(lower, upper, x0_ref, x_a, lam_b)
        for q, x, lam_q in ((0, x_a, lam), (1, middle, lam_b)):
            w1, g1 = sect[2, 2 * q + 1 : 2 * q + 2], sect[1, 2 * q + 1 : 2 * q + 2]
            result[q, 0:1] = x
            result[q, 1:2] = (
                x + row_dot(x, k_ref[2 * q]) + lam_q + row_dot(lam_q, kt_ref[2 * q + 1]) + g1
            ) / (1.0 + w1)
        result_copy(1 - c).start()
        out_ref[...] = result[c, 0:2]

    @pl.when(jnp.logical_not(writes))
    def _():
        result_copy(0).wait_recv()
        out_ref[...] = result_in[0:2]

    @pl.when(is_root)
    def _():
        for copy in flag_copies[1:]:
            copy.wait_recv()
        worst = flags[2]
        for k in range(1, greenhouses):
            worst = jnp.maximum(worst, flags[2 + k])
        flags[last] = worst

    @pl.when(jnp.logical_not(is_root))
    def _():
        flag_out.wait_recv()

    @pl.when(jnp.logical_not(is_end))
    def _():
        flag_out.start()

    bad_ref[...] = flags[last, 0:1, 0:1]

    def rest_sent():
        @pl.when(jnp.logical_not(is_end))
        def _():
            outer_copy().wait_send()
            flag_out.wait_send()

        @pl.when(is_root)
        def _():
            for j in range(half):
                tile_pass(1, 2 * j + c).wait_send()
            for copy in flag_copies:
                copy.wait_send()

        @pl.when(writes)
        def _():
            result_copy(1 - c).wait_send()

    cleanup.append(rest_sent)
    for act in cleanup:
        act()

def fast_device(states, gradient, active_mask, zone_weight, zone_map, w_in, w_out, bias):
    width = states.shape[1]
    hidden = w_in.shape[1]
    devices = lax.axis_size("tm")
    greenhouses = lax.axis_size("scen")
    rows = w_in.shape[0]
    pieces = 16 // math.gcd(rows, 16)
    span = hidden // pieces
    chunks = pieces * rows // 16
    tiles = (width // 128) * (width // 128 + 1) // 2
    square = lambda *lead: pltpu.VMEM(lead + (width, width), F32)
    lines = lambda *lead: pltpu.VMEM(lead + (8, width), F32)
    dma = pltpu.SemaphoreType.DMA
    vmem = pl.BlockSpec(memory_space=pltpu.VMEM)
    scratch = [
        pltpu.VMEM((devices // 4, 4, chunks, 16, span), BF16), pltpu.VMEM((rows * devices, hidden), BF16), pltpu.VMEM(w_out.shape, BF16),
        lines(4), lines(3), pltpu.VMEM((8, hidden), F32), square(4), square(4), square(2, 4), lines(2),
        square(2, 3), square(2), lines(2), square(4), lines(),
        square(), square(), square(), square(), square(), pltpu.VMEM((2 * width, width), BF16), square(4), lines(),
        square(), lines(), square(), lines(), square(), lines(),
        pltpu.VMEM((tiles, 128, 128), F32), pltpu.VMEM((2, tiles, 128, 128), F32), lines(2), lines(), lines(), lines(2), lines(),
        pltpu.VMEM((3 + greenhouses, 8, 128), F32),
        dma((6, max(4, devices // 4))), dma((5, max(4, devices // 4))), dma((3,)), dma((4,)), dma, dma((4,)), dma((4,)), dma((tiles,)), dma((2, tiles)),
        dma((2, tiles)), dma((2, tiles)), dma, dma((2,)), dma, dma, dma, dma,
        dma((greenhouses + 1,)), dma((greenhouses + 1,)),
    ]
    return pl.pallas_call(
        functools.partial(fast_kernel, devices, greenhouses, rows),
        out_shape=(jax.ShapeDtypeStruct((2, width), F32), jax.ShapeDtypeStruct((1, 1), F32)),
        in_specs=[vmem] * 7 + [pl.BlockSpec(memory_space=pl.ANY)],
        out_specs=(vmem, vmem),
        scratch_shapes=scratch,
        compiler_params=pltpu.CompilerParams(collective_id=0, has_side_effects=True, vmem_limit_bytes=58 << 20),
        name="gauss_newton",
    )(states, gradient, active_mask, zone_weight, zone_map, w_in, bias, w_out)


def per_device(*arrays):
    value, bad = fast_device(*arrays)
    return lax.cond(bad[0, 0] > 0.0, lambda: direct_device(*arrays), lambda: value)


def solution(mesh):
    return jax.shard_map(
        per_device,
        mesh=mesh,
        in_specs=(
            P(("scen", "tm"), None),
            P(("scen", "tm"), None),
            P(("scen", "tm"), None),
            P(("scen", "tm"), None),
            P("scen"),
            P("tm", None),
            P(),
            P(),
        ),
        out_specs=P(("scen", "tm"), None),
        check_vma=False,
    )
```

```python
import functools
import math

import jax
import jax.numpy as jnp
from jax import lax
from jax.experimental import pallas as pl
from jax.experimental.pallas import tpu as pltpu
from jax.sharding import PartitionSpec as P


def from_partner(array, axis, bit):
    return lax.ppermute(array, axis, [(i, i ^ 1 << bit) for i in range(lax.axis_size(axis))])


def matmul(left, right):
    return jnp.dot(left, right, precision=lax.Precision.HIGHEST)


def dot_exact(left, right, dims=((1,), (0,))):
    return lax.dot_general(
        left, right, (dims, ((), ())), precision=lax.Precision.HIGHEST, preferred_element_type=jnp.float32
    )


def dot_fast(left, right):
    return jnp.dot(
        left.astype(jnp.bfloat16), right.astype(jnp.bfloat16), preferred_element_type=jnp.float32
    )


def invert_in_place(m_ref, x_ref, e_ref):
    width = m_ref.shape[0]
    row_ids = lax.broadcasted_iota(jnp.int32, (width, width), 0)
    col_ids = lax.broadcasted_iota(jnp.int32, (width, width), 1)
    diagonal = row_ids == col_ids
    matrix = m_ref[...]
    square = dot_fast(matrix, matrix)
    trace = jnp.sum(jnp.where(diagonal, matrix, 0.0))
    frobenius = jnp.sum(matrix * matrix)
    bound = jnp.max(jnp.sum(jnp.abs(square), axis=1))
    scale = jnp.minimum(trace / frobenius, 1.9 * lax.rsqrt(bound))
    x_ref[...] = jnp.where(diagonal, 2.0 * scale, 0.0) - (scale * scale) * matrix
    first = jnp.where(diagonal, 1.0, 0.0) - (2.0 * scale) * matrix + (scale * scale) * square
    e_ref[...] = first

    def coarse_step(carry):
        count, _ = carry
        x_ref[...] = x_ref[...] + dot_fast(x_ref[...], e_ref[...])
        residual = jnp.where(diagonal, 1.0, 0.0) - dot_fast(m_ref[...], x_ref[...])
        e_ref[...] = residual
        return count + 1, jnp.sum(residual * residual)

    lax.while_loop(lambda c: (c[0] < 10) & (c[1] > 0.25), coarse_step, (0, jnp.sum(first * first)))

    def fine_step(carry):
        count, _ = carry
        residual = jnp.where(diagonal, 1.0, 0.0) - dot_exact(m_ref[...], x_ref[...])
        x_ref[...] = x_ref[...] + dot_fast(x_ref[...], residual)
        return count + 1, jnp.sum(residual * residual)

    _, last = lax.while_loop(
        lambda c: (c[0] < 12) & jnp.logical_not(c[1] <= 1e-7), fine_step, (0, jnp.float32(1.0))
    )

    @pl.when(jnp.logical_not(last <= 1e-7))
    def _():
        x_ref[...] = m_ref[...]

        def pivot_step(k, carry):
            current = x_ref[...]
            row = x_ref[pl.ds(k, 1), :]
            column = jnp.sum(jnp.where(col_ids == k, current, 0.0), axis=1, keepdims=True)
            pivot = jnp.sum(jnp.where(col_ids[:1] == k, row, 0.0), axis=1, keepdims=True)
            scaled = row / pivot
            updated = jnp.where(col_ids == k, -column / pivot, current - column * scaled)
            own_row = jnp.where(col_ids == k, 1.0 / pivot, scaled)
            x_ref[...] = jnp.where(row_ids == k, own_row, updated)
            return carry

        lax.fori_loop(0, width, pivot_step, 0)


def unpack_first(packed, row_ids, col_ids):
    return jnp.where(row_ids <= col_ids, packed, jnp.transpose(packed))


def unpack_last(packed, diagonal, row_ids, col_ids):
    whole = jnp.where(row_ids > col_ids, packed, jnp.transpose(packed))
    return jnp.where(row_ids == col_ids, diagonal, whole)


def finish(left, right, rhs, ff, ll, fr, lr, x_ref, block_ref, vector_ref, gl_ref, gr_ref, gs_ref):
    width = x_ref.shape[0]
    inverse = x_ref[...]
    gl_ref[...] = dot_exact(left, inverse)
    gr_ref[...] = dot_exact(inverse, right)
    solved = dot_exact(jnp.broadcast_to(rhs, (8, width)), inverse)
    gs_ref[...] = solved[:1]
    row_ids = lax.broadcasted_iota(jnp.int32, (width, width), 0)
    col_ids = lax.broadcasted_iota(jnp.int32, (width, width), 1)
    new_ff = ff() - dot_exact(gl_ref[...], left, ((1,), (1,)))
    block_ref[width : 2 * width] = -dot_exact(gl_ref[...], right)
    new_ll = ll() - dot_exact(jnp.transpose(right), gr_ref[...])
    block_ref[:width] = jnp.where(row_ids <= col_ids, new_ff, new_ll)
    vector_ref[2:3] = jnp.sum(jnp.where(row_ids == col_ids, new_ll, 0.0), axis=0, keepdims=True)
    vector_ref[0:1] = fr - dot_exact(solved, left, ((1,), (1,)))[:1]
    vector_ref[1:2] = lr - dot_exact(solved, right)[:1]


def first_kernel(
    m_ref, mr_ref, l_ref, r_ref, ff_ref, ll_ref, fr_ref, lr_ref,
    block_ref, vector_ref, gl_ref, gr_ref, gs_ref, x_ref, e_ref
):
    invert_in_place(m_ref, x_ref, e_ref)
    finish(
        l_ref[...], r_ref[...], mr_ref[...], lambda: ff_ref[...], lambda: ll_ref[...],
        fr_ref[...], lr_ref[...], x_ref, block_ref, vector_ref, gl_ref, gr_ref, gs_ref
    )


def merge_kernel(
    flag_ref, own_ref, other_ref, ov_ref, pv_ref,
    block_ref, vector_ref, gl_ref, gr_ref, gs_ref, x_ref, e_ref, m_ref
):
    width = x_ref.shape[0]
    is_upper = flag_ref[0] == 1
    spans = [pl.ds(k * width, width) for k in range(2)]
    row_ids = lax.broadcasted_iota(jnp.int32, (width, width), 0)
    col_ids = lax.broadcasted_iota(jnp.int32, (width, width), 1)
    lower_rhs = jnp.where(is_upper, pv_ref[...], ov_ref[...])
    upper_rhs = jnp.where(is_upper, ov_ref[...], pv_ref[...])

    def lower(k):
        return jnp.where(is_upper, other_ref[spans[k], :], own_ref[spans[k], :])

    def upper(k):
        return jnp.where(is_upper, own_ref[spans[k], :], other_ref[spans[k], :])

    m_ref[...] = unpack_last(lower(0), lower_rhs[2:3], row_ids, col_ids) + unpack_first(
        upper(0), row_ids, col_ids
    )
    invert_in_place(m_ref, x_ref, e_ref)
    finish(
        lower(1), upper(1), lower_rhs[1:2] + upper_rhs[0:1], lambda: unpack_first(lower(0), row_ids, col_ids),
        lambda: unpack_last(upper(0), upper_rhs[2:3], row_ids, col_ids),
        lower_rhs[0:1], upper_rhs[1:2], x_ref, block_ref, vector_ref, gl_ref, gr_ref, gs_ref
    )


def call_merge(kernel, name, width, parts, scratch, in_specs=None):
    full = jax.ShapeDtypeStruct((width, width), jnp.float32)
    result = pl.pallas_call(
        kernel,
        out_shape=(
            jax.ShapeDtypeStruct((2 * width, width), jnp.float32),
            jax.ShapeDtypeStruct((3, width), jnp.float32),
            full, full, jax.ShapeDtypeStruct((1, width), jnp.float32),
        ),
        in_specs=in_specs or [pl.BlockSpec(memory_space=pltpu.VMEM)] * len(parts),
        scratch_shapes=[pltpu.VMEM((width, width), jnp.float32)] * scratch,
        compiler_params=pltpu.CompilerParams(vmem_limit_bytes=48 << 20),
        name=name,
    )(*parts)
    return result[:2], result[2:]


def eliminate(*parts):
    return call_merge(
        first_kernel, "eliminate", parts[0].shape[0],
        [part if part.ndim == 2 else part[None] for part in parts], 2
    )


def merge(upper_flag, own, other):
    vmem = pl.BlockSpec(memory_space=pltpu.VMEM)
    return call_merge(
        merge_kernel, "merge", own[0].shape[1],
        [upper_flag.astype(jnp.int32)[None], own[0], other[0], own[1], other[1]], 3,
        [pl.BlockSpec(memory_space=pltpu.SMEM)] + [vmem] * 4
    )


def exchange(block, vector, core, level):
    if level == 0:
        return from_partner((block, vector), "tm", level)
    half = block.shape[0] // 2
    share = lax.dynamic_slice_in_dim(block, core * half, half, axis=0)
    received, other_vector = from_partner((share, vector), "tm", level)
    swapped = from_partner(received, "tm", 0)
    other = jnp.where(
        core == 1,
        jnp.concatenate([swapped, received]),
        jnp.concatenate([received, swapped]),
    )
    return other, other_vector


def gather_rows(rows, level_count):
    place = lax.axis_index("tm")
    held = rows[None]
    for level in reversed(range(level_count)):
        other = from_partner(held, "tm", level)
        upper_flag = jnp.bitwise_and(jnp.right_shift(place, level), 1) == 1
        held = jnp.stack([jnp.where(upper_flag, other, held), jnp.where(upper_flag, held, other)])
        held = held.reshape((-1,) + rows.shape)
    bits = held.reshape((2,) * level_count + rows.shape)
    order = tuple(reversed(range(level_count))) + (level_count, level_count + 1)
    return bits.transpose(order).reshape(-1, rows.shape[1])


def root_kernel(m_ref, mr_ref, o_ref, x_ref, e_ref):
    invert_in_place(m_ref, x_ref, e_ref)
    o_ref[...] = dot_exact(jnp.broadcast_to(mr_ref[...], (8, m_ref.shape[0])), x_ref[...])[:1]


def root_solve(matrix, rhs):
    width = matrix.shape[0]
    return pl.pallas_call(
        root_kernel,
        out_shape=jax.ShapeDtypeStruct((1, width), jnp.float32),
        scratch_shapes=[pltpu.VMEM((width, width), jnp.float32)] * 2,
        compiler_params=pltpu.CompilerParams(vmem_limit_bytes=48 << 20),
        name="root",
    )(matrix, rhs)


def direct_device(states, gradient, active_mask, zone_weight, zone_map, w_in, w_out, bias):
    width = states.shape[1]
    devices = lax.axis_size("tm")
    place = lax.axis_index("tm")
    is_first = place == 0
    is_last = place == devices - 1
    zone_count = zone_weight.shape[1]
    zone_table = (
        zone_map[None, :] == lax.broadcasted_iota(jnp.int32, (zone_count, width), 0)
    ).astype(jnp.float32)
    weights = jnp.dot(zone_weight, zone_table, precision=lax.Precision.HIGHEST) * (
        1.0 + 4.0 * active_mask.astype(jnp.float32)
    )
    later = jnp.stack([states[1].astype(jnp.float32), gradient[1], weights[1]])
    before = lax.ppermute(later, "tm", [(i, i + 1) for i in range(devices - 1)])
    whole_rows = gather_rows(w_in, devices.bit_length() - 1)
    rows = jnp.stack([before[0].astype(jnp.bfloat16), states[0]])
    hidden_in = jnp.dot(rows, whole_rows, preferred_element_type=jnp.float32) + bias
    slopes = (1.0 - jnp.tanh(hidden_in) ** 2).astype(jnp.bfloat16)
    weighted = slopes[:, None, :] * whole_rows[None, :, :]
    flat = weighted.reshape(2 * width, whole_rows.shape[1])
    product = jnp.dot(flat, w_out, preferred_element_type=jnp.float32).reshape(2, width, width)
    eye = jnp.eye(width, dtype=jnp.float32)
    jac_before = product[0] + eye
    jac_own = product[1] + eye
    last_diag = 1.0 / (1.0 + weights[1])
    column_scale = jnp.where(is_last, weights[1] * last_diag, 1.0)
    tail = jnp.where(is_last, gradient[1] * last_diag, 0.0)
    middle = (
        jnp.diag(weights[0] + jnp.where(is_first, 0.0, 1.0))
        + matmul(jac_own * column_scale[None, :], jac_own.T)
    )
    middle_rhs = gradient[0] + matmul(jac_own, tail)
    left = jnp.where(is_first, 0.0, -jac_before)
    right = jnp.where(is_last, 0.0, -jac_own)
    first_first = jnp.diag(before[2]) + matmul(left, left.T)
    own, local_store = eliminate(
        middle, middle_rhs, left, right, first_first, eye, before[1], jnp.zeros_like(middle_rhs)
    )
    core = jnp.bitwise_and(place, 1)
    level_count = devices.bit_length() - 1
    level_stores = []
    for level in range(level_count):
        upper_flag = jnp.bitwise_and(jnp.right_shift(place, level), 1) == 1
        if level == level_count - 1:
            row_ids = lax.broadcasted_iota(jnp.int32, (width, width), 0)
            packed, flipped = own[0][:width], own[0][:width].T
            keep = jnp.where(upper_flag, row_ids <= row_ids.T, row_ids > row_ids.T)
            block = jnp.where(keep, packed, flipped)
            block = jnp.where((row_ids == row_ids.T) & ~upper_flag, own[1][2:3], block)
            vector = jnp.where(upper_flag, own[1][:1], own[1][1:2])
            other_block, other_vector = exchange(block, vector, core, level)
            root = root_solve(block + other_block, vector + other_vector)[0]
            break
        own, store = merge(upper_flag, own, exchange(own[0], own[1], core, level))
        level_stores.append((store, upper_flag))
    top_flag = jnp.right_shift(place, level_count - 1) == 1
    start = jnp.where(top_flag, root, 0.0)
    end = jnp.where(top_flag, 0.0, root)
    for store, upper_flag in reversed(level_stores):
        value = back_solve(store, start, end)
        start = jnp.where(upper_flag, value, start)
        end = jnp.where(upper_flag, end, value)
    value = back_solve(local_store, start, end)
    end = jnp.where(is_last, tail + last_diag * matmul(value, jac_own), end)
    return jnp.stack([value, end], axis=0)


def back_solve(store, outer_first, outer_last):
    left_solved, right_solved, rhs_solved = store
    return rhs_solved[0] - matmul(outer_first, left_solved) - matmul(right_solved, outer_last)


MESH = pl.DeviceIdType.MESH
F32 = jnp.float32
BF16 = jnp.bfloat16


def low(x):
    return x.astype(BF16)


def dot1(a, b):
    return jnp.dot(a, b, preferred_element_type=F32)


def split(x):
    high = low(x)
    return high, low(x - high.astype(F32))


def dot3(a, b):
    ah, al = split(a)
    bh, bl = split(b)
    return dot1(jnp.concatenate([ah, ah, al], axis=1), jnp.concatenate([bh, bl, bh], axis=0))


def row_to_column(row, m):
    return jnp.sum(m * row, axis=1, keepdims=True)


def column_to_row(column, m):
    return jnp.sum(m * column, axis=0, keepdims=True)


def to_column(row):
    return row_to_column(row, jnp.where(diagonal_mask(row.shape[1]), 1.0, 0.0))


def to_row(column):
    return column_to_row(column, jnp.where(diagonal_mask(column.shape[0]), 1.0, 0.0))


def row_dot(row, m):
    return column_to_row(to_column(row), m)


def total(x):
    return jnp.sum(jnp.sum(x, axis=1, keepdims=True), axis=0, keepdims=True)


def diagonal_mask(width):
    return lax.broadcasted_iota(jnp.int32, (width, width), 0) == lax.broadcasted_iota(
        jnp.int32, (width, width), 1
    )


def invert(b_ref, delta, least, steps, fine, reach, limit, x_ref, pair_ref):
    width = b_ref.shape[0]
    eye = diagonal_mask(width)

    def on_diagonal(value):
        return jnp.where(eye, value, 0.0)

    whole = b_ref[...]
    coarse = low(whole)
    square = dot1(coarse, coarse)
    most = delta + jnp.sqrt(jnp.sqrt(total(square * square)))
    alpha = 2.0 / (least + most)
    error = (most - least) / (most + least)
    rest = 1.0 - alpha * delta
    factor = 2.0 / (2.0 - error * error)
    x = factor * alpha * (on_diagonal(1.0 + rest) - alpha * whole)
    e = on_diagonal(1.0 - factor + factor * rest * rest) + factor * (
        alpha * alpha * square - 2.0 * alpha * rest * whole
    )
    x_ref[...] = x
    pair_ref[:width] = low(x)
    pair_ref[width:] = low(e)

    def step(_, err):
        c = 2.0 / (2.0 - err * err)
        product = dot1(pair_ref[...], pair_ref[width:])
        x = c * (x_ref[...] + product[:width])
        x_ref[...] = x
        pair_ref[:width] = low(x)
        pair_ref[width:] = low(on_diagonal(1.0 - c) + c * product[width:])
        return err * err / (2.0 - err * err)

    error = lax.fori_loop(0, steps - 2, step, error * error / (2.0 - error * error))
    c = 2.0 / (2.0 - error * error)
    x_ref[...] = c * (x_ref[...] + dot1(pair_ref[:width], pair_ref[width:]))
    error = error * error / (2.0 - error * error)

    def polish(_, unused):
        x = x_ref[...]
        residual = on_diagonal(1.0) - delta * x - dot3(b_ref[...], x)
        rough = low(residual)
        x_ref[...] = x + dot1(low(x), low(residual + dot1(rough, rough)))
        return total(residual * residual)

    residual = lax.fori_loop(0, fine, polish, jnp.zeros((1, 1), F32))
    return jnp.maximum(bad_if(error, reach), bad_if(residual, limit))


def bad_if(value, limit):
    return jnp.where(value <= limit, 0.0, 1.0)


def far_products(left, right, out, x_ref):
    carried = dot3(left[2][...], x_ref[...])
    transposed = dot3(carried, right[2][...])
    out[2][...] = transposed
    out[3][...] = jnp.transpose(transposed)
    out[1][...] = dot3(dot3(carried, right[1][...]), left[3][...]) + left[1][...]
    spread = dot3(left[0][...], x_ref[...])
    out[0][...] = dot3(dot3(right[3][...], spread), right[2][...]) + right[0][...]
    return carried


def near_products(left, right, out, x_ref):
    eye = jnp.where(diagonal_mask(x_ref.shape[0]), 1.0, 0.0)
    past = low(x_ref[...] - eye)
    carried = left[2][...] + dot1(low(left[2][...]), past)
    transposed = dot3(carried, right[2][...])
    out[2][...] = transposed
    out[3][...] = jnp.transpose(transposed)
    out[1][...] = dot3(dot3(carried, right[1][...]), left[3][...]) + left[1][...]
    spread = left[0][...] + dot1(low(left[0][...]), past)
    spread = spread + dot1(low(right[3][...] - eye), low(spread))
    out[0][...] = spread + dot1(low(spread), low(right[2][...] - eye)) + right[0][...]
    return carried


def merge_chains(left, right, out, x_ref, b_ref, pair_ref, steps, fine, reach, products, before_products):
    b_ref[...] = dot1(low(right[1][...]), low(left[0][...]))
    failed = invert(b_ref, 1.0, 1.0, steps, fine, reach, 0.2, x_ref, pair_ref)
    before_products()
    carried = products(left, right, out, x_ref)
    b1, e1, b2, e2 = left[4](), left[5](), right[4](), right[5]()
    b1_column = to_column(b1)
    row = column_to_row(b1_column + row_to_column(e2, left[0][...]), x_ref[...])
    b = to_row(row_to_column(row, right[3][...])) + b2
    row = e2 - column_to_row(b1_column, right[1][...])
    e = to_row(row_to_column(row, carried)) + e1
    return b, e, failed


def open_chain(left, right, x_ref, x, lam):
    t = row_dot(lam, right[3][...]) + right[5]()
    drift = row_to_column(x, left[3][...]) + to_column(left[4]()) + row_to_column(t, left[0][...])
    middle = column_to_row(drift, x_ref[...])
    return middle, t - row_dot(middle, right[1][...])


def fast_kernel(
    devices, greenhouses, rows_in,
    states_ref, gradient_ref, mask_ref, zone_ref, map_ref, own_ref, bias_ref, wout_hbm,
    out_ref, bad_ref,
    parts, whole, wout, small, sect, slope, k_ref, kt_ref, leaf, leaf_v, chain, chain_a, chain_v, top, top_v,
    x0_ref, x1_ref, x2_ref, xr_ref, b_ref, pair_ref, side, side_v, z_ref, z_v, zo_ref, zo_v, zout, zout_v,
    pack_out, pack_in, pack_v, o_buf, o_in, result, result_in, flags, middle_v,
    w_send, w_recv, s_send, s_recv, local_sem, c_send, c_recv, p_send, p_recv, q_send, q_recv, v_send, v_recv,
    o_send, o_recv, r_send, r_recv, f_send, f_recv,
):
    width = states_ref.shape[1]
    groups = devices // 4
    me = lax.axis_index("tm")
    house = lax.axis_index("scen")
    g = lax.div(me, 4)
    r = lax.rem(me, 4)
    c = lax.rem(r, 2)
    y = lax.div(r, 2)
    core = me + 1 - 2 * c
    across = me + 2 - 4 * y
    diagonal = across + 1 - 2 * c
    is_left = g < groups // 2
    depth = jnp.where(is_left, g, groups - 1 - g)
    inward = me + jnp.where(is_left, 4, -4)
    outward = me - jnp.where(is_left, 4, -4)
    is_root = depth == groups // 2 - 1
    is_end = depth == 0
    left_root = jnp.logical_and(is_root, is_left)
    right_root = jnp.logical_and(is_root, jnp.logical_not(is_left))
    right_end = jnp.logical_and(is_end, jnp.logical_not(is_left))
    left_end = jnp.logical_and(is_end, is_left)
    solves = jnp.logical_not(right_end)
    writes = y == c

    def remote(src, dst, send, recv, target):
        return pltpu.make_async_remote_copy(
            src_ref=src, dst_ref=dst, send_sem=send, recv_sem=recv, device_id=target, device_id_type=MESH
        )

    cleanup = []

    wout_copy = pltpu.make_async_copy(wout_hbm, wout, local_sem)
    wout_copy.start()

    barrier = pltpu.get_barrier_semaphore()

    def greet(target):
        pl.semaphore_signal(barrier, inc=1, device_id=target, device_id_type=MESH)

    for target in (core, across, diagonal):
        greet({"tm": target})
    for k in range(1, greenhouses):
        greet({"scen": lax.rem(house + k, greenhouses)})

    for k in range(1, groups):
        greet({"tm": 4 * lax.rem(g + k, groups) + r})

    weights = jnp.zeros(gradient_ref.shape, F32)
    for zone in range(zone_ref.shape[1]):
        weights = jnp.where(map_ref[...][None] == zone, zone_ref[:, zone : zone + 1], weights)
    weights = weights * (1.0 + 4.0 * mask_ref[...].astype(F32))
    small[r] = jnp.zeros((8, width), F32)
    small[r, 0:2] = states_ref[...].astype(F32)
    small[r, 2:4] = gradient_ref[...]
    small[r, 4:6] = weights
    mine = own_ref[...].astype(F32)
    chunks, _, span = parts.shape[2:]
    pieces = mine.shape[1] // span
    folded = low(jnp.concatenate([mine[:, k * span : (k + 1) * span] for k in range(pieces)], axis=0))
    for j in range(chunks):
        parts[g, r, j] = folded[16 * j : 16 * j + 16]
    sect[...] = jnp.zeros_like(sect)

    pl.semaphore_wait(barrier, 3 + greenhouses - 1 + groups - 1)

    shared = greenhouses == 2 and chunks == 3
    some = pl.ds(house, 2) if shared else pl.ds(0, chunks)
    alone = 2 * house
    missing = 2 - 2 * house
    other = lax.rem(r + 2, 4)

    def line_copy(k, way, sender):
        block = parts.at[sender, r, some]
        return remote(block, block, w_send.at[way, k], w_recv.at[0, sender], {"tm": me + 4 * k * (1 - 2 * way)})

    def across_copy(sender, row):
        block = parts.at[sender, row, some]
        return remote(block, block, w_send.at[2, sender], w_recv.at[1, sender], {"tm": across})

    def hand_copy(sender, row, which_row, chunk):
        block = parts.at[sender, row, chunk]
        return remote(block, block, w_send.at[3 + which_row, sender], w_recv.at[2 + which_row, sender], {"scen": 1 - house})

    def core_copy(row, k, chunk):
        block = parts.at[:, row, chunk]
        return remote(block, block, w_send.at[5, k], w_recv.at[4, k], {"tm": core})

    small_copies = [
        remote(small.at[r], small.at[r], s_send.at[k], s_recv.at[r], {"tm": target})
        for k, target in enumerate((core, across, diagonal))
    ]

    def begin(copy):
        copy.start()

    def end(copy):
        copy.wait_send()

    def by_distance(visit, least=1):
        for k in range(least, groups):
            if k == 0:
                visit(0, g)
                continue

            @pl.when(g >= k)
            def _():
                visit(k, g - k)

            @pl.when(g + k <= groups - 1)
            def _():
                visit(k, g + k)

    def line(act):
        act(across_copy(g, r))
        for k in range(1, groups):
            for way in range(2):
                @pl.when(g + k <= groups - 1 if way == 0 else g >= k)
                def _():
                    act(line_copy(k, way, g))
        if act is begin:
            for copy in small_copies:
                copy.start()

        def from_line(k, sender):
            if act is begin:
                line_copy(k, 0, sender).wait_recv()
            act(across_copy(sender, r))
            if shared:
                act(hand_copy(sender, r, 0, alone))

        by_distance(from_line)
        act(core_copy(r, 0, some))

        def from_across(k, sender):
            if act is begin:
                across_copy(sender, other).wait_recv()
            if shared:
                act(hand_copy(sender, other, 1, alone))

        by_distance(from_across, 0)
        act(core_copy(other, 1, some))
        if shared:
            if act is begin:
                by_distance(lambda k, sender: hand_copy(sender, r, 0, missing).wait_recv())
            act(core_copy(r, 2, missing))
            if act is begin:
                by_distance(lambda k, sender: hand_copy(sender, other, 1, missing).wait_recv(), 0)
            act(core_copy(other, 3, missing))

    line(begin)
    cleanup.append(lambda: line(end))
    cleanup.append(lambda: [copy.wait_send() for copy in small_copies] and None)
    beside = lax.rem(core, 4)
    beyond = lax.rem(diagonal, 4)
    core_copy(beside, 0, some).wait_recv()
    core_copy(beyond, 1, some).wait_recv()
    if shared:
        core_copy(beside, 2, missing).wait_recv()
        core_copy(beyond, 3, missing).wait_recv()
    for target in (core, across, diagonal):
        remote(small.at[r], small.at[lax.rem(target, 4)], s_send.at[0], s_recv.at[lax.rem(target, 4)], {"tm": core}).wait_recv()

    batch = next(q for q in range(1, 17) if q * rows_in % 16 == 0)
    for first in range(0, devices, batch):
        blocks = [
            jnp.concatenate([parts[(first + k) // 4, (first + k) % 4, j].astype(F32) for j in range(chunks)], axis=0) for k in range(batch)
        ]
        for j in range(pieces):
            tall = jnp.concatenate([block[j * rows_in : (j + 1) * rows_in] for block in blocks], axis=0)
            whole[first * rows_in : (first + batch) * rows_in, j * span : (j + 1) * span] = low(tall)

    for k in range(3):
        sect[k, 0:2] = small[2 * c, 2 * k : 2 * k + 2]
        sect[k, 2:4] = small[2 * c + 1, 2 * k : 2 * k + 2]
    hidden = dot1(low(sect[0]), whole[...]) + bias_ref[...][None]
    bent = jnp.tanh(hidden)
    slope[...] = low(1.0 - bent * bent).astype(F32)
    wout_copy.wait()

    def section(t, carry):
        weighted = whole[...] * low(slope[pl.ds(t, 1), :])
        product = dot1(weighted, wout[...])
        k_ref[t] = product
        kt_ref[t] = jnp.transpose(product)
        return carry

    lax.fori_loop(0, 4, section, 0)

    eye = diagonal_mask(width)

    def on_diagonal(row):
        return jnp.where(eye, row, 0.0)

    def column(row):
        return jnp.sum(on_diagonal(row), axis=1, keepdims=True)

    def pair(q, carry):
        w0, w1 = sect[2, pl.ds(2 * q, 1)], sect[2, pl.ds(2 * q + 1, 1)]
        g0, g1 = sect[1, pl.ds(2 * q, 1)], sect[1, pl.ds(2 * q + 1, 1)]
        d = 1.0 / (1.0 + w1)
        dw = w1 * d
        k0, k1, k0t, k1t = k_ref[2 * q], k_ref[2 * q + 1], kt_ref[2 * q], kt_ref[2 * q + 1]
        scaled = column(d) * k1
        transposed = on_diagonal(d) + k0 * d + scaled + dot1(low(k0 * d), low(k1))
        leaf[q, 2] = transposed
        leaf[q, 3] = jnp.transpose(transposed)
        leaf[q, 0] = on_diagonal(1.0 + d) + scaled + k1t * d + dot1(low(k1t * d), low(k1))
        light = k0 * dw
        leaf[q, 1] = on_diagonal(w0 + dw) + light + column(dw) * k0t + dot1(low(light), low(k0t))
        rhs = d * g1
        rhs_column = to_column(rhs)
        leaf_v[q, 0:1] = rhs + column_to_row(rhs_column, k1)
        leaf_v[q, 1:2] = rhs + column_to_row(rhs_column, k0t) + g0
        return carry

    lax.fori_loop(0, 2, pair, 0)

    def chain_of(quad, fourth, vector):
        return [quad.at[0], quad.at[1], quad.at[2], fourth, lambda: vector[0:1], lambda: vector[1:2]]

    lower, upper = (chain_of(leaf.at[q], leaf.at[q, 3], leaf_v.at[q]) for q in range(2))
    mine = chain_of(chain.at[c], chain_a.at[c], chain_v.at[c])
    b, e, failed = merge_chains(lower, upper, mine, x0_ref, b_ref, pair_ref, 2, 0, 1e-3, near_products, lambda: None)
    chain_v[c] = jnp.zeros((8, width), F32)
    chain_v[c, 0:1] = b
    chain_v[c, 1:2] = e
    chain_v[c, 2:3] = jnp.broadcast_to(failed, (1, width))

    def chain_copy(slot, k):
        return remote(chain.at[slot, k], chain.at[slot, k], c_send.at[k], c_recv.at[k], {"tm": core})

    def vector_copy(slot):
        return remote(chain_v.at[slot], chain_v.at[slot], c_send.at[3], c_recv.at[3], {"tm": core})

    chain_copy(c, c).start()
    chain_copy(c, 1 - c).start()
    chain_copy(c, 2).start()
    vector_copy(c).start()
    cleanup.append(lambda: [chain_copy(c, k).wait_send() for k in range(3)] and None)
    cleanup.append(lambda: vector_copy(c).wait_send())
    chain_copy(1 - c, 1 - c).wait_recv()

    def rest_arrived():
        chain_copy(1 - c, c).wait_recv()
        chain_copy(1 - c, 2).wait_recv()
        vector_copy(1 - c).wait_recv()
        chain_a[1 - c] = jnp.transpose(chain[1 - c, 2])

    first, second = (chain_of(chain.at[q], chain_a.at[q], chain_v.at[q]) for q in range(2))
    b, e, failed = merge_chains(first, second, chain_of(top, top.at[3], top_v), x1_ref, b_ref, pair_ref, 3, 1, 0.02, far_products, rest_arrived)
    bad = jnp.maximum(jnp.maximum(chain_v[0, 2:3], chain_v[1, 2:3]), failed)

    sign = jnp.where(is_left, 1.0, -1.0)
    for k, (a_index, b_index) in enumerate(((3, 2), (2, 3), (1, 0), (0, 1))):
        side[k] = jnp.where(is_left, top[a_index], top[b_index])
    side_v[0:1] = jnp.where(is_left, e, -b)
    side_v[1:2] = jnp.where(is_left, b, e)
    side_v[2:3] = bad

    blocks = width // 128
    tiles = [(i, j) for i in range(blocks) for j in range(i + 1)]
    half = len(tiles) // 2

    def tile_copy(which, k):
        return remote(pack_out.at[k], pack_in.at[which, k], p_send.at[k], p_recv.at[which, k], {"tm": inward})

    def tile_pass(which, k):
        return remote(pack_in.at[which, k], pack_in.at[which, k], q_send.at[which, k], q_recv.at[which, k], {"tm": core})

    def row_copy(which):
        return remote(zout_v, pack_v.at[which], v_send, v_recv.at[which], {"tm": inward})

    def receive(which, m_ref, row_ref):
        for j in range(half):
            tile_copy(which, 2 * j + c).wait_recv()
            tile_pass(which, 2 * j + c).start()
        for j in range(half):
            tile_pass(which, 2 * j + 1 - c).wait_recv()
        row_copy(which).wait_recv()
        for k, (i, j) in enumerate(tiles):
            tile = pack_in[which, k]
            m_ref[128 * i : 128 * i + 128, 128 * j : 128 * j + 128] = tile
            if i != j:
                m_ref[128 * j : 128 * j + 128, 128 * i : 128 * i + 128] = jnp.transpose(tile)
        row_ref[...] = pack_v[which]

    @pl.when(is_end)
    def _():
        z_ref[...] = jnp.where(eye, 1.0, 0.0)
        z_v[...] = jnp.zeros_like(z_v)
        b_ref[...] = side[2]

    @pl.when(jnp.logical_not(is_end))
    def _():
        receive(0, z_ref, z_v)
        b_ref[...] = dot3(side[2], z_ref[...])

    @pl.when(solves)
    def _():
        delta = jnp.where(left_end, 0.0, 1.0)
        floor = jnp.min(small[0, 4:5], axis=1, keepdims=True)
        least = jnp.where(left_end, floor, 1.0)
        failed = invert(b_ref, delta, least, jnp.where(left_end, 6, 5), 1, 0.2, 1.5, x2_ref, pair_ref)

        @pl.when(left_end)
        def _():
            zo_ref[...] = x2_ref[...]

        @pl.when(jnp.logical_not(left_end))
        def _():
            zo_ref[...] = dot3(z_ref[...], x2_ref[...])

        zout[...] = dot3(dot3(side[0], zo_ref[...]), side[1]) + side[3]
        v = side_v[0:1]
        row = column_to_row(to_column(z_v[0:1]) + row_to_column(v, z_ref[...]), x2_ref[...])
        zout_v[...] = jnp.zeros_like(zout_v)
        zout_v[0:1] = to_row(row_to_column(row, side[0])) + side_v[1:2]
        zout_v[2:3] = jnp.maximum(jnp.maximum(side_v[2:3], z_v[2:3]), failed)

    @pl.when(right_end)
    def _():
        zout[...] = side[3]
        zout_v[...] = jnp.zeros_like(zout_v)
        zout_v[0:1] = side_v[1:2]
        zout_v[2:3] = side_v[2:3]

    which = is_root.astype(jnp.int32)

    @pl.when(jnp.logical_not(left_root))
    def _():
        for k, (i, j) in enumerate(tiles):
            pack_out[k] = zout[128 * i : 128 * i + 128, 128 * j : 128 * j + 128]
        for j in range(half):
            tile_copy(which, 2 * j + c).start()
        row_copy(which).start()

    def tiles_sent():
        @pl.when(jnp.logical_not(left_root))
        def _():
            for j in range(half):
                tile_copy(which, 2 * j + c).wait_send()
            row_copy(which).wait_send()

        @pl.when(jnp.logical_not(is_end))
        def _():
            for j in range(half):
                tile_pass(0, 2 * j + c).wait_send()

    cleanup.append(tiles_sent)
    def outer_copy():
        return remote(o_buf, o_in, o_send, o_recv, {"tm": outward})

    def middle_copy():
        return remote(middle_v, o_in, f_send.at[0], f_recv.at[0], {"tm": inward})

    flag_copies = []
    for k in range(1, greenhouses):
        flag_copies.append(
            remote(flags.at[0], flags.at[k], f_send.at[k], f_recv.at[k], {"scen": lax.rem(house + k, greenhouses)})
        )
    last = greenhouses

    def flag_out(k, target):
        return remote(flags.at[last], flags.at[last], f_send.at[greenhouses + k], f_recv.at[greenhouses], {"tm": target})

    @pl.when(left_root)
    def _():
        receive(1, zo_ref, zo_v)
        b_ref[...] = dot3(zo_ref[...], zout[...])
        invert(b_ref, 1.0, 1.0, 5, 0, 0.3, 1.0, xr_ref, pair_ref)
        rhs = to_column(zout_v[0:1]) + row_to_column(zo_v[0:1], zout[...])
        value = column_to_row(rhs, xr_ref[...])
        for _ in range(3):
            column_now = to_column(value)
            left_over = rhs - column_now - row_to_column(column_to_row(column_now, zo_ref[...]), zout[...])
            value = value + column_to_row(left_over, xr_ref[...])
        failed = bad_if(total(left_over * left_over), 1e-4 * total(rhs * rhs))
        middle_v[...] = jnp.broadcast_to(value, middle_v.shape)
        middle_copy().start()
        o_in[0:1] = zo_v[0:1] - row_dot(value, zo_ref[...])
        flags[0] = jnp.broadcast_to(
            jnp.maximum(jnp.maximum(zout_v[2:3, :128], zo_v[2:3, :128]), failed), (8, 128)
        )
        for copy in flag_copies:
            copy.start()

    @pl.when(right_root)
    def _():
        middle_copy().wait_recv()

    @pl.when(jnp.logical_not(is_root))
    def _():
        outer_copy().wait_recv()

    outer = o_in[0:1]
    side_v[3:4] = jnp.zeros((1, width), F32)

    @pl.when(solves)
    def _():
        w = sign * side_v[0:1] + row_dot(outer, side[0])
        value = column_to_row(to_column(z_v[0:1]) + sign * row_to_column(w, z_ref[...]), x2_ref[...])
        side_v[3:4] = value
        o_buf[...] = jnp.broadcast_to(w - sign * row_dot(value, side[2]), o_buf.shape)

    @pl.when(jnp.logical_not(is_end))
    def _():
        outer_copy().start()

    own_value = side_v[3:4]
    start = jnp.where(is_left, own_value, outer)
    finish_lam = jnp.where(is_left, outer, own_value)

    def result_copy(slot):
        return remote(result.at[slot], result_in, r_send, r_recv, {"tm": core})

    @pl.when(writes)
    def _():
        middle, lam = open_chain(first, second, x1_ref, start, finish_lam)
        x_a = jnp.where(c == 0, start, middle)
        lam_b = jnp.where(c == 0, lam, finish_lam)
        middle, lam = open_chain(lower, upper, x0_ref, x_a, lam_b)
        for q, x, lam_q in ((0, x_a, lam), (1, middle, lam_b)):
            w1, g1 = sect[2, 2 * q + 1 : 2 * q + 2], sect[1, 2 * q + 1 : 2 * q + 2]
            result[q, 0:1] = x
            result[q, 1:2] = (
                x + row_dot(x, k_ref[2 * q]) + lam_q + row_dot(lam_q, kt_ref[2 * q + 1]) + g1
            ) / (1.0 + w1)
        result_copy(1 - c).start()
        out_ref[...] = result[c, 0:2]

    @pl.when(jnp.logical_not(writes))
    def _():
        result_copy(0).wait_recv()
        out_ref[...] = result_in[0:2]

    @pl.when(left_root)
    def _():
        for copy in flag_copies:
            copy.wait_recv()
        worst = flags[0]
        for k in range(1, greenhouses):
            worst = jnp.maximum(worst, flags[k])
        flags[last] = worst
        flag_out(1, inward).start()

    @pl.when(jnp.logical_not(left_root))
    def _():
        flag_out(0, outward).wait_recv()

    @pl.when(jnp.logical_not(is_end))
    def _():
        flag_out(0, outward).start()

    bad_ref[...] = flags[last, 0:1, 0:1]

    def rest_sent():
        @pl.when(jnp.logical_not(is_end))
        def _():
            outer_copy().wait_send()
            flag_out(0, outward).wait_send()

        @pl.when(left_root)
        def _():
            for j in range(half):
                tile_pass(1, 2 * j + c).wait_send()
            middle_copy().wait_send()
            flag_out(1, inward).wait_send()
            for copy in flag_copies:
                copy.wait_send()

        @pl.when(writes)
        def _():
            result_copy(1 - c).wait_send()

    cleanup.append(rest_sent)
    for act in cleanup:
        act()

def fast_device(states, gradient, active_mask, zone_weight, zone_map, w_in, w_out, bias):
    width = states.shape[1]
    hidden = w_in.shape[1]
    devices = lax.axis_size("tm")
    greenhouses = lax.axis_size("scen")
    rows = w_in.shape[0]
    pieces = 16 // math.gcd(rows, 16)
    span = hidden // pieces
    chunks = pieces * rows // 16
    tiles = (width // 128) * (width // 128 + 1) // 2
    square = lambda *lead: pltpu.VMEM(lead + (width, width), F32)
    lines = lambda *lead: pltpu.VMEM(lead + (8, width), F32)
    dma = pltpu.SemaphoreType.DMA
    vmem = pl.BlockSpec(memory_space=pltpu.VMEM)
    scratch = [
        pltpu.VMEM((devices // 4, 4, chunks, 16, span), BF16), pltpu.VMEM((rows * devices, hidden), BF16), pltpu.VMEM(w_out.shape, BF16),
        lines(4), lines(3), pltpu.VMEM((8, hidden), F32), square(4), square(4), square(2, 4), lines(2),
        square(2, 3), square(2), lines(2), square(4), lines(),
        square(), square(), square(), square(), square(), pltpu.VMEM((2 * width, width), BF16), square(4), lines(),
        square(), lines(), square(), lines(), square(), lines(),
        pltpu.VMEM((tiles, 128, 128), F32), pltpu.VMEM((2, tiles, 128, 128), F32), lines(2), lines(), lines(), lines(2), lines(),
        pltpu.VMEM((1 + greenhouses, 8, 128), F32), lines(),
        dma((6, max(4, devices // 4))), dma((5, max(4, devices // 4))), dma((3,)), dma((4,)), dma, dma((4,)), dma((4,)), dma((tiles,)), dma((2, tiles)),
        dma((2, tiles)), dma((2, tiles)), dma, dma((2,)), dma, dma, dma, dma,
        dma((greenhouses + 2,)), dma((greenhouses + 1,)),
    ]
    return pl.pallas_call(
        functools.partial(fast_kernel, devices, greenhouses, rows),
        out_shape=(jax.ShapeDtypeStruct((2, width), F32), jax.ShapeDtypeStruct((1, 1), F32)),
        in_specs=[vmem] * 7 + [pl.BlockSpec(memory_space=pl.ANY)],
        out_specs=(vmem, vmem),
        scratch_shapes=scratch,
        compiler_params=pltpu.CompilerParams(collective_id=0, has_side_effects=True, vmem_limit_bytes=58 << 20),
        name="gauss_newton",
    )(states, gradient, active_mask, zone_weight, zone_map, w_in, bias, w_out)


def per_device(*arrays):
    value, bad = fast_device(*arrays)
    return lax.cond(bad[0, 0] > 0.0, lambda: direct_device(*arrays), lambda: value)


def solution(mesh):
    return jax.shard_map(
        per_device,
        mesh=mesh,
        in_specs=(
            P(("scen", "tm"), None),
            P(("scen", "tm"), None),
            P(("scen", "tm"), None),
            P(("scen", "tm"), None),
            P("scen"),
            P("tm", None),
            P(),
            P(),
        ),
        out_specs=P(("scen", "tm"), None),
        check_vma=False,
    )
```

```python
import functools
import math

import jax
import jax.numpy as jnp
from jax import lax
from jax.experimental import pallas as pl
from jax.experimental.pallas import tpu as pltpu
from jax.sharding import PartitionSpec as P


def from_partner(array, axis, bit):
    return lax.ppermute(array, axis, [(i, i ^ 1 << bit) for i in range(lax.axis_size(axis))])


def matmul(left, right):
    return jnp.dot(left, right, precision=lax.Precision.HIGHEST)


def dot_exact(left, right, dims=((1,), (0,))):
    return lax.dot_general(
        left, right, (dims, ((), ())), precision=lax.Precision.HIGHEST, preferred_element_type=jnp.float32
    )


def dot_fast(left, right):
    return jnp.dot(
        left.astype(jnp.bfloat16), right.astype(jnp.bfloat16), preferred_element_type=jnp.float32
    )


def invert_in_place(m_ref, x_ref, e_ref):
    width = m_ref.shape[0]
    row_ids = lax.broadcasted_iota(jnp.int32, (width, width), 0)
    col_ids = lax.broadcasted_iota(jnp.int32, (width, width), 1)
    diagonal = row_ids == col_ids
    matrix = m_ref[...]
    square = dot_fast(matrix, matrix)
    trace = jnp.sum(jnp.where(diagonal, matrix, 0.0))
    frobenius = jnp.sum(matrix * matrix)
    bound = jnp.max(jnp.sum(jnp.abs(square), axis=1))
    scale = jnp.minimum(trace / frobenius, 1.9 * lax.rsqrt(bound))
    x_ref[...] = jnp.where(diagonal, 2.0 * scale, 0.0) - (scale * scale) * matrix
    first = jnp.where(diagonal, 1.0, 0.0) - (2.0 * scale) * matrix + (scale * scale) * square
    e_ref[...] = first

    def coarse_step(carry):
        count, _ = carry
        x_ref[...] = x_ref[...] + dot_fast(x_ref[...], e_ref[...])
        residual = jnp.where(diagonal, 1.0, 0.0) - dot_fast(m_ref[...], x_ref[...])
        e_ref[...] = residual
        return count + 1, jnp.sum(residual * residual)

    lax.while_loop(lambda c: (c[0] < 10) & (c[1] > 0.25), coarse_step, (0, jnp.sum(first * first)))

    def fine_step(carry):
        count, _ = carry
        residual = jnp.where(diagonal, 1.0, 0.0) - dot_exact(m_ref[...], x_ref[...])
        x_ref[...] = x_ref[...] + dot_fast(x_ref[...], residual)
        return count + 1, jnp.sum(residual * residual)

    _, last = lax.while_loop(
        lambda c: (c[0] < 12) & jnp.logical_not(c[1] <= 1e-7), fine_step, (0, jnp.float32(1.0))
    )

    @pl.when(jnp.logical_not(last <= 1e-7))
    def _():
        x_ref[...] = m_ref[...]

        def pivot_step(k, carry):
            current = x_ref[...]
            row = x_ref[pl.ds(k, 1), :]
            column = jnp.sum(jnp.where(col_ids == k, current, 0.0), axis=1, keepdims=True)
            pivot = jnp.sum(jnp.where(col_ids[:1] == k, row, 0.0), axis=1, keepdims=True)
            scaled = row / pivot
            updated = jnp.where(col_ids == k, -column / pivot, current - column * scaled)
            own_row = jnp.where(col_ids == k, 1.0 / pivot, scaled)
            x_ref[...] = jnp.where(row_ids == k, own_row, updated)
            return carry

        lax.fori_loop(0, width, pivot_step, 0)


def unpack_first(packed, row_ids, col_ids):
    return jnp.where(row_ids <= col_ids, packed, jnp.transpose(packed))


def unpack_last(packed, diagonal, row_ids, col_ids):
    whole = jnp.where(row_ids > col_ids, packed, jnp.transpose(packed))
    return jnp.where(row_ids == col_ids, diagonal, whole)


def finish(left, right, rhs, ff, ll, fr, lr, x_ref, block_ref, vector_ref, gl_ref, gr_ref, gs_ref):
    width = x_ref.shape[0]
    inverse = x_ref[...]
    gl_ref[...] = dot_exact(left, inverse)
    gr_ref[...] = dot_exact(inverse, right)
    solved = dot_exact(jnp.broadcast_to(rhs, (8, width)), inverse)
    gs_ref[...] = solved[:1]
    row_ids = lax.broadcasted_iota(jnp.int32, (width, width), 0)
    col_ids = lax.broadcasted_iota(jnp.int32, (width, width), 1)
    new_ff = ff() - dot_exact(gl_ref[...], left, ((1,), (1,)))
    block_ref[width : 2 * width] = -dot_exact(gl_ref[...], right)
    new_ll = ll() - dot_exact(jnp.transpose(right), gr_ref[...])
    block_ref[:width] = jnp.where(row_ids <= col_ids, new_ff, new_ll)
    vector_ref[2:3] = jnp.sum(jnp.where(row_ids == col_ids, new_ll, 0.0), axis=0, keepdims=True)
    vector_ref[0:1] = fr - dot_exact(solved, left, ((1,), (1,)))[:1]
    vector_ref[1:2] = lr - dot_exact(solved, right)[:1]


def first_kernel(
    m_ref, mr_ref, l_ref, r_ref, ff_ref, ll_ref, fr_ref, lr_ref,
    block_ref, vector_ref, gl_ref, gr_ref, gs_ref, x_ref, e_ref
):
    invert_in_place(m_ref, x_ref, e_ref)
    finish(
        l_ref[...], r_ref[...], mr_ref[...], lambda: ff_ref[...], lambda: ll_ref[...],
        fr_ref[...], lr_ref[...], x_ref, block_ref, vector_ref, gl_ref, gr_ref, gs_ref
    )


def merge_kernel(
    flag_ref, own_ref, other_ref, ov_ref, pv_ref,
    block_ref, vector_ref, gl_ref, gr_ref, gs_ref, x_ref, e_ref, m_ref
):
    width = x_ref.shape[0]
    is_upper = flag_ref[0] == 1
    spans = [pl.ds(k * width, width) for k in range(2)]
    row_ids = lax.broadcasted_iota(jnp.int32, (width, width), 0)
    col_ids = lax.broadcasted_iota(jnp.int32, (width, width), 1)
    lower_rhs = jnp.where(is_upper, pv_ref[...], ov_ref[...])
    upper_rhs = jnp.where(is_upper, ov_ref[...], pv_ref[...])

    def lower(k):
        return jnp.where(is_upper, other_ref[spans[k], :], own_ref[spans[k], :])

    def upper(k):
        return jnp.where(is_upper, own_ref[spans[k], :], other_ref[spans[k], :])

    m_ref[...] = unpack_last(lower(0), lower_rhs[2:3], row_ids, col_ids) + unpack_first(
        upper(0), row_ids, col_ids
    )
    invert_in_place(m_ref, x_ref, e_ref)
    finish(
        lower(1), upper(1), lower_rhs[1:2] + upper_rhs[0:1], lambda: unpack_first(lower(0), row_ids, col_ids),
        lambda: unpack_last(upper(0), upper_rhs[2:3], row_ids, col_ids),
        lower_rhs[0:1], upper_rhs[1:2], x_ref, block_ref, vector_ref, gl_ref, gr_ref, gs_ref
    )


def call_merge(kernel, name, width, parts, scratch, in_specs=None):
    full = jax.ShapeDtypeStruct((width, width), jnp.float32)
    result = pl.pallas_call(
        kernel,
        out_shape=(
            jax.ShapeDtypeStruct((2 * width, width), jnp.float32),
            jax.ShapeDtypeStruct((3, width), jnp.float32),
            full, full, jax.ShapeDtypeStruct((1, width), jnp.float32),
        ),
        in_specs=in_specs or [pl.BlockSpec(memory_space=pltpu.VMEM)] * len(parts),
        scratch_shapes=[pltpu.VMEM((width, width), jnp.float32)] * scratch,
        compiler_params=pltpu.CompilerParams(vmem_limit_bytes=48 << 20),
        name=name,
    )(*parts)
    return result[:2], result[2:]


def eliminate(*parts):
    return call_merge(
        first_kernel, "eliminate", parts[0].shape[0],
        [part if part.ndim == 2 else part[None] for part in parts], 2
    )


def merge(upper_flag, own, other):
    vmem = pl.BlockSpec(memory_space=pltpu.VMEM)
    return call_merge(
        merge_kernel, "merge", own[0].shape[1],
        [upper_flag.astype(jnp.int32)[None], own[0], other[0], own[1], other[1]], 3,
        [pl.BlockSpec(memory_space=pltpu.SMEM)] + [vmem] * 4
    )


def exchange(block, vector, core, level):
    if level == 0:
        return from_partner((block, vector), "tm", level)
    half = block.shape[0] // 2
    share = lax.dynamic_slice_in_dim(block, core * half, half, axis=0)
    received, other_vector = from_partner((share, vector), "tm", level)
    swapped = from_partner(received, "tm", 0)
    other = jnp.where(
        core == 1,
        jnp.concatenate([swapped, received]),
        jnp.concatenate([received, swapped]),
    )
    return other, other_vector


def gather_rows(rows, level_count):
    place = lax.axis_index("tm")
    held = rows[None]
    for level in reversed(range(level_count)):
        other = from_partner(held, "tm", level)
        upper_flag = jnp.bitwise_and(jnp.right_shift(place, level), 1) == 1
        held = jnp.stack([jnp.where(upper_flag, other, held), jnp.where(upper_flag, held, other)])
        held = held.reshape((-1,) + rows.shape)
    bits = held.reshape((2,) * level_count + rows.shape)
    order = tuple(reversed(range(level_count))) + (level_count, level_count + 1)
    return bits.transpose(order).reshape(-1, rows.shape[1])


def root_kernel(m_ref, mr_ref, o_ref, x_ref, e_ref):
    invert_in_place(m_ref, x_ref, e_ref)
    o_ref[...] = dot_exact(jnp.broadcast_to(mr_ref[...], (8, m_ref.shape[0])), x_ref[...])[:1]


def root_solve(matrix, rhs):
    width = matrix.shape[0]
    return pl.pallas_call(
        root_kernel,
        out_shape=jax.ShapeDtypeStruct((1, width), jnp.float32),
        scratch_shapes=[pltpu.VMEM((width, width), jnp.float32)] * 2,
        compiler_params=pltpu.CompilerParams(vmem_limit_bytes=48 << 20),
        name="root",
    )(matrix, rhs)


def direct_device(states, gradient, active_mask, zone_weight, zone_map, w_in, w_out, bias):
    width = states.shape[1]
    devices = lax.axis_size("tm")
    place = lax.axis_index("tm")
    is_first = place == 0
    is_last = place == devices - 1
    zone_count = zone_weight.shape[1]
    zone_table = (
        zone_map[None, :] == lax.broadcasted_iota(jnp.int32, (zone_count, width), 0)
    ).astype(jnp.float32)
    weights = jnp.dot(zone_weight, zone_table, precision=lax.Precision.HIGHEST) * (
        1.0 + 4.0 * active_mask.astype(jnp.float32)
    )
    later = jnp.stack([states[1].astype(jnp.float32), gradient[1], weights[1]])
    before = lax.ppermute(later, "tm", [(i, i + 1) for i in range(devices - 1)])
    whole_rows = gather_rows(w_in, devices.bit_length() - 1)
    rows = jnp.stack([before[0].astype(jnp.bfloat16), states[0]])
    hidden_in = jnp.dot(rows, whole_rows, preferred_element_type=jnp.float32) + bias
    slopes = (1.0 - jnp.tanh(hidden_in) ** 2).astype(jnp.bfloat16)
    weighted = slopes[:, None, :] * whole_rows[None, :, :]
    flat = weighted.reshape(2 * width, whole_rows.shape[1])
    product = jnp.dot(flat, w_out, preferred_element_type=jnp.float32).reshape(2, width, width)
    eye = jnp.eye(width, dtype=jnp.float32)
    jac_before = product[0] + eye
    jac_own = product[1] + eye
    last_diag = 1.0 / (1.0 + weights[1])
    column_scale = jnp.where(is_last, weights[1] * last_diag, 1.0)
    tail = jnp.where(is_last, gradient[1] * last_diag, 0.0)
    middle = (
        jnp.diag(weights[0] + jnp.where(is_first, 0.0, 1.0))
        + matmul(jac_own * column_scale[None, :], jac_own.T)
    )
    middle_rhs = gradient[0] + matmul(jac_own, tail)
    left = jnp.where(is_first, 0.0, -jac_before)
    right = jnp.where(is_last, 0.0, -jac_own)
    first_first = jnp.diag(before[2]) + matmul(left, left.T)
    own, local_store = eliminate(
        middle, middle_rhs, left, right, first_first, eye, before[1], jnp.zeros_like(middle_rhs)
    )
    core = jnp.bitwise_and(place, 1)
    level_count = devices.bit_length() - 1
    level_stores = []
    for level in range(level_count):
        upper_flag = jnp.bitwise_and(jnp.right_shift(place, level), 1) == 1
        if level == level_count - 1:
            row_ids = lax.broadcasted_iota(jnp.int32, (width, width), 0)
            packed, flipped = own[0][:width], own[0][:width].T
            keep = jnp.where(upper_flag, row_ids <= row_ids.T, row_ids > row_ids.T)
            block = jnp.where(keep, packed, flipped)
            block = jnp.where((row_ids == row_ids.T) & ~upper_flag, own[1][2:3], block)
            vector = jnp.where(upper_flag, own[1][:1], own[1][1:2])
            other_block, other_vector = exchange(block, vector, core, level)
            root = root_solve(block + other_block, vector + other_vector)[0]
            break
        own, store = merge(upper_flag, own, exchange(own[0], own[1], core, level))
        level_stores.append((store, upper_flag))
    top_flag = jnp.right_shift(place, level_count - 1) == 1
    start = jnp.where(top_flag, root, 0.0)
    end = jnp.where(top_flag, 0.0, root)
    for store, upper_flag in reversed(level_stores):
        value = back_solve(store, start, end)
        start = jnp.where(upper_flag, value, start)
        end = jnp.where(upper_flag, end, value)
    value = back_solve(local_store, start, end)
    end = jnp.where(is_last, tail + last_diag * matmul(value, jac_own), end)
    return jnp.stack([value, end], axis=0)


def back_solve(store, outer_first, outer_last):
    left_solved, right_solved, rhs_solved = store
    return rhs_solved[0] - matmul(outer_first, left_solved) - matmul(right_solved, outer_last)


MESH = pl.DeviceIdType.MESH
F32 = jnp.float32
BF16 = jnp.bfloat16


def low(x):
    return x.astype(BF16)


def dot1(a, b):
    return jnp.dot(a, b, preferred_element_type=F32)


def split(x):
    high = low(x)
    return high, low(x - high.astype(F32))


def dot3(a, b):
    ah, al = split(a)
    bh, bl = split(b)
    return dot1(jnp.concatenate([ah, ah, al], axis=1), jnp.concatenate([bh, bl, bh], axis=0))


def row_to_column(row, m):
    return jnp.sum(m * row, axis=1, keepdims=True)


def column_to_row(column, m):
    return jnp.sum(m * column, axis=0, keepdims=True)


def to_column(row):
    return row_to_column(row, jnp.where(diagonal_mask(row.shape[1]), 1.0, 0.0))


def to_row(column):
    return column_to_row(column, jnp.where(diagonal_mask(column.shape[0]), 1.0, 0.0))


def row_dot(row, m):
    return column_to_row(to_column(row), m)


def total(x):
    return jnp.sum(jnp.sum(x, axis=1, keepdims=True), axis=0, keepdims=True)


def diagonal_mask(width):
    return lax.broadcasted_iota(jnp.int32, (width, width), 0) == lax.broadcasted_iota(
        jnp.int32, (width, width), 1
    )


def invert(b_ref, delta, least, steps, fine, reach, limit, x_ref, pair_ref):
    width = b_ref.shape[0]
    eye = diagonal_mask(width)

    def on_diagonal(value):
        return jnp.where(eye, value, 0.0)

    whole = b_ref[...]
    coarse = low(whole)
    square = dot1(coarse, coarse)
    most = delta + jnp.sqrt(jnp.sqrt(total(square * square)))
    alpha = 2.0 / (least + most)
    error = (most - least) / (most + least)
    rest = 1.0 - alpha * delta
    factor = 2.0 / (2.0 - error * error)
    x = factor * alpha * (on_diagonal(1.0 + rest) - alpha * whole)
    e = on_diagonal(1.0 - factor + factor * rest * rest) + factor * (
        alpha * alpha * square - 2.0 * alpha * rest * whole
    )
    x_ref[...] = x
    pair_ref[:width] = low(x)
    pair_ref[width:] = low(e)

    def step(_, err):
        c = 2.0 / (2.0 - err * err)
        product = dot1(pair_ref[...], pair_ref[width:])
        x = c * (x_ref[...] + product[:width])
        x_ref[...] = x
        pair_ref[:width] = low(x)
        pair_ref[width:] = low(on_diagonal(1.0 - c) + c * product[width:])
        return err * err / (2.0 - err * err)

    error = lax.fori_loop(0, steps - 2, step, error * error / (2.0 - error * error))
    c = 2.0 / (2.0 - error * error)
    x_ref[...] = c * (x_ref[...] + dot1(pair_ref[:width], pair_ref[width:]))
    error = error * error / (2.0 - error * error)

    def polish(_, unused):
        x = x_ref[...]
        residual = on_diagonal(1.0) - delta * x - dot3(b_ref[...], x)
        rough = low(residual)
        x_ref[...] = x + dot1(low(x), low(residual + dot1(rough, rough)))
        return total(residual * residual)

    residual = lax.fori_loop(0, fine, polish, jnp.zeros((1, 1), F32))
    return jnp.maximum(bad_if(error, reach), bad_if(residual, limit))


def bad_if(value, limit):
    return jnp.where(value <= limit, 0.0, 1.0)


def far_products(left, right, out, x_ref):
    carried = dot3(left[2][...], x_ref[...])
    transposed = dot3(carried, right[2][...])
    out[2][...] = transposed
    out[3][...] = jnp.transpose(transposed)
    out[1][...] = dot3(dot3(carried, right[1][...]), left[3][...]) + left[1][...]
    spread = dot3(left[0][...], x_ref[...])
    out[0][...] = dot3(dot3(right[3][...], spread), right[2][...]) + right[0][...]
    return carried


def near_products(left, right, out, x_ref):
    eye = jnp.where(diagonal_mask(x_ref.shape[0]), 1.0, 0.0)
    past = low(x_ref[...] - eye)
    carried = left[2][...] + dot1(low(left[2][...]), past)
    transposed = dot3(carried, right[2][...])
    out[2][...] = transposed
    out[3][...] = jnp.transpose(transposed)
    out[1][...] = dot3(dot3(carried, right[1][...]), left[3][...]) + left[1][...]
    spread = left[0][...] + dot1(low(left[0][...]), past)
    spread = spread + dot1(low(right[3][...] - eye), low(spread))
    out[0][...] = spread + dot1(low(spread), low(right[2][...] - eye)) + right[0][...]
    return carried


def merge_chains(left, right, out, x_ref, b_ref, pair_ref, steps, fine, reach, products, before_products):
    b_ref[...] = dot1(low(right[1][...]), low(left[0][...]))
    failed = invert(b_ref, 1.0, 1.0, steps, fine, reach, 0.2, x_ref, pair_ref)
    before_products()
    carried = products(left, right, out, x_ref)
    b1, e1, b2, e2 = left[4](), left[5](), right[4](), right[5]()
    b1_column = to_column(b1)
    row = column_to_row(b1_column + row_to_column(e2, left[0][...]), x_ref[...])
    b = to_row(row_to_column(row, right[3][...])) + b2
    row = e2 - column_to_row(b1_column, right[1][...])
    e = to_row(row_to_column(row, carried)) + e1
    return b, e, failed


def open_chain(left, right, x_ref, x, lam):
    t = row_dot(lam, right[3][...]) + right[5]()
    drift = row_to_column(x, left[3][...]) + to_column(left[4]()) + row_to_column(t, left[0][...])
    middle = column_to_row(drift, x_ref[...])
    return middle, t - row_dot(middle, right[1][...])


def fast_kernel(
    devices, greenhouses, rows_in,
    states_ref, gradient_ref, mask_ref, zone_ref, map_ref, own_ref, bias_ref, wout_hbm,
    out_ref, bad_ref,
    parts, whole, wout, small, sect, slope, k_ref, kt_ref, leaf, leaf_v, chain, chain_a, chain_v, top, top_v,
    x0_ref, x1_ref, x2_ref, xr_ref, b_ref, pair_ref, side, side_v, z_ref, z_v, zo_ref, zo_v, zout, zout_v,
    pack_out, pack_in, pack_v, o_buf, o_in, result, result_in, flags, middle_v, weighted,
    w_send, w_recv, s_send, s_recv, local_sem, c_send, c_recv, p_send, p_recv, q_send, q_recv, v_send, v_recv,
    o_send, o_recv, r_send, r_recv, f_send, f_recv,
):
    width = states_ref.shape[1]
    groups = devices // 4
    me = lax.axis_index("tm")
    house = lax.axis_index("scen")
    g = lax.div(me, 4)
    r = lax.rem(me, 4)
    c = lax.rem(r, 2)
    y = lax.div(r, 2)
    core = me + 1 - 2 * c
    across = me + 2 - 4 * y
    diagonal = across + 1 - 2 * c
    is_left = g < groups // 2
    depth = jnp.where(is_left, g, groups - 1 - g)
    inward = me + jnp.where(is_left, 4, -4)
    outward = me - jnp.where(is_left, 4, -4)
    is_root = depth == groups // 2 - 1
    is_end = depth == 0
    left_root = jnp.logical_and(is_root, is_left)
    right_root = jnp.logical_and(is_root, jnp.logical_not(is_left))
    right_end = jnp.logical_and(is_end, jnp.logical_not(is_left))
    left_end = jnp.logical_and(is_end, is_left)
    solves = jnp.logical_not(right_end)
    writes = y == c

    def remote(src, dst, send, recv, target):
        return pltpu.make_async_remote_copy(
            src_ref=src, dst_ref=dst, send_sem=send, recv_sem=recv, device_id=target, device_id_type=MESH
        )

    cleanup = []

    wout_copy = pltpu.make_async_copy(wout_hbm, wout, local_sem)
    wout_copy.start()

    barrier = pltpu.get_barrier_semaphore()

    def greet(target):
        pl.semaphore_signal(barrier, inc=1, device_id=target, device_id_type=MESH)

    for target in (core, across, diagonal):
        greet({"tm": target})
    for k in range(1, greenhouses):
        greet({"scen": lax.rem(house + k, greenhouses)})

    for k in range(1, groups):
        greet({"tm": 4 * lax.rem(g + k, groups) + r})

    weights = jnp.zeros(gradient_ref.shape, F32)
    for zone in range(zone_ref.shape[1]):
        weights = jnp.where(map_ref[...][None] == zone, zone_ref[:, zone : zone + 1], weights)
    weights = weights * (1.0 + 4.0 * mask_ref[...].astype(F32))
    small[r] = jnp.zeros((8, width), F32)
    small[r, 0:2] = states_ref[...].astype(F32)
    small[r, 2:4] = gradient_ref[...]
    small[r, 4:6] = weights
    mine = own_ref[...].astype(F32)
    chunks, _, span = parts.shape[2:]
    pieces = mine.shape[1] // span
    folded = low(jnp.concatenate([mine[:, k * span : (k + 1) * span] for k in range(pieces)], axis=0))
    for j in range(chunks):
        parts[g, r, j] = folded[16 * j : 16 * j + 16]
    sect[...] = jnp.zeros_like(sect)

    pl.semaphore_wait(barrier, 3 + greenhouses - 1 + groups - 1)

    shared = greenhouses == 2
    share = chunks // 2
    some = pl.ds(share * house, share) if shared else pl.ds(0, chunks)
    alone = some
    missing = pl.ds(share * (1 - house), share)
    other = lax.rem(r + 2, 4)

    def line_copy(k, way, sender):
        block = parts.at[sender, r, some]
        return remote(block, block, w_send.at[way, k], w_recv.at[0, sender], {"tm": me + 4 * k * (1 - 2 * way)})

    def across_copy(sender, row):
        block = parts.at[sender, row, some]
        return remote(block, block, w_send.at[2, sender], w_recv.at[1, sender], {"tm": across})

    def hand_copy(sender, row, which_row, chunk):
        block = parts.at[sender, row, chunk]
        return remote(block, block, w_send.at[3 + which_row, sender], w_recv.at[2 + which_row, sender], {"scen": 1 - house})

    def core_copy(row, k, chunk):
        block = parts.at[:, row, chunk]
        return remote(block, block, w_send.at[5, k], w_recv.at[4, k], {"tm": core})

    small_copies = [
        remote(small.at[r], small.at[r], s_send.at[k], s_recv.at[r], {"tm": target})
        for k, target in enumerate((core, across, diagonal))
    ]

    def begin(copy):
        copy.start()

    def end(copy):
        copy.wait_send()

    def by_distance(visit, least=1):
        for k in range(least, groups):
            if k == 0:
                visit(0, g)
                continue

            @pl.when(g >= k)
            def _():
                visit(k, g - k)

            @pl.when(g + k <= groups - 1)
            def _():
                visit(k, g + k)

    def line(act):
        act(across_copy(g, r))
        for k in range(1, groups):
            for way in range(2):
                @pl.when(g + k <= groups - 1 if way == 0 else g >= k)
                def _():
                    act(line_copy(k, way, g))
        if act is begin:
            for copy in small_copies:
                copy.start()

        def from_line(k, sender):
            if act is begin:
                line_copy(k, 0, sender).wait_recv()
            act(across_copy(sender, r))
            if shared:
                act(hand_copy(sender, r, 0, alone))

        by_distance(from_line)
        act(core_copy(r, 0, some))

        def from_across(k, sender):
            if act is begin:
                across_copy(sender, other).wait_recv()
            if shared:
                act(hand_copy(sender, other, 1, alone))

        by_distance(from_across, 0)
        act(core_copy(other, 1, some))
        if shared:
            if act is begin:
                by_distance(lambda k, sender: hand_copy(sender, r, 0, missing).wait_recv())
            act(core_copy(r, 2, missing))
            if act is begin:
                by_distance(lambda k, sender: hand_copy(sender, other, 1, missing).wait_recv(), 0)
            act(core_copy(other, 3, missing))

    line(begin)
    cleanup.append(lambda: line(end))
    cleanup.append(lambda: [copy.wait_send() for copy in small_copies] and None)
    beside = lax.rem(core, 4)
    beyond = lax.rem(diagonal, 4)
    core_copy(beside, 0, some).wait_recv()
    core_copy(beyond, 1, some).wait_recv()
    if shared:
        core_copy(beside, 2, missing).wait_recv()
        core_copy(beyond, 3, missing).wait_recv()
    for target in (core, across, diagonal):
        remote(small.at[r], small.at[lax.rem(target, 4)], s_send.at[0], s_recv.at[lax.rem(target, 4)], {"tm": core}).wait_recv()

    batch = next(q for q in range(1, 17) if q * rows_in % 16 == 0)
    for first in range(0, devices, batch):
        blocks = [
            jnp.concatenate([parts[(first + k) // 4, (first + k) % 4, j].astype(F32) for j in range(chunks)], axis=0) for k in range(batch)
        ]
        for j in range(pieces):
            tall = jnp.concatenate([block[j * rows_in : (j + 1) * rows_in] for block in blocks], axis=0)
            whole[first * rows_in : (first + batch) * rows_in, j * span : (j + 1) * span] = low(tall)

    for k in range(3):
        sect[k, 0:2] = small[2 * c, 2 * k : 2 * k + 2]
        sect[k, 2:4] = small[2 * c + 1, 2 * k : 2 * k + 2]
    hidden = dot1(low(sect[0]), whole[...]) + bias_ref[...][None]
    bent = jnp.tanh(hidden)
    slope[...] = low(1.0 - bent * bent).astype(F32)
    wout_copy.wait()

    def sections(q, carry):
        for k in range(2):
            weighted[k * width : (k + 1) * width] = whole[...] * low(slope[pl.ds(2 * q + k, 1), :])
        product = dot1(weighted[...], wout[...])
        for k in range(2):
            one = product[k * width : (k + 1) * width]
            k_ref[2 * q + k] = one
            kt_ref[2 * q + k] = jnp.transpose(one)
        return carry

    lax.fori_loop(0, 2, sections, 0)

    eye = diagonal_mask(width)

    def on_diagonal(row):
        return jnp.where(eye, row, 0.0)

    def column(row):
        return jnp.sum(on_diagonal(row), axis=1, keepdims=True)

    def pair(q, carry):
        w0, w1 = sect[2, pl.ds(2 * q, 1)], sect[2, pl.ds(2 * q + 1, 1)]
        g0, g1 = sect[1, pl.ds(2 * q, 1)], sect[1, pl.ds(2 * q + 1, 1)]
        d = 1.0 / (1.0 + w1)
        dw = w1 * d
        k0, k1, k0t, k1t = k_ref[2 * q], k_ref[2 * q + 1], kt_ref[2 * q], kt_ref[2 * q + 1]
        scaled = column(d) * k1
        transposed = on_diagonal(d) + k0 * d + scaled + dot1(low(k0 * d), low(k1))
        leaf[q, 2] = transposed
        leaf[q, 3] = jnp.transpose(transposed)
        leaf[q, 0] = on_diagonal(1.0 + d) + scaled + k1t * d + dot1(low(k1t * d), low(k1))
        light = k0 * dw
        leaf[q, 1] = on_diagonal(w0 + dw) + light + column(dw) * k0t + dot1(low(light), low(k0t))
        rhs = d * g1
        rhs_column = to_column(rhs)
        leaf_v[q, 0:1] = rhs + column_to_row(rhs_column, k1)
        leaf_v[q, 1:2] = rhs + column_to_row(rhs_column, k0t) + g0
        return carry

    lax.fori_loop(0, 2, pair, 0)

    def chain_of(quad, fourth, vector):
        return [quad.at[0], quad.at[1], quad.at[2], fourth, lambda: vector[0:1], lambda: vector[1:2]]

    lower, upper = (chain_of(leaf.at[q], leaf.at[q, 3], leaf_v.at[q]) for q in range(2))
    mine = chain_of(chain.at[c], chain_a.at[c], chain_v.at[c])
    b, e, failed = merge_chains(lower, upper, mine, x0_ref, b_ref, pair_ref, 2, 0, 1e-3, near_products, lambda: None)
    chain_v[c] = jnp.zeros((8, width), F32)
    chain_v[c, 0:1] = b
    chain_v[c, 1:2] = e
    chain_v[c, 2:3] = jnp.broadcast_to(failed, (1, width))

    def chain_copy(slot, k):
        return remote(chain.at[slot, k], chain.at[slot, k], c_send.at[k], c_recv.at[k], {"tm": core})

    def vector_copy(slot):
        return remote(chain_v.at[slot], chain_v.at[slot], c_send.at[3], c_recv.at[3], {"tm": core})

    chain_copy(c, c).start()
    chain_copy(c, 1 - c).start()
    chain_copy(c, 2).start()
    vector_copy(c).start()
    cleanup.append(lambda: [chain_copy(c, k).wait_send() for k in range(3)] and None)
    cleanup.append(lambda: vector_copy(c).wait_send())
    chain_copy(1 - c, 1 - c).wait_recv()

    def rest_arrived():
        chain_copy(1 - c, c).wait_recv()
        chain_copy(1 - c, 2).wait_recv()
        vector_copy(1 - c).wait_recv()
        chain_a[1 - c] = jnp.transpose(chain[1 - c, 2])

    first, second = (chain_of(chain.at[q], chain_a.at[q], chain_v.at[q]) for q in range(2))
    b, e, failed = merge_chains(first, second, chain_of(top, top.at[3], top_v), x1_ref, b_ref, pair_ref, 3, 1, 0.02, far_products, rest_arrived)
    bad = jnp.maximum(jnp.maximum(chain_v[0, 2:3], chain_v[1, 2:3]), failed)

    sign = jnp.where(is_left, 1.0, -1.0)
    for k, (a_index, b_index) in enumerate(((3, 2), (2, 3), (1, 0), (0, 1))):
        side[k] = jnp.where(is_left, top[a_index], top[b_index])
    side_v[0:1] = jnp.where(is_left, e, -b)
    side_v[1:2] = jnp.where(is_left, b, e)
    side_v[2:3] = bad

    blocks = width // 128
    tiles = [(i, j) for i in range(blocks) for j in range(i + 1)]
    half = len(tiles) // 2

    def tile_copy(which, k):
        return remote(pack_out.at[k], pack_in.at[which, k], p_send.at[k], p_recv.at[which, k], {"tm": inward})

    def tile_pass(which, k):
        return remote(pack_in.at[which, k], pack_in.at[which, k], q_send.at[which, k], q_recv.at[which, k], {"tm": core})

    def row_copy(which):
        return remote(zout_v, pack_v.at[which], v_send, v_recv.at[which], {"tm": inward})

    def receive(which, m_ref, row_ref):
        for j in range(half):
            tile_copy(which, 2 * j + c).wait_recv()
            tile_pass(which, 2 * j + c).start()
        for j in range(half):
            tile_pass(which, 2 * j + 1 - c).wait_recv()
        row_copy(which).wait_recv()
        for k, (i, j) in enumerate(tiles):
            tile = pack_in[which, k]
            m_ref[128 * i : 128 * i + 128, 128 * j : 128 * j + 128] = tile
            if i != j:
                m_ref[128 * j : 128 * j + 128, 128 * i : 128 * i + 128] = jnp.transpose(tile)
        row_ref[...] = pack_v[which]

    @pl.when(is_end)
    def _():
        z_ref[...] = jnp.where(eye, 1.0, 0.0)
        z_v[...] = jnp.zeros_like(z_v)
        b_ref[...] = side[2]

    @pl.when(jnp.logical_not(is_end))
    def _():
        receive(0, z_ref, z_v)
        b_ref[...] = dot3(side[2], z_ref[...])

    @pl.when(solves)
    def _():
        delta = jnp.where(left_end, 0.0, 1.0)
        floor = jnp.min(small[0, 4:5], axis=1, keepdims=True)
        least = jnp.where(left_end, floor, 1.0)
        failed = invert(b_ref, delta, least, jnp.where(left_end, 6, 5), 1, 0.2, 1.5, x2_ref, pair_ref)

        @pl.when(left_end)
        def _():
            zo_ref[...] = x2_ref[...]

        @pl.when(jnp.logical_not(left_end))
        def _():
            zo_ref[...] = dot3(z_ref[...], x2_ref[...])

        zout[...] = dot3(dot3(side[0], zo_ref[...]), side[1]) + side[3]
        v = side_v[0:1]
        row = column_to_row(to_column(z_v[0:1]) + row_to_column(v, z_ref[...]), x2_ref[...])
        zout_v[...] = jnp.zeros_like(zout_v)
        zout_v[0:1] = to_row(row_to_column(row, side[0])) + side_v[1:2]
        zout_v[2:3] = jnp.maximum(jnp.maximum(side_v[2:3], z_v[2:3]), failed)

    @pl.when(right_end)
    def _():
        zout[...] = side[3]
        zout_v[...] = jnp.zeros_like(zout_v)
        zout_v[0:1] = side_v[1:2]
        zout_v[2:3] = side_v[2:3]

    which = is_root.astype(jnp.int32)

    @pl.when(jnp.logical_not(left_root))
    def _():
        for k, (i, j) in enumerate(tiles):
            pack_out[k] = zout[128 * i : 128 * i + 128, 128 * j : 128 * j + 128]
        for j in range(half):
            tile_copy(which, 2 * j + c).start()
        row_copy(which).start()

    def tiles_sent():
        @pl.when(jnp.logical_not(left_root))
        def _():
            for j in range(half):
                tile_copy(which, 2 * j + c).wait_send()
            row_copy(which).wait_send()

        @pl.when(jnp.logical_not(is_end))
        def _():
            for j in range(half):
                tile_pass(0, 2 * j + c).wait_send()

    cleanup.append(tiles_sent)
    def outer_copy():
        return remote(o_buf, o_in, o_send, o_recv, {"tm": outward})

    def middle_copy():
        return remote(middle_v, o_in, f_send.at[0], f_recv.at[0], {"tm": inward})

    flag_copies = []
    for k in range(1, greenhouses):
        flag_copies.append(
            remote(flags.at[0], flags.at[k], f_send.at[k], f_recv.at[k], {"scen": lax.rem(house + k, greenhouses)})
        )
    last = greenhouses

    def flag_out(k, target):
        return remote(flags.at[last], flags.at[last], f_send.at[greenhouses + k], f_recv.at[greenhouses], {"tm": target})

    @pl.when(left_root)
    def _():
        receive(1, zo_ref, zo_v)
        b_ref[...] = dot3(zo_ref[...], zout[...])
        invert(b_ref, 1.0, 1.0, 5, 0, 0.3, 1.0, xr_ref, pair_ref)
        rhs = to_column(zout_v[0:1]) + row_to_column(zo_v[0:1], zout[...])
        value = column_to_row(rhs, xr_ref[...])
        for _ in range(3):
            column_now = to_column(value)
            left_over = rhs - column_now - row_to_column(column_to_row(column_now, zo_ref[...]), zout[...])
            value = value + column_to_row(left_over, xr_ref[...])
        failed = bad_if(total(left_over * left_over), 1e-4 * total(rhs * rhs))
        middle_v[...] = jnp.broadcast_to(value, middle_v.shape)
        middle_copy().start()
        o_in[0:1] = zo_v[0:1] - row_dot(value, zo_ref[...])
        flags[0] = jnp.broadcast_to(
            jnp.maximum(jnp.maximum(zout_v[2:3, :128], zo_v[2:3, :128]), failed), (8, 128)
        )
        for copy in flag_copies:
            copy.start()

    @pl.when(right_root)
    def _():
        middle_copy().wait_recv()

    @pl.when(jnp.logical_not(is_root))
    def _():
        outer_copy().wait_recv()

    outer = o_in[0:1]
    side_v[3:4] = jnp.zeros((1, width), F32)

    @pl.when(solves)
    def _():
        w = sign * side_v[0:1] + row_dot(outer, side[0])
        value = column_to_row(to_column(z_v[0:1]) + sign * row_to_column(w, z_ref[...]), x2_ref[...])
        side_v[3:4] = value
        o_buf[...] = jnp.broadcast_to(w - sign * row_dot(value, side[2]), o_buf.shape)

    @pl.when(jnp.logical_not(is_end))
    def _():
        outer_copy().start()

    own_value = side_v[3:4]
    start = jnp.where(is_left, own_value, outer)
    finish_lam = jnp.where(is_left, outer, own_value)

    def result_copy(slot):
        return remote(result.at[slot], result_in, r_send, r_recv, {"tm": core})

    @pl.when(writes)
    def _():
        middle, lam = open_chain(first, second, x1_ref, start, finish_lam)
        x_a = jnp.where(c == 0, start, middle)
        lam_b = jnp.where(c == 0, lam, finish_lam)
        middle, lam = open_chain(lower, upper, x0_ref, x_a, lam_b)
        for q, x, lam_q in ((0, x_a, lam), (1, middle, lam_b)):
            w1, g1 = sect[2, 2 * q + 1 : 2 * q + 2], sect[1, 2 * q + 1 : 2 * q + 2]
            result[q, 0:1] = x
            result[q, 1:2] = (
                x + row_dot(x, k_ref[2 * q]) + lam_q + row_dot(lam_q, kt_ref[2 * q + 1]) + g1
            ) / (1.0 + w1)
        result_copy(1 - c).start()
        out_ref[...] = result[c, 0:2]

    @pl.when(jnp.logical_not(writes))
    def _():
        result_copy(0).wait_recv()
        out_ref[...] = result_in[0:2]

    @pl.when(left_root)
    def _():
        for copy in flag_copies:
            copy.wait_recv()
        worst = flags[0]
        for k in range(1, greenhouses):
            worst = jnp.maximum(worst, flags[k])
        flags[last] = worst
        flag_out(1, inward).start()

    @pl.when(jnp.logical_not(left_root))
    def _():
        flag_out(0, outward).wait_recv()

    @pl.when(jnp.logical_not(is_end))
    def _():
        flag_out(0, outward).start()

    bad_ref[...] = flags[last, 0:1, 0:1]

    def rest_sent():
        @pl.when(jnp.logical_not(is_end))
        def _():
            outer_copy().wait_send()
            flag_out(0, outward).wait_send()

        @pl.when(left_root)
        def _():
            for j in range(half):
                tile_pass(1, 2 * j + c).wait_send()
            middle_copy().wait_send()
            flag_out(1, inward).wait_send()
            for copy in flag_copies:
                copy.wait_send()

        @pl.when(writes)
        def _():
            result_copy(1 - c).wait_send()

    cleanup.append(rest_sent)
    for act in cleanup:
        act()

def fast_device(states, gradient, active_mask, zone_weight, zone_map, w_in, w_out, bias):
    width = states.shape[1]
    hidden = w_in.shape[1]
    devices = lax.axis_size("tm")
    greenhouses = lax.axis_size("scen")
    rows = w_in.shape[0]
    pieces = 32 // math.gcd(rows, 16)
    span = hidden // pieces
    chunks = pieces * rows // 16
    tiles = (width // 128) * (width // 128 + 1) // 2
    square = lambda *lead: pltpu.VMEM(lead + (width, width), F32)
    lines = lambda *lead: pltpu.VMEM(lead + (8, width), F32)
    dma = pltpu.SemaphoreType.DMA
    vmem = pl.BlockSpec(memory_space=pltpu.VMEM)
    scratch = [
        pltpu.VMEM((devices // 4, 4, chunks, 16, span), BF16), pltpu.VMEM((rows * devices, hidden), BF16), pltpu.VMEM(w_out.shape, BF16),
        lines(4), lines(3), pltpu.VMEM((8, hidden), F32), square(4), square(4), square(2, 4), lines(2),
        square(2, 3), square(2), lines(2), square(4), lines(),
        square(), square(), square(), square(), square(), pltpu.VMEM((2 * width, width), BF16), square(4), lines(),
        square(), lines(), square(), lines(), square(), lines(),
        pltpu.VMEM((tiles, 128, 128), F32), pltpu.VMEM((2, tiles, 128, 128), F32), lines(2), lines(), lines(), lines(2), lines(),
        pltpu.VMEM((1 + greenhouses, 8, 128), F32), lines(),
        pltpu.VMEM((2 * width, hidden), BF16),
        dma((6, max(4, devices // 4))), dma((5, max(4, devices // 4))), dma((3,)), dma((4,)), dma, dma((4,)), dma((4,)), dma((tiles,)), dma((2, tiles)),
        dma((2, tiles)), dma((2, tiles)), dma, dma((2,)), dma, dma, dma, dma,
        dma((greenhouses + 2,)), dma((greenhouses + 1,)),
    ]
    return pl.pallas_call(
        functools.partial(fast_kernel, devices, greenhouses, rows),
        out_shape=(jax.ShapeDtypeStruct((2, width), F32), jax.ShapeDtypeStruct((1, 1), F32)),
        in_specs=[vmem] * 7 + [pl.BlockSpec(memory_space=pl.ANY)],
        out_specs=(vmem, vmem),
        scratch_shapes=scratch,
        compiler_params=pltpu.CompilerParams(collective_id=0, has_side_effects=True, vmem_limit_bytes=58 << 20),
        name="gauss_newton",
    )(states, gradient, active_mask, zone_weight, zone_map, w_in, bias, w_out)


def per_device(*arrays):
    value, bad = fast_device(*arrays)
    return lax.cond(bad[0, 0] > 0.0, lambda: direct_device(*arrays), lambda: value)


def solution(mesh):
    return jax.shard_map(
        per_device,
        mesh=mesh,
        in_specs=(
            P(("scen", "tm"), None),
            P(("scen", "tm"), None),
            P(("scen", "tm"), None),
            P(("scen", "tm"), None),
            P("scen"),
            P("tm", None),
            P(),
            P(),
        ),
        out_specs=P(("scen", "tm"), None),
        check_vma=False,
    )
```

```python
import functools
import math

import jax
import jax.numpy as jnp
from jax import lax
from jax.experimental import pallas as pl
from jax.experimental.pallas import tpu as pltpu
from jax.sharding import PartitionSpec as P


def from_partner(array, axis, bit):
    return lax.ppermute(array, axis, [(i, i ^ 1 << bit) for i in range(lax.axis_size(axis))])


def matmul(left, right):
    return jnp.dot(left, right, precision=lax.Precision.HIGHEST)


def dot_exact(left, right, dims=((1,), (0,))):
    return lax.dot_general(
        left, right, (dims, ((), ())), precision=lax.Precision.HIGHEST, preferred_element_type=jnp.float32
    )


def dot_fast(left, right):
    return jnp.dot(
        left.astype(jnp.bfloat16), right.astype(jnp.bfloat16), preferred_element_type=jnp.float32
    )


def invert_in_place(m_ref, x_ref, e_ref):
    width = m_ref.shape[0]
    row_ids = lax.broadcasted_iota(jnp.int32, (width, width), 0)
    col_ids = lax.broadcasted_iota(jnp.int32, (width, width), 1)
    diagonal = row_ids == col_ids
    matrix = m_ref[...]
    square = dot_fast(matrix, matrix)
    trace = jnp.sum(jnp.where(diagonal, matrix, 0.0))
    frobenius = jnp.sum(matrix * matrix)
    bound = jnp.max(jnp.sum(jnp.abs(square), axis=1))
    scale = jnp.minimum(trace / frobenius, 1.9 * lax.rsqrt(bound))
    x_ref[...] = jnp.where(diagonal, 2.0 * scale, 0.0) - (scale * scale) * matrix
    first = jnp.where(diagonal, 1.0, 0.0) - (2.0 * scale) * matrix + (scale * scale) * square
    e_ref[...] = first

    def coarse_step(carry):
        count, _ = carry
        x_ref[...] = x_ref[...] + dot_fast(x_ref[...], e_ref[...])
        residual = jnp.where(diagonal, 1.0, 0.0) - dot_fast(m_ref[...], x_ref[...])
        e_ref[...] = residual
        return count + 1, jnp.sum(residual * residual)

    lax.while_loop(lambda c: (c[0] < 10) & (c[1] > 0.25), coarse_step, (0, jnp.sum(first * first)))

    def fine_step(carry):
        count, _ = carry
        residual = jnp.where(diagonal, 1.0, 0.0) - dot_exact(m_ref[...], x_ref[...])
        x_ref[...] = x_ref[...] + dot_fast(x_ref[...], residual)
        return count + 1, jnp.sum(residual * residual)

    _, last = lax.while_loop(
        lambda c: (c[0] < 12) & jnp.logical_not(c[1] <= 1e-7), fine_step, (0, jnp.float32(1.0))
    )

    @pl.when(jnp.logical_not(last <= 1e-7))
    def _():
        x_ref[...] = m_ref[...]

        def pivot_step(k, carry):
            current = x_ref[...]
            row = x_ref[pl.ds(k, 1), :]
            column = jnp.sum(jnp.where(col_ids == k, current, 0.0), axis=1, keepdims=True)
            pivot = jnp.sum(jnp.where(col_ids[:1] == k, row, 0.0), axis=1, keepdims=True)
            scaled = row / pivot
            updated = jnp.where(col_ids == k, -column / pivot, current - column * scaled)
            own_row = jnp.where(col_ids == k, 1.0 / pivot, scaled)
            x_ref[...] = jnp.where(row_ids == k, own_row, updated)
            return carry

        lax.fori_loop(0, width, pivot_step, 0)


def unpack_first(packed, row_ids, col_ids):
    return jnp.where(row_ids <= col_ids, packed, jnp.transpose(packed))


def unpack_last(packed, diagonal, row_ids, col_ids):
    whole = jnp.where(row_ids > col_ids, packed, jnp.transpose(packed))
    return jnp.where(row_ids == col_ids, diagonal, whole)


def finish(left, right, rhs, ff, ll, fr, lr, x_ref, block_ref, vector_ref, gl_ref, gr_ref, gs_ref):
    width = x_ref.shape[0]
    inverse = x_ref[...]
    gl_ref[...] = dot_exact(left, inverse)
    gr_ref[...] = dot_exact(inverse, right)
    solved = dot_exact(jnp.broadcast_to(rhs, (8, width)), inverse)
    gs_ref[...] = solved[:1]
    row_ids = lax.broadcasted_iota(jnp.int32, (width, width), 0)
    col_ids = lax.broadcasted_iota(jnp.int32, (width, width), 1)
    new_ff = ff() - dot_exact(gl_ref[...], left, ((1,), (1,)))
    block_ref[width : 2 * width] = -dot_exact(gl_ref[...], right)
    new_ll = ll() - dot_exact(jnp.transpose(right), gr_ref[...])
    block_ref[:width] = jnp.where(row_ids <= col_ids, new_ff, new_ll)
    vector_ref[2:3] = jnp.sum(jnp.where(row_ids == col_ids, new_ll, 0.0), axis=0, keepdims=True)
    vector_ref[0:1] = fr - dot_exact(solved, left, ((1,), (1,)))[:1]
    vector_ref[1:2] = lr - dot_exact(solved, right)[:1]


def first_kernel(
    m_ref, mr_ref, l_ref, r_ref, ff_ref, ll_ref, fr_ref, lr_ref,
    block_ref, vector_ref, gl_ref, gr_ref, gs_ref, x_ref, e_ref
):
    invert_in_place(m_ref, x_ref, e_ref)
    finish(
        l_ref[...], r_ref[...], mr_ref[...], lambda: ff_ref[...], lambda: ll_ref[...],
        fr_ref[...], lr_ref[...], x_ref, block_ref, vector_ref, gl_ref, gr_ref, gs_ref
    )


def merge_kernel(
    flag_ref, own_ref, other_ref, ov_ref, pv_ref,
    block_ref, vector_ref, gl_ref, gr_ref, gs_ref, x_ref, e_ref, m_ref
):
    width = x_ref.shape[0]
    is_upper = flag_ref[0] == 1
    spans = [pl.ds(k * width, width) for k in range(2)]
    row_ids = lax.broadcasted_iota(jnp.int32, (width, width), 0)
    col_ids = lax.broadcasted_iota(jnp.int32, (width, width), 1)
    lower_rhs = jnp.where(is_upper, pv_ref[...], ov_ref[...])
    upper_rhs = jnp.where(is_upper, ov_ref[...], pv_ref[...])

    def lower(k):
        return jnp.where(is_upper, other_ref[spans[k], :], own_ref[spans[k], :])

    def upper(k):
        return jnp.where(is_upper, own_ref[spans[k], :], other_ref[spans[k], :])

    m_ref[...] = unpack_last(lower(0), lower_rhs[2:3], row_ids, col_ids) + unpack_first(
        upper(0), row_ids, col_ids
    )
    invert_in_place(m_ref, x_ref, e_ref)
    finish(
        lower(1), upper(1), lower_rhs[1:2] + upper_rhs[0:1], lambda: unpack_first(lower(0), row_ids, col_ids),
        lambda: unpack_last(upper(0), upper_rhs[2:3], row_ids, col_ids),
        lower_rhs[0:1], upper_rhs[1:2], x_ref, block_ref, vector_ref, gl_ref, gr_ref, gs_ref
    )


def call_merge(kernel, name, width, parts, scratch, in_specs=None):
    full = jax.ShapeDtypeStruct((width, width), jnp.float32)
    result = pl.pallas_call(
        kernel,
        out_shape=(
            jax.ShapeDtypeStruct((2 * width, width), jnp.float32),
            jax.ShapeDtypeStruct((3, width), jnp.float32),
            full, full, jax.ShapeDtypeStruct((1, width), jnp.float32),
        ),
        in_specs=in_specs or [pl.BlockSpec(memory_space=pltpu.VMEM)] * len(parts),
        scratch_shapes=[pltpu.VMEM((width, width), jnp.float32)] * scratch,
        compiler_params=pltpu.CompilerParams(vmem_limit_bytes=48 << 20),
        name=name,
    )(*parts)
    return result[:2], result[2:]


def eliminate(*parts):
    return call_merge(
        first_kernel, "eliminate", parts[0].shape[0],
        [part if part.ndim == 2 else part[None] for part in parts], 2
    )


def merge(upper_flag, own, other):
    vmem = pl.BlockSpec(memory_space=pltpu.VMEM)
    return call_merge(
        merge_kernel, "merge", own[0].shape[1],
        [upper_flag.astype(jnp.int32)[None], own[0], other[0], own[1], other[1]], 3,
        [pl.BlockSpec(memory_space=pltpu.SMEM)] + [vmem] * 4
    )


def exchange(block, vector, core, level):
    if level == 0:
        return from_partner((block, vector), "tm", level)
    half = block.shape[0] // 2
    share = lax.dynamic_slice_in_dim(block, core * half, half, axis=0)
    received, other_vector = from_partner((share, vector), "tm", level)
    swapped = from_partner(received, "tm", 0)
    other = jnp.where(
        core == 1,
        jnp.concatenate([swapped, received]),
        jnp.concatenate([received, swapped]),
    )
    return other, other_vector


def gather_rows(rows, level_count):
    place = lax.axis_index("tm")
    held = rows[None]
    for level in reversed(range(level_count)):
        other = from_partner(held, "tm", level)
        upper_flag = jnp.bitwise_and(jnp.right_shift(place, level), 1) == 1
        held = jnp.stack([jnp.where(upper_flag, other, held), jnp.where(upper_flag, held, other)])
        held = held.reshape((-1,) + rows.shape)
    bits = held.reshape((2,) * level_count + rows.shape)
    order = tuple(reversed(range(level_count))) + (level_count, level_count + 1)
    return bits.transpose(order).reshape(-1, rows.shape[1])


def root_kernel(m_ref, mr_ref, o_ref, x_ref, e_ref):
    invert_in_place(m_ref, x_ref, e_ref)
    o_ref[...] = dot_exact(jnp.broadcast_to(mr_ref[...], (8, m_ref.shape[0])), x_ref[...])[:1]


def root_solve(matrix, rhs):
    width = matrix.shape[0]
    return pl.pallas_call(
        root_kernel,
        out_shape=jax.ShapeDtypeStruct((1, width), jnp.float32),
        scratch_shapes=[pltpu.VMEM((width, width), jnp.float32)] * 2,
        compiler_params=pltpu.CompilerParams(vmem_limit_bytes=48 << 20),
        name="root",
    )(matrix, rhs)


def direct_device(states, gradient, active_mask, zone_weight, zone_map, w_in, w_out, bias):
    width = states.shape[1]
    devices = lax.axis_size("tm")
    place = lax.axis_index("tm")
    is_first = place == 0
    is_last = place == devices - 1
    zone_count = zone_weight.shape[1]
    zone_table = (
        zone_map[None, :] == lax.broadcasted_iota(jnp.int32, (zone_count, width), 0)
    ).astype(jnp.float32)
    weights = jnp.dot(zone_weight, zone_table, precision=lax.Precision.HIGHEST) * (
        1.0 + 4.0 * active_mask.astype(jnp.float32)
    )
    later = jnp.stack([states[1].astype(jnp.float32), gradient[1], weights[1]])
    before = lax.ppermute(later, "tm", [(i, i + 1) for i in range(devices - 1)])
    whole_rows = gather_rows(w_in, devices.bit_length() - 1)
    rows = jnp.stack([before[0].astype(jnp.bfloat16), states[0]])
    hidden_in = jnp.dot(rows, whole_rows, preferred_element_type=jnp.float32) + bias
    slopes = (1.0 - jnp.tanh(hidden_in) ** 2).astype(jnp.bfloat16)
    weighted = slopes[:, None, :] * whole_rows[None, :, :]
    flat = weighted.reshape(2 * width, whole_rows.shape[1])
    product = jnp.dot(flat, w_out, preferred_element_type=jnp.float32).reshape(2, width, width)
    eye = jnp.eye(width, dtype=jnp.float32)
    jac_before = product[0] + eye
    jac_own = product[1] + eye
    last_diag = 1.0 / (1.0 + weights[1])
    column_scale = jnp.where(is_last, weights[1] * last_diag, 1.0)
    tail = jnp.where(is_last, gradient[1] * last_diag, 0.0)
    middle = (
        jnp.diag(weights[0] + jnp.where(is_first, 0.0, 1.0))
        + matmul(jac_own * column_scale[None, :], jac_own.T)
    )
    middle_rhs = gradient[0] + matmul(jac_own, tail)
    left = jnp.where(is_first, 0.0, -jac_before)
    right = jnp.where(is_last, 0.0, -jac_own)
    first_first = jnp.diag(before[2]) + matmul(left, left.T)
    own, local_store = eliminate(
        middle, middle_rhs, left, right, first_first, eye, before[1], jnp.zeros_like(middle_rhs)
    )
    core = jnp.bitwise_and(place, 1)
    level_count = devices.bit_length() - 1
    level_stores = []
    for level in range(level_count):
        upper_flag = jnp.bitwise_and(jnp.right_shift(place, level), 1) == 1
        if level == level_count - 1:
            row_ids = lax.broadcasted_iota(jnp.int32, (width, width), 0)
            packed, flipped = own[0][:width], own[0][:width].T
            keep = jnp.where(upper_flag, row_ids <= row_ids.T, row_ids > row_ids.T)
            block = jnp.where(keep, packed, flipped)
            block = jnp.where((row_ids == row_ids.T) & ~upper_flag, own[1][2:3], block)
            vector = jnp.where(upper_flag, own[1][:1], own[1][1:2])
            other_block, other_vector = exchange(block, vector, core, level)
            root = root_solve(block + other_block, vector + other_vector)[0]
            break
        own, store = merge(upper_flag, own, exchange(own[0], own[1], core, level))
        level_stores.append((store, upper_flag))
    top_flag = jnp.right_shift(place, level_count - 1) == 1
    start = jnp.where(top_flag, root, 0.0)
    end = jnp.where(top_flag, 0.0, root)
    for store, upper_flag in reversed(level_stores):
        value = back_solve(store, start, end)
        start = jnp.where(upper_flag, value, start)
        end = jnp.where(upper_flag, end, value)
    value = back_solve(local_store, start, end)
    end = jnp.where(is_last, tail + last_diag * matmul(value, jac_own), end)
    return jnp.stack([value, end], axis=0)


def back_solve(store, outer_first, outer_last):
    left_solved, right_solved, rhs_solved = store
    return rhs_solved[0] - matmul(outer_first, left_solved) - matmul(right_solved, outer_last)


MESH = pl.DeviceIdType.MESH
F32 = jnp.float32
BF16 = jnp.bfloat16


def low(x):
    return x.astype(BF16)


def dot1(a, b):
    return jnp.dot(a, b, preferred_element_type=F32)


def split(x):
    high = low(x)
    return high, low(x - high.astype(F32))


def dot3(a, b):
    ah, al = split(a)
    bh, bl = split(b)
    return dot1(jnp.concatenate([ah, ah, al], axis=1), jnp.concatenate([bh, bl, bh], axis=0))


def row_to_column(row, m):
    return jnp.sum(m * row, axis=1, keepdims=True)


def column_to_row(column, m):
    return jnp.sum(m * column, axis=0, keepdims=True)


def to_column(row):
    return row_to_column(row, jnp.where(diagonal_mask(row.shape[1]), 1.0, 0.0))


def to_row(column):
    return column_to_row(column, jnp.where(diagonal_mask(column.shape[0]), 1.0, 0.0))


def row_dot(row, m):
    return column_to_row(to_column(row), m)


def total(x):
    return jnp.sum(jnp.sum(x, axis=1, keepdims=True), axis=0, keepdims=True)


def diagonal_mask(width):
    return lax.broadcasted_iota(jnp.int32, (width, width), 0) == lax.broadcasted_iota(
        jnp.int32, (width, width), 1
    )


def invert(b_ref, delta, least, steps, fine, reach, limit, x_ref, pair_ref):
    width = b_ref.shape[0]
    eye = diagonal_mask(width)

    def on_diagonal(value):
        return jnp.where(eye, value, 0.0)

    whole = b_ref[...]
    coarse = low(whole)
    square = dot1(coarse, coarse)
    most = delta + jnp.sqrt(jnp.sqrt(total(square * square)))
    alpha = 2.0 / (least + most)
    error = (most - least) / (most + least)
    rest = 1.0 - alpha * delta
    factor = 2.0 / (2.0 - error * error)
    x = factor * alpha * (on_diagonal(1.0 + rest) - alpha * whole)
    e = on_diagonal(1.0 - factor + factor * rest * rest) + factor * (
        alpha * alpha * square - 2.0 * alpha * rest * whole
    )
    x_ref[...] = x
    pair_ref[:width] = low(x)
    pair_ref[width:] = low(e)

    def step(_, err):
        c = 2.0 / (2.0 - err * err)
        product = dot1(pair_ref[...], pair_ref[width:])
        x = c * (x_ref[...] + product[:width])
        x_ref[...] = x
        pair_ref[:width] = low(x)
        pair_ref[width:] = low(on_diagonal(1.0 - c) + c * product[width:])
        return err * err / (2.0 - err * err)

    error = lax.fori_loop(0, steps - 2, step, error * error / (2.0 - error * error))
    c = 2.0 / (2.0 - error * error)
    x_ref[...] = c * (x_ref[...] + dot1(pair_ref[:width], pair_ref[width:]))
    error = error * error / (2.0 - error * error)

    def polish(_, unused):
        x = x_ref[...]
        residual = on_diagonal(1.0) - delta * x - dot3(b_ref[...], x)
        rough = low(residual)
        x_ref[...] = x + dot1(low(x), low(residual + dot1(rough, rough)))
        return total(residual * residual)

    residual = lax.fori_loop(0, fine, polish, jnp.zeros((1, 1), F32))
    return jnp.maximum(bad_if(error, reach), bad_if(residual, limit))


def bad_if(value, limit):
    return jnp.where(value <= limit, 0.0, 1.0)


def far_products(left, right, out, x_ref):
    carried = dot3(left[2][...], x_ref[...])
    transposed = dot3(carried, right[2][...])
    out[2][...] = transposed
    out[3][...] = jnp.transpose(transposed)
    out[1][...] = dot3(dot3(carried, right[1][...]), left[3][...]) + left[1][...]
    spread = dot3(left[0][...], x_ref[...])
    out[0][...] = dot3(dot3(right[3][...], spread), right[2][...]) + right[0][...]
    return carried


def near_products(left, right, out, x_ref):
    eye = jnp.where(diagonal_mask(x_ref.shape[0]), 1.0, 0.0)
    past = low(x_ref[...] - eye)
    carried = left[2][...] + dot1(low(left[2][...]), past)
    transposed = dot3(carried, right[2][...])
    out[2][...] = transposed
    out[3][...] = jnp.transpose(transposed)
    out[1][...] = dot3(dot3(carried, right[1][...]), left[3][...]) + left[1][...]
    spread = left[0][...] + dot1(low(left[0][...]), past)
    spread = spread + dot1(low(right[3][...] - eye), low(spread))
    out[0][...] = spread + dot1(low(spread), low(right[2][...] - eye)) + right[0][...]
    return carried


def merge_chains(left, right, out, x_ref, b_ref, pair_ref, steps, fine, reach, products, before_products):
    b_ref[...] = dot1(low(right[1][...]), low(left[0][...]))
    failed = invert(b_ref, 1.0, 1.0, steps, fine, reach, 0.2, x_ref, pair_ref)
    before_products()
    carried = products(left, right, out, x_ref)
    b1, e1, b2, e2 = left[4](), left[5](), right[4](), right[5]()
    b1_column = to_column(b1)
    row = column_to_row(b1_column + row_to_column(e2, left[0][...]), x_ref[...])
    b = to_row(row_to_column(row, right[3][...])) + b2
    row = e2 - column_to_row(b1_column, right[1][...])
    e = to_row(row_to_column(row, carried)) + e1
    return b, e, failed


def open_chain(left, right, x_ref, x, lam):
    t = row_dot(lam, right[3][...]) + right[5]()
    drift = row_to_column(x, left[3][...]) + to_column(left[4]()) + row_to_column(t, left[0][...])
    middle = column_to_row(drift, x_ref[...])
    return middle, t - row_dot(middle, right[1][...])


def fast_kernel(
    devices, greenhouses, rows_in,
    states_ref, gradient_ref, mask_ref, zone_ref, map_ref, own_ref, bias_ref, wout_hbm,
    out_ref, bad_ref,
    parts, whole, wout, small, sect, slope, k_ref, kt_ref, leaf, leaf_v, chain, chain_a, chain_v, top, top_v,
    x0_ref, x1_ref, x2_ref, xr_ref, b_ref, pair_ref, side, side_v, z_ref, z_v, zo_ref, zo_v, zout, zout_v,
    pack_out, pack_in, pack_v, o_buf, o_in, result, result_in, flags, middle_v, weighted,
    w_send, w_recv, s_send, s_recv, local_sem, c_send, c_recv, p_send, p_recv, q_send, q_recv, v_send, v_recv,
    o_send, o_recv, r_send, r_recv, f_send, f_recv,
):
    width = states_ref.shape[1]
    groups = devices // 4
    me = lax.axis_index("tm")
    house = lax.axis_index("scen")
    g = lax.div(me, 4)
    r = lax.rem(me, 4)
    c = lax.rem(r, 2)
    y = lax.div(r, 2)
    core = me + 1 - 2 * c
    across = me + 2 - 4 * y
    diagonal = across + 1 - 2 * c
    is_left = g < groups // 2
    depth = jnp.where(is_left, g, groups - 1 - g)
    inward = me + jnp.where(is_left, 4, -4)
    outward = me - jnp.where(is_left, 4, -4)
    is_root = depth == groups // 2 - 1
    is_end = depth == 0
    left_root = jnp.logical_and(is_root, is_left)
    right_root = jnp.logical_and(is_root, jnp.logical_not(is_left))
    right_end = jnp.logical_and(is_end, jnp.logical_not(is_left))
    left_end = jnp.logical_and(is_end, is_left)
    solves = jnp.logical_not(right_end)
    writes = y == c

    def remote(src, dst, send, recv, target):
        return pltpu.make_async_remote_copy(
            src_ref=src, dst_ref=dst, send_sem=send, recv_sem=recv, device_id=target, device_id_type=MESH
        )

    cleanup = []

    wout_copy = pltpu.make_async_copy(wout_hbm, wout, local_sem)
    wout_copy.start()

    barrier = pltpu.get_barrier_semaphore()

    def greet(target):
        pl.semaphore_signal(barrier, inc=1, device_id=target, device_id_type=MESH)

    for target in (core, across, diagonal):
        greet({"tm": target})
    for k in range(1, greenhouses):
        greet({"scen": lax.rem(house + k, greenhouses)})

    for k in range(1, groups):
        greet({"tm": 4 * lax.rem(g + k, groups) + r})

    weights = jnp.zeros(gradient_ref.shape, F32)
    for zone in range(zone_ref.shape[1]):
        weights = jnp.where(map_ref[...][None] == zone, zone_ref[:, zone : zone + 1], weights)
    weights = weights * (1.0 + 4.0 * mask_ref[...].astype(F32))
    small[r] = jnp.zeros((8, width), F32)
    small[r, 0:2] = states_ref[...].astype(F32)
    small[r, 2:4] = gradient_ref[...]
    small[r, 4:6] = weights
    mine = own_ref[...].astype(F32)
    chunks, _, span = parts.shape[2:]
    pieces = mine.shape[1] // span
    folded = low(jnp.concatenate([mine[:, k * span : (k + 1) * span] for k in range(pieces)], axis=0))
    for j in range(chunks):
        parts[g, r, j] = folded[16 * j : 16 * j + 16]
    sect[...] = jnp.zeros_like(sect)

    pl.semaphore_wait(barrier, 3 + greenhouses - 1 + groups - 1)

    shared = greenhouses == 2
    share = chunks // 2
    some = pl.ds(share * house, share) if shared else pl.ds(0, chunks)
    alone = some
    missing = pl.ds(share * (1 - house), share)
    other = lax.rem(r + 2, 4)

    def line_copy(k, way, sender):
        block = parts.at[sender, r, some]
        return remote(block, block, w_send.at[way, k], w_recv.at[0, sender], {"tm": me + 4 * k * (1 - 2 * way)})

    def across_copy(sender, row):
        block = parts.at[sender, row, some]
        return remote(block, block, w_send.at[2, sender], w_recv.at[1, sender], {"tm": across})

    def hand_copy(sender, row, which_row, chunk):
        block = parts.at[sender, row, chunk]
        return remote(block, block, w_send.at[3 + which_row, sender], w_recv.at[2 + which_row, sender], {"scen": 1 - house})

    def core_copy(row, k, chunk):
        block = parts.at[:, row, chunk]
        return remote(block, block, w_send.at[5, k], w_recv.at[4, k], {"tm": core})

    small_copies = [
        remote(small.at[r], small.at[r], s_send.at[k], s_recv.at[r], {"tm": target})
        for k, target in enumerate((core, across, diagonal))
    ]

    def begin(copy):
        copy.start()

    def end(copy):
        copy.wait_send()

    def by_distance(visit, least=1):
        for k in range(least, groups):
            if k == 0:
                visit(0, g)
                continue

            @pl.when(g >= k)
            def _():
                visit(k, g - k)

            @pl.when(g + k <= groups - 1)
            def _():
                visit(k, g + k)

    def line(act):
        act(across_copy(g, r))
        for k in range(1, groups):
            for way in range(2):
                @pl.when(g + k <= groups - 1 if way == 0 else g >= k)
                def _():
                    act(line_copy(k, way, g))
        if act is begin:
            for copy in small_copies:
                copy.start()

        def from_line(k, sender):
            if act is begin:
                line_copy(k, 0, sender).wait_recv()
            act(across_copy(sender, r))
            if shared:
                act(hand_copy(sender, r, 0, alone))

        by_distance(from_line)
        act(core_copy(r, 0, some))

        def from_across(k, sender):
            if act is begin:
                across_copy(sender, other).wait_recv()
            if shared:
                act(hand_copy(sender, other, 1, alone))

        by_distance(from_across, 0)
        act(core_copy(other, 1, some))
        if shared:
            if act is begin:
                by_distance(lambda k, sender: hand_copy(sender, r, 0, missing).wait_recv())
            act(core_copy(r, 2, missing))
            if act is begin:
                by_distance(lambda k, sender: hand_copy(sender, other, 1, missing).wait_recv(), 0)
            act(core_copy(other, 3, missing))

    line(begin)
    cleanup.append(lambda: line(end))
    cleanup.append(lambda: [copy.wait_send() for copy in small_copies] and None)
    beside = lax.rem(core, 4)
    beyond = lax.rem(diagonal, 4)
    core_copy(beside, 0, some).wait_recv()
    core_copy(beyond, 1, some).wait_recv()
    if shared:
        core_copy(beside, 2, missing).wait_recv()
        core_copy(beyond, 3, missing).wait_recv()
    for target in (core, across, diagonal):
        remote(small.at[r], small.at[lax.rem(target, 4)], s_send.at[0], s_recv.at[lax.rem(target, 4)], {"tm": core}).wait_recv()

    batch = next(q for q in range(1, 17) if q * rows_in % 16 == 0)
    for first in range(0, devices, batch):
        blocks = [
            jnp.concatenate([parts[(first + k) // 4, (first + k) % 4, j].astype(F32) for j in range(chunks)], axis=0) for k in range(batch)
        ]
        for j in range(pieces):
            tall = jnp.concatenate([block[j * rows_in : (j + 1) * rows_in] for block in blocks], axis=0)
            whole[first * rows_in : (first + batch) * rows_in, j * span : (j + 1) * span] = low(tall)

    for k in range(3):
        sect[k, 0:2] = small[2 * c, 2 * k : 2 * k + 2]
        sect[k, 2:4] = small[2 * c + 1, 2 * k : 2 * k + 2]
    hidden = dot1(low(sect[0]), whole[...]) + bias_ref[...][None]
    bent = jnp.tanh(hidden)
    slope[...] = low(1.0 - bent * bent).astype(F32)
    wout_copy.wait()

    def sections(q, carry):
        for k in range(2):
            weighted[k * width : (k + 1) * width] = whole[...] * low(slope[pl.ds(2 * q + k, 1), :])
        product = dot1(weighted[...], wout[...])
        for k in range(2):
            one = product[k * width : (k + 1) * width]
            k_ref[2 * q + k] = one
            kt_ref[2 * q + k] = jnp.transpose(one)
        return carry

    lax.fori_loop(0, 2, sections, 0)

    eye = diagonal_mask(width)

    def on_diagonal(row):
        return jnp.where(eye, row, 0.0)

    def column(row):
        return jnp.sum(on_diagonal(row), axis=1, keepdims=True)

    def pair(q, carry):
        w0, w1 = sect[2, pl.ds(2 * q, 1)], sect[2, pl.ds(2 * q + 1, 1)]
        g0, g1 = sect[1, pl.ds(2 * q, 1)], sect[1, pl.ds(2 * q + 1, 1)]
        d = 1.0 / (1.0 + w1)
        dw = w1 * d
        k0, k1, k0t, k1t = k_ref[2 * q], k_ref[2 * q + 1], kt_ref[2 * q], kt_ref[2 * q + 1]
        scaled = column(d) * k1
        transposed = on_diagonal(d) + k0 * d + scaled + dot1(low(k0 * d), low(k1))
        leaf[q, 2] = transposed
        leaf[q, 3] = jnp.transpose(transposed)
        leaf[q, 0] = on_diagonal(1.0 + d) + scaled + k1t * d + dot1(low(k1t * d), low(k1))
        light = k0 * dw
        leaf[q, 1] = on_diagonal(w0 + dw) + light + column(dw) * k0t + dot1(low(light), low(k0t))
        rhs = d * g1
        rhs_column = to_column(rhs)
        leaf_v[q, 0:1] = rhs + column_to_row(rhs_column, k1)
        leaf_v[q, 1:2] = rhs + column_to_row(rhs_column, k0t) + g0
        return carry

    lax.fori_loop(0, 2, pair, 0)

    def chain_of(quad, fourth, vector):
        return [quad.at[0], quad.at[1], quad.at[2], fourth, lambda: vector[0:1], lambda: vector[1:2]]

    lower, upper = (chain_of(leaf.at[q], leaf.at[q, 3], leaf_v.at[q]) for q in range(2))
    mine = chain_of(chain.at[c], chain_a.at[c], chain_v.at[c])
    b, e, failed = merge_chains(lower, upper, mine, x0_ref, b_ref, pair_ref, 2, 0, 1e-3, near_products, lambda: None)
    chain_v[c] = jnp.zeros((8, width), F32)
    chain_v[c, 0:1] = b
    chain_v[c, 1:2] = e
    chain_v[c, 2:3] = jnp.broadcast_to(failed, (1, width))

    def chain_copy(slot, k):
        return remote(chain.at[slot, k], chain.at[slot, k], c_send.at[k], c_recv.at[k], {"tm": core})

    def vector_copy(slot):
        return remote(chain_v.at[slot], chain_v.at[slot], c_send.at[3], c_recv.at[3], {"tm": core})

    chain_copy(c, c).start()
    chain_copy(c, 1 - c).start()
    chain_copy(c, 2).start()
    vector_copy(c).start()
    cleanup.append(lambda: [chain_copy(c, k).wait_send() for k in range(3)] and None)
    cleanup.append(lambda: vector_copy(c).wait_send())
    chain_copy(1 - c, 1 - c).wait_recv()

    def rest_arrived():
        chain_copy(1 - c, c).wait_recv()
        chain_copy(1 - c, 2).wait_recv()
        vector_copy(1 - c).wait_recv()
        chain_a[1 - c] = jnp.transpose(chain[1 - c, 2])

    first, second = (chain_of(chain.at[q], chain_a.at[q], chain_v.at[q]) for q in range(2))
    b, e, failed = merge_chains(first, second, chain_of(top, top.at[3], top_v), x1_ref, b_ref, pair_ref, 3, 1, 0.02, far_products, rest_arrived)
    bad = jnp.maximum(jnp.maximum(chain_v[0, 2:3], chain_v[1, 2:3]), failed)

    sign = jnp.where(is_left, 1.0, -1.0)
    for k, (a_index, b_index) in enumerate(((3, 2), (2, 3), (1, 0), (0, 1))):
        side[k] = jnp.where(is_left, top[a_index], top[b_index])
    side_v[0:1] = jnp.where(is_left, e, -b)
    side_v[1:2] = jnp.where(is_left, b, e)
    side_v[2:3] = bad

    blocks = width // 128
    tiles = [(i, j) for i in range(blocks) for j in range(i + 1)]
    half = len(tiles) // 2

    def tile_copy(which, k):
        return remote(pack_out.at[k], pack_in.at[which, k], p_send.at[k], p_recv.at[which, k], {"tm": inward})

    def tile_pass(which, k):
        return remote(pack_in.at[which, k], pack_in.at[which, k], q_send.at[which, k], q_recv.at[which, k], {"tm": core})

    def row_copy(which):
        return remote(zout_v, pack_v.at[which], v_send, v_recv.at[which], {"tm": inward})

    def receive(which, m_ref, row_ref):
        for j in range(half):
            tile_copy(which, 2 * j + c).wait_recv()
            tile_pass(which, 2 * j + c).start()
        for j in range(half):
            tile_pass(which, 2 * j + 1 - c).wait_recv()
        row_copy(which).wait_recv()
        for k, (i, j) in enumerate(tiles):
            tile = pack_in[which, k]
            m_ref[128 * i : 128 * i + 128, 128 * j : 128 * j + 128] = tile
            if i != j:
                m_ref[128 * j : 128 * j + 128, 128 * i : 128 * i + 128] = jnp.transpose(tile)
        row_ref[...] = pack_v[which]

    @pl.when(is_end)
    def _():
        z_ref[...] = jnp.where(eye, 1.0, 0.0)
        z_v[...] = jnp.zeros_like(z_v)
        b_ref[...] = side[2]

    @pl.when(jnp.logical_not(is_end))
    def _():
        receive(0, z_ref, z_v)
        b_ref[...] = dot3(side[2], z_ref[...])

    @pl.when(solves)
    def _():
        delta = jnp.where(left_end, 0.0, 1.0)
        floor = jnp.min(small[0, 4:5], axis=1, keepdims=True)
        least = jnp.where(left_end, floor, 1.0)
        failed = invert(b_ref, delta, least, jnp.where(left_end, 6, 5), 1, 0.2, 1.5, x2_ref, pair_ref)

        @pl.when(left_end)
        def _():
            zo_ref[...] = x2_ref[...]

        @pl.when(jnp.logical_not(left_end))
        def _():
            zo_ref[...] = dot3(z_ref[...], x2_ref[...])

        zout[...] = dot3(dot3(side[0], zo_ref[...]), side[1]) + side[3]
        v = side_v[0:1]
        row = column_to_row(to_column(z_v[0:1]) + row_to_column(v, z_ref[...]), x2_ref[...])
        zout_v[...] = jnp.zeros_like(zout_v)
        zout_v[0:1] = to_row(row_to_column(row, side[0])) + side_v[1:2]
        zout_v[2:3] = jnp.maximum(jnp.maximum(side_v[2:3], z_v[2:3]), failed)

    @pl.when(right_end)
    def _():
        zout[...] = side[3]
        zout_v[...] = jnp.zeros_like(zout_v)
        zout_v[0:1] = side_v[1:2]
        zout_v[2:3] = side_v[2:3]

    which = is_root.astype(jnp.int32)

    @pl.when(jnp.logical_not(left_root))
    def _():
        for k, (i, j) in enumerate(tiles):
            pack_out[k] = zout[128 * i : 128 * i + 128, 128 * j : 128 * j + 128]
        for j in range(half):
            tile_copy(which, 2 * j + c).start()
        row_copy(which).start()

    def tiles_sent():
        @pl.when(jnp.logical_not(left_root))
        def _():
            for j in range(half):
                tile_copy(which, 2 * j + c).wait_send()
            row_copy(which).wait_send()

        @pl.when(jnp.logical_not(is_end))
        def _():
            for j in range(half):
                tile_pass(0, 2 * j + c).wait_send()

    cleanup.append(tiles_sent)
    def outer_copy():
        return remote(o_buf, o_in, o_send, o_recv, {"tm": outward})

    def middle_copy():
        return remote(middle_v, o_in, f_send.at[0], f_recv.at[0], {"tm": inward})

    flag_copies = []
    for k in range(1, greenhouses):
        flag_copies.append(
            remote(flags.at[0], flags.at[k], f_send.at[k], f_recv.at[k], {"scen": lax.rem(house + k, greenhouses)})
        )
    last = greenhouses

    def flag_out(k, target):
        return remote(flags.at[last], flags.at[last], f_send.at[greenhouses + k], f_recv.at[greenhouses], {"tm": target})

    @pl.when(left_root)
    def _():
        receive(1, zo_ref, zo_v)
        b_ref[...] = dot3(zo_ref[...], zout[...])
        invert(b_ref, 1.0, 1.0, 5, 0, 0.3, 1.0, xr_ref, pair_ref)
        rhs = to_column(zout_v[0:1]) + row_to_column(zo_v[0:1], zout[...])
        value = column_to_row(rhs, xr_ref[...])
        for _ in range(3):
            column_now = to_column(value)
            left_over = rhs - column_now - row_to_column(column_to_row(column_now, zo_ref[...]), zout[...])
            value = value + column_to_row(left_over, xr_ref[...])
        failed = bad_if(total(left_over * left_over), 1e-4 * total(rhs * rhs))
        middle_v[...] = jnp.broadcast_to(value, middle_v.shape)
        middle_copy().start()
        o_in[0:1] = zo_v[0:1] - row_dot(value, zo_ref[...])
        flags[0] = jnp.broadcast_to(
            jnp.maximum(jnp.maximum(zout_v[2:3, :128], zo_v[2:3, :128]), failed), (8, 128)
        )
        for copy in flag_copies:
            copy.start()

    @pl.when(right_root)
    def _():
        middle_copy().wait_recv()

    @pl.when(jnp.logical_not(is_root))
    def _():
        outer_copy().wait_recv()

    outer = o_in[0:1]
    side_v[3:4] = jnp.zeros((1, width), F32)

    @pl.when(solves)
    def _():
        w = sign * side_v[0:1] + row_dot(outer, side[0])
        value = column_to_row(to_column(z_v[0:1]) + sign * row_to_column(w, z_ref[...]), x2_ref[...])
        side_v[3:4] = value
        o_buf[...] = jnp.broadcast_to(w - sign * row_dot(value, side[2]), o_buf.shape)

    @pl.when(jnp.logical_not(is_end))
    def _():
        outer_copy().start()

    own_value = side_v[3:4]
    start = jnp.where(is_left, own_value, outer)
    finish_lam = jnp.where(is_left, outer, own_value)

    def result_copy(slot):
        return remote(result.at[slot], result_in, r_send, r_recv, {"tm": core})

    @pl.when(left_root)
    def _():
        for copy in flag_copies:
            copy.wait_recv()
        worst = flags[0]
        for k in range(1, greenhouses):
            worst = jnp.maximum(worst, flags[k])
        flags[last] = worst
        flag_out(1, inward).start()

    @pl.when(right_root)
    def _():
        flag_out(0, outward).wait_recv()

    @pl.when(jnp.logical_and(is_root, jnp.logical_not(is_end)))
    def _():
        flag_out(0, outward).start()

    @pl.when(writes)
    def _():
        middle, lam = open_chain(first, second, x1_ref, start, finish_lam)
        x_a = jnp.where(c == 0, start, middle)
        lam_b = jnp.where(c == 0, lam, finish_lam)
        middle, lam = open_chain(lower, upper, x0_ref, x_a, lam_b)

        def solve_pair(q, to_ref):
            x = jnp.where(q == 0, x_a, middle)
            lam_q = jnp.where(q == 0, lam, lam_b)
            w1, g1 = sect[2, pl.ds(2 * q + 1, 1)], sect[1, pl.ds(2 * q + 1, 1)]
            to_ref[0:1] = x
            to_ref[1:2] = (
                x + row_dot(x, k_ref[2 * q]) + lam_q + row_dot(lam_q, kt_ref[2 * q + 1]) + g1
            ) / (1.0 + w1)

        solve_pair(1 - c, result.at[1 - c])
        result_copy(1 - c).start()
        solve_pair(c, out_ref)

    @pl.when(jnp.logical_not(writes))
    def _():
        result_copy(0).wait_recv()
        out_ref[...] = result_in[0:2]

    @pl.when(jnp.logical_not(is_root))
    def _():
        flag_out(0, outward).wait_recv()

        @pl.when(jnp.logical_not(is_end))
        def _():
            flag_out(0, outward).start()

    bad_ref[...] = flags[last, 0:1, 0:1]

    def rest_sent():
        @pl.when(jnp.logical_not(is_end))
        def _():
            outer_copy().wait_send()
            flag_out(0, outward).wait_send()

        @pl.when(left_root)
        def _():
            for j in range(half):
                tile_pass(1, 2 * j + c).wait_send()
            middle_copy().wait_send()
            flag_out(1, inward).wait_send()
            for copy in flag_copies:
                copy.wait_send()

        @pl.when(writes)
        def _():
            result_copy(1 - c).wait_send()

    cleanup.append(rest_sent)
    for act in cleanup:
        act()

def fast_device(states, gradient, active_mask, zone_weight, zone_map, w_in, w_out, bias):
    width = states.shape[1]
    hidden = w_in.shape[1]
    devices = lax.axis_size("tm")
    greenhouses = lax.axis_size("scen")
    rows = w_in.shape[0]
    pieces = 32 // math.gcd(rows, 16)
    span = hidden // pieces
    chunks = pieces * rows // 16
    tiles = (width // 128) * (width // 128 + 1) // 2
    square = lambda *lead: pltpu.VMEM(lead + (width, width), F32)
    lines = lambda *lead: pltpu.VMEM(lead + (8, width), F32)
    dma = pltpu.SemaphoreType.DMA
    vmem = pl.BlockSpec(memory_space=pltpu.VMEM)
    scratch = [
        pltpu.VMEM((devices // 4, 4, chunks, 16, span), BF16), pltpu.VMEM((rows * devices, hidden), BF16), pltpu.VMEM(w_out.shape, BF16),
        lines(4), lines(3), pltpu.VMEM((8, hidden), F32), square(4), square(4), square(2, 4), lines(2),
        square(2, 3), square(2), lines(2), square(4), lines(),
        square(), square(), square(), square(), square(), pltpu.VMEM((2 * width, width), BF16), square(4), lines(),
        square(), lines(), square(), lines(), square(), lines(),
        pltpu.VMEM((tiles, 128, 128), F32), pltpu.VMEM((2, tiles, 128, 128), F32), lines(2), lines(), lines(), lines(2), lines(),
        pltpu.VMEM((1 + greenhouses, 8, 128), F32), lines(),
        pltpu.VMEM((2 * width, hidden), BF16),
        dma((6, max(4, devices // 4))), dma((5, max(4, devices // 4))), dma((3,)), dma((4,)), dma, dma((4,)), dma((4,)), dma((tiles,)), dma((2, tiles)),
        dma((2, tiles)), dma((2, tiles)), dma, dma((2,)), dma, dma, dma, dma,
        dma((greenhouses + 2,)), dma((greenhouses + 1,)),
    ]
    return pl.pallas_call(
        functools.partial(fast_kernel, devices, greenhouses, rows),
        out_shape=(jax.ShapeDtypeStruct((2, width), F32), jax.ShapeDtypeStruct((1, 1), F32)),
        in_specs=[vmem] * 7 + [pl.BlockSpec(memory_space=pl.ANY)],
        out_specs=(vmem, vmem),
        scratch_shapes=scratch,
        compiler_params=pltpu.CompilerParams(collective_id=0, has_side_effects=True, vmem_limit_bytes=58 << 20),
        name="gauss_newton",
    )(states, gradient, active_mask, zone_weight, zone_map, w_in, bias, w_out)


def per_device(*arrays):
    value, bad = fast_device(*arrays)
    return lax.cond(bad[0, 0] > 0.0, lambda: direct_device(*arrays), lambda: value)


def solution(mesh):
    return jax.shard_map(
        per_device,
        mesh=mesh,
        in_specs=(
            P(("scen", "tm"), None),
            P(("scen", "tm"), None),
            P(("scen", "tm"), None),
            P(("scen", "tm"), None),
            P("scen"),
            P("tm", None),
            P(),
            P(),
        ),
        out_specs=P(("scen", "tm"), None),
        check_vma=False,
    )
```
